128 devices in a mesh: grid: 16 (over x, y), dom: 8 (over z, core).
Axes of the slice: x: 4, y: 4, z: 4, core: 2. Of those that a mesh axis runs over, the one named last changes fastest.
Arguments:
- concentration: float32 [16, 128, 8192], P('grid', 'dom'), may hold values from -6 to 6
- diffusion: float32 [16, 128, 8192], P('grid', 'dom'), may hold values from 0.25 to 1
- velocity: float32 [4], replicated, may hold values from -1 to 1
- levels: int32 [16, 3], P('grid'), may hold values from 3 to 7, as said below
- grid_signs: int32 [16], P('grid'), may hold values from -1 to 1, as said below
- owner_list: int32 [128, 128], P(('grid', 'dom')), may hold values from 0 to 127, as said below
- slot_list: int32 [128, 128], P(('grid', 'dom')), may hold values from 0 to 63
Outputs:
- combined: float32 [16, 128, 8192], P('grid', 'dom')
The draws below stay inside these ranges and needn't reach their ends.
Inputs may be any that keep to these rules, and one draw needn't show every extreme that they name: Each row's three levels sum to 13. `grid_signs`: each is -1 or 1. `owner_list`: at most 2 blocks of one device name the same owner; some owner is named by 2 blocks of every device.
All inputs are finite; a program needn't handle non-finite values.
Results may differ from the reference program's by a relative error of at most 0.0003.
Values sent between devices are 32-bit elements; how exact they have to be, the bound alone decides.
A program may use at most 192 MiB of HBM per device.

```python
import math
import jax
import jax.numpy as jnp
from jax import lax

LR = 13
LMIN = 3
N4_DEV = 16
TSTEPS = 2
GPD = 1
BLK = 1024
ROWCELLS = 8192
N4 = 128
GRIDS = 16
NBLK = 128
CAP = 2
SLOTS = 64
N_GRID = 16
N_DOM = 8


def draw_levels(key, part):
    spare_levels = LR - 3 * LMIN
    first_key, second_key, third_key = jax.random.split(key, 3)
    first_extra = jax.random.randint(first_key, (GRIDS,), 0, spare_levels + 1)
    second_raw = jax.random.randint(second_key, (GRIDS,), 0, spare_levels + 1)
    second_extra = second_raw % (spare_levels - first_extra + 1)
    third_extra = spare_levels - first_extra - second_extra
    stacked = jnp.stack([first_extra, second_extra, third_extra], axis=1)
    rotation = jax.random.randint(third_key, (GRIDS, 1), 0, 3)
    columns = (jnp.arange(3)[None, :] + rotation) % 3
    rotated = jnp.take_along_axis(stacked, columns, axis=1)
    rotated = rotated.at[0].set(jnp.array([spare_levels, 0, 0], jnp.int32))
    return (rotated + LMIN).astype(jnp.int32)


def draw_grid_signs(key, part):
    picks = jax.random.randint(key, (GRIDS,), 0, 2)
    return (2 * picks - 1).at[0].set(1).at[1].set(-1).astype(jnp.int32)


def draw_owner_list(key, part):
    busy_key, rest_key = jax.random.split(key)
    busiest = jax.random.randint(busy_key, (), 0, N_GRID * N_DOM)

    def one_device(dev_key):
        perm_key, order_key = jax.random.split(dev_key)
        places = jax.random.permutation(perm_key, N_GRID * N_DOM * CAP)
        owners = places // CAP
        is_busy = (owners == busiest).astype(jnp.int32)
        ordering = jnp.argsort(is_busy, stable=True)
        others = owners[ordering][:NBLK - CAP]
        picked = jnp.concatenate([jnp.full((CAP,), busiest, jnp.int32), others.astype(jnp.int32)])
        return jax.random.permutation(order_key, picked)
    return jax.vmap(one_device)(jax.random.split(rest_key, N_GRID * N_DOM)).astype(jnp.int32)


def draw_slot_list(key, part):
    drawn = jax.random.randint(key, (N_GRID * N_DOM, NBLK), 0, SLOTS)
    return drawn.at[0, 0].set(SLOTS - 1).at[0, 1].set(0).astype(jnp.int32)


def level_of(stream_key, extent, cuts, smallest, top_value):
    loudness, own = 1.0, jax.random.fold_in(stream_key, 6)
    for axis_at, blocks in cuts:
        heights = jnp.exp(jax.random.uniform(jax.random.fold_in(own, axis_at), (blocks,), jnp.float32, smallest / len(cuts), top_value / len(cuts)))
        loudness = loudness * jnp.repeat(heights, extent[axis_at] // blocks).reshape([-1 if axis == axis_at else 1 for axis in range(len(extent))])
    return loudness


def scatter_about(rng, extent, width, most, cuts=(), kind=jnp.bfloat16):
    values = width * jax.random.normal(rng, extent, jnp.float32)
    if cuts:
        values = values * level_of(rng, extent, cuts, -0.22, 0.18)
    return jnp.clip(values, -most, most).astype(kind)


def setup_inputs(seed: int = 0) -> dict:
    key_list = jax.random.split(jax.random.key(seed), 8)
    return {
        "concentration": scatter_about(key_list[0], (GRIDS, N4, ROWCELLS), 1.0, 6.0, ((0, 16), (1, 8)), jnp.float32),
        "diffusion": jnp.clip(jnp.exp(math.log(1.0) - 1.3862944 * jax.random.uniform(key_list[1], (GRIDS, N4, ROWCELLS), jnp.float32) ** level_of(key_list[1], (GRIDS, N4, ROWCELLS), ((0, 16), (1, 8)), -0.2, 0.2)), 0.25, 1.0),
        "velocity": jnp.clip(jax.random.uniform(key_list[2], (4,), jnp.float32, -1.0, 1.0), -1.0, 1.0),
        "levels": draw_levels(jax.random.fold_in(key_list[7], 71), 0),
        "grid_signs": draw_grid_signs(jax.random.fold_in(key_list[7], 71), 0),
        "owner_list": draw_owner_list(jax.random.fold_in(key_list[7], 71), 0),
        "slot_list": draw_slot_list(jax.random.fold_in(key_list[7], 71), 0),
    }


def level_table():
    level_rows = []
    for first_level in range(LMIN, LR - 2 * LMIN + 1):
        for second_level in range(LMIN, LR - first_level - LMIN + 1):
            level_rows.append((first_level, second_level, LR - first_level - second_level))
    return level_rows


def branch_index(grid_levels):
    level_rows = jnp.array(level_table(), jnp.int32)
    matching = jnp.all(grid_levels[None, :] == level_rows, axis=1)
    return jnp.sum(jnp.where(matching, jnp.arange(level_rows.shape[0], dtype=jnp.int32), 0)).astype(jnp.int32)


def step_ahead(values, axis_num):
    length = values.shape[axis_num]
    shifted = lax.slice_in_dim(values, 1, length, axis=axis_num)
    return jnp.concatenate([shifted, jnp.zeros_like(lax.slice_in_dim(values, 0, 1, axis=axis_num))], axis=axis_num)


def behind(values, axis_num):
    length = values.shape[axis_num]
    shifted = lax.slice_in_dim(values, 0, length - 1, axis=axis_num)
    return jnp.concatenate([jnp.zeros_like(lax.slice_in_dim(values, 0, 1, axis=axis_num)), shifted], axis=axis_num)


def inner_terms(level_combo):
    def branch_fn(values, velocity):
        shaped = values.reshape(values.shape[0], 2 ** level_combo[2], 2 ** level_combo[1], 2 ** level_combo[0])
        second = jnp.zeros_like(shaped)
        drift = jnp.zeros_like(shaped)
        for direction in range(3):
            axis_num = 3 - direction
            ahead_vals = step_ahead(shaped, axis_num)
            before = behind(shaped, axis_num)
            second = second + (ahead_vals - 2.0 * shaped + before)
            drift = drift + velocity[direction] * (ahead_vals - before)
        return second.reshape(values.shape), drift.reshape(values.shape)
    return branch_fn


def hier_axis(values, axis_num):
    length = values.shape[axis_num]
    result = values
    for level_bit in range(length.bit_length() - 1):
        stride = 2 ** (level_bit + 1)
        before = lax.slice_in_dim(values, 0, length, stride, axis=axis_num)
        ahead_vals = lax.slice_in_dim(values, stride, length, stride, axis=axis_num)
        ahead_vals = jnp.concatenate([ahead_vals, jnp.zeros_like(lax.slice_in_dim(before, 0, 1, axis=axis_num))], axis=axis_num)
        position = [slice(None)] * values.ndim
        position[axis_num] = slice(2 ** level_bit, None, stride)
        result = result.at[tuple(position)].add(-0.5 * (before + ahead_vals))
    return result


def inner_surplus(level_combo):
    def branch_fn(values):
        shaped = values.reshape(values.shape[0], 2 ** level_combo[2], 2 ** level_combo[1], 2 ** level_combo[0])
        for axis_num in (3, 2, 1):
            shaped = hier_axis(shaped, axis_num)
        return shaped.reshape(values.shape)
    return branch_fn


def reference(concentration, diffusion, velocity, levels, grid_signs, owner_list, slot_list):
    level_rows = level_table()
    term_fns = [inner_terms(level_combo) for level_combo in level_rows]
    surplus_fns = [inner_surplus(level_combo) for level_combo in level_rows]

    def one_grid(operands):
        values, coefficient, grid_levels, grid_sign = operands
        branch = branch_index(grid_levels)
        for step_num in range(TSTEPS):
            second, drift = lax.switch(branch, term_fns, values, velocity)
            ahead_vals = step_ahead(values, 0)
            before = behind(values, 0)
            second = second + (ahead_vals - 2.0 * values + before)
            drift = drift + velocity[3] * (ahead_vals - before)
            values = values + 0.1 * coefficient * second - 0.1 * drift
        values = hier_axis(values, 0)
        values = lax.switch(branch, surplus_fns, values)
        return grid_sign.astype(jnp.float32) * values

    signed = lax.map(one_grid, (concentration, diffusion, levels, grid_signs))
    blocks = signed.reshape(N_GRID, GPD, N_DOM, N4_DEV, ROWCELLS).transpose(0, 2, 1, 3, 4).reshape(N_GRID * N_DOM * NBLK, BLK)
    targets = (owner_list * SLOTS + slot_list).reshape(-1).astype(jnp.int32)
    pieces = jax.ops.segment_sum(blocks, targets, num_segments=N_GRID * N_DOM * SLOTS)
    returned = pieces[targets]
    return returned.reshape(N_GRID, N_DOM, GPD, N4_DEV, ROWCELLS).transpose(0, 2, 1, 3, 4).reshape(GRIDS, N4, ROWCELLS)
```

```python
import jax
import jax.numpy as jnp
from jax import lax
from jax.experimental import pallas as pl
from jax.experimental.pallas import tpu as pltpu
from jax.sharding import PartitionSpec as P

MESH = pl.DeviceIdType.MESH
F32 = jnp.float32
BF16 = jnp.bfloat16
I32 = jnp.int32

COLS = 64
PAD = 8
TILE_HALO = PAD + 2 * COLS


def tile(at):
    return pl.ds(at * 8, 8)


def node_rows(base, node):
    return pl.ds(base + (node // 8) * COLS * 8 + node % 8, COLS, stride=8)


def dot_exact(left, right):
    first = left.astype(BF16)
    rest = left - first.astype(F32)
    second = rest.astype(BF16)
    third = (rest - second.astype(F32)).astype(BF16)
    total = jnp.dot(third, right, preferred_element_type=F32)
    total = total + jnp.dot(second, right, preferred_element_type=F32)
    return total + jnp.dot(first, right, preferred_element_type=F32)


def lane_matrices(l1, l2, sign):
    source = lax.broadcasted_iota(I32, (128, 128), 0)
    target = lax.broadcasted_iota(I32, (128, 128), 1)
    both = l1 + l2
    low = [0, l1, both]
    top = [jnp.minimum(l1, 7), jnp.minimum(both, 7), 7]
    here = jnp.full((128, 128), sign, F32)
    after = jnp.full((128, 128), sign, F32)
    for field in range(3):
        width = jnp.maximum(top[field] - jnp.minimum(low[field], 7), 0)
        mask = jnp.left_shift(1, width) - 1
        shift = jnp.minimum(low[field], 7)
        fro = jnp.right_shift(source, shift) & mask
        to = jnp.right_shift(target, shift) & mask
        bit = to & (-to)
        same = jnp.where(fro == to, 1.0, 0.0)
        near = jnp.where((to != 0) & ((fro == to - bit) | (fro == to + bit)), -0.5, 0.0)
        plain = same + near
        wraps = (to != 0) & (to + bit == mask + 1) & (fro == 0)
        carry = jnp.where(wraps, -0.5, 0.0)
        here = here * plain
        if field == 0:
            after = after * plain
        elif field == 1:
            after = after * jnp.where(both > 6, jnp.where(width > 0, carry, 0.0), plain)
        else:
            after = after * jnp.where(both > 6, 1.0, carry)
    return here, after


def surplus_kernel(
    lev_ref, vel_ref, sign_ref, u_hbm, k_hbm, s_ref,
    start, mid, coef, stepped, lanes_done, rows_done, packs, low_in, high_in, lead, lead_in,
    load_sem, send_sem, recv_sem, lead_send, lead_recv,
):
    g = lax.axis_index("grid")
    d = lax.axis_index("dom")
    barrier = pltpu.get_barrier_semaphore()
    for k in range(1, 8):
        pl.semaphore_signal(
            barrier, inc=1, device_id=(g, lax.rem(d + k, 8)), device_id_type=MESH
        )
    load_u = pltpu.make_async_copy(u_hbm, start.at[pl.ds(PAD * 8, 1024)], load_sem.at[0])
    load_k = pltpu.make_async_copy(k_hbm, coef.at[pl.ds(0, 1024)], load_sem.at[1])
    load_u.start()
    load_k.start()
    zero_pad = jnp.zeros((PAD * 8, 128), F32)
    for buffer in (start, mid):
        buffer[0 : PAD * 8] = zero_pad
        buffer[(TILE_HALO + COLS) * 8 : (TILE_HALO + COLS + PAD) * 8] = zero_pad
    load_u.wait()
    load_k.wait()
    base = PAD * 8
    packs[0, 0:64] = start[node_rows(base, 0), :]
    packs[0, 64:128] = start[node_rows(base, 1), :]
    packs[0, 128:192] = coef[node_rows(0, 0), :]
    packs[1, 0:64] = start[node_rows(base, 14), :]
    packs[1, 64:128] = start[node_rows(base, 15), :]
    packs[1, 128:192] = coef[node_rows(0, 15), :]
    pl.semaphore_wait(barrier, 7)

    def down():
        return pltpu.make_async_remote_copy(
            src_ref=packs.at[0], dst_ref=high_in, send_sem=send_sem.at[0], recv_sem=recv_sem.at[0],
            device_id=(g, lax.rem(d + 7, 8)), device_id_type=MESH,
        )

    def upward():
        return pltpu.make_async_remote_copy(
            src_ref=packs.at[1], dst_ref=low_in, send_sem=send_sem.at[1], recv_sem=recv_sem.at[1],
            device_id=(g, lax.rem(d + 1, 8)), device_id_type=MESH,
        )

    @pl.when(d > 0)
    def _():
        down().start()

    @pl.when(d < 7)
    def _():
        upward().start()

    zero_rows = jnp.zeros((192, 128), F32)

    @pl.when(d == 0)
    def _():
        low_in[...] = zero_rows

    @pl.when(d == 7)
    def _():
        high_in[...] = zero_rows

    l1 = lev_ref[0, 0]
    l2 = lev_ref[0, 1]
    l3 = lev_ref[0, 2]
    both = l1 + l2
    lane = lax.broadcasted_iota(I32, (8, 128), 1)
    sub = lax.broadcasted_iota(I32, (8, 128), 0)
    span2 = jnp.left_shift(1, l1)
    span3 = jnp.minimum(jnp.left_shift(1, both), 128)
    skip3 = jnp.where(both == 8, 2, jnp.where(both == 9, 4, jnp.where(both == 10, 8, 1)))
    last1 = jnp.left_shift(1, l1) - 1
    last2 = jnp.left_shift(1, l2) - 1
    last3 = jnp.left_shift(1, l3) - 1
    drift1 = 0.1 * vel_ref[0]
    drift2 = 0.1 * vel_ref[1]
    drift3 = 0.1 * vel_ref[2]
    drift4 = 0.1 * vel_ref[3]
    from_next2 = lane < span2
    from_last2 = lane >= 128 - span2
    from_next3 = lane < span3
    from_last3 = lane >= 128 - span3
    ahead2 = (128 - span2) & 127
    behind2 = span2 & 127
    ahead3 = (128 - span3) & 127
    behind3 = span3 & 127

    def masks(c):
        cell = c * 128 + lane
        i1 = cell & last1
        i2 = jnp.right_shift(cell, l1) & last2
        i3 = jnp.right_shift(cell, both) & last3
        return (i1 != last1, i1 != 0, i2 != last2, i2 != 0, i3 != last3, i3 != 0)

    def advance(ref, at, x, ahead4, behind4, diff, ok):
        p1 = jnp.where(ok[0], pltpu.roll(x, 127, 1), 0.0)
        m1 = jnp.where(ok[1], pltpu.roll(x, 1, 1), 0.0)
        p2 = pltpu.roll(jnp.where(from_next2, ref[tile(at + 1), :], x), ahead2, 1)
        p2 = jnp.where(ok[2], p2, 0.0)
        m2 = pltpu.roll(jnp.where(from_last2, ref[tile(at - 1), :], x), behind2, 1)
        m2 = jnp.where(ok[3], m2, 0.0)
        p3 = pltpu.roll(jnp.where(from_next3, ref[tile(at + skip3), :], x), ahead3, 1)
        p3 = jnp.where(ok[4], p3, 0.0)
        m3 = pltpu.roll(jnp.where(from_last3, ref[tile(at - skip3), :], x), behind3, 1)
        m3 = jnp.where(ok[5], m3, 0.0)
        second = ((p1 + m1) + (p2 + m2)) + ((p3 + m3) + (ahead4 + behind4)) - 8.0 * x
        drift = (drift1 * (p1 - m1) + drift2 * (p2 - m2)) + (
            drift3 * (p3 - m3) + drift4 * (ahead4 - behind4)
        )
        return x + 0.1 * diff * second - drift

    def both_groups(ref, c, write):
        ok = masks(c)
        x0 = ref[tile(PAD + c), :]
        x1 = ref[tile(PAD + COLS + c), :]
        xh = ref[tile(TILE_HALO + c), :]
        before = pltpu.roll(xh, 6, 0)
        after = pltpu.roll(xh, 2, 0)
        write(0, c, advance(
            ref, PAD + c, x0, pltpu.roll(jnp.where(sub == 0, x1, x0), 7, 0),
            pltpu.roll(jnp.where(sub == 7, before, x0), 1, 0), coef[tile(c), :], ok,
        ))
        write(1, c, advance(
            ref, PAD + COLS + c, x1, pltpu.roll(jnp.where(sub == 0, after, x1), 7, 0),
            pltpu.roll(jnp.where(sub == 7, x0, x1), 1, 0), coef[tile(COLS + c), :], ok,
        ))
        return xh, ok

    @pl.when(d < 7)
    def _():
        down().wait_recv()

    @pl.when(d > 0)
    def _():
        upward().wait_recv()

    halo = TILE_HALO * 8

    def halo_rows(s):
        return pl.ds(halo + s, COLS, stride=8)

    start[halo_rows(0), :] = low_in[0:64]
    start[halo_rows(1), :] = low_in[64:128]
    start[halo_rows(2), :] = packs[0, 0:64]
    start[halo_rows(3), :] = packs[0, 64:128]
    start[halo_rows(4), :] = packs[1, 0:64]
    start[halo_rows(5), :] = packs[1, 64:128]
    start[halo_rows(6), :] = high_in[0:64]
    start[halo_rows(7), :] = high_in[64:128]
    coef[1024:1536] = jnp.zeros((512, 128), F32)
    coef[pl.ds(1024 + 1, COLS, stride=8), :] = low_in[128:192]
    coef[pl.ds(1024 + 6, COLS, stride=8), :] = high_in[128:192]
    outside = jnp.where(d == 0, 1, jnp.where(d == 7, 6, -1))

    def write_mid(t, c, value):
        mid[tile(PAD + t * COLS + c), :] = value

    def first_step(c, carry):
        xh, ok = both_groups(start, c, write_mid)
        value = advance(
            start, TILE_HALO + c, xh, pltpu.roll(xh, 7, 0), pltpu.roll(xh, 1, 0),
            coef[tile(2 * COLS + c), :], ok,
        )
        mid[tile(TILE_HALO + c), :] = jnp.where(sub == outside, 0.0, value)
        return carry

    def write_stepped(t, c, value):
        stepped[tile(t * COLS + c), :] = value

    def second_step(c, carry):
        both_groups(mid, c, write_stepped)
        return carry

    lax.fori_loop(0, COLS, first_step, 0)
    lax.fori_loop(0, COLS, second_step, 0)

    here, after = lane_matrices(l1, l2, sign_ref[0].astype(F32))
    here = here.astype(BF16)
    after = after.astype(BF16)
    straddles = jnp.where(both > 7, jnp.where(l1 < 7, 1, 0), jnp.where(both == 6, 1, 0))
    mask_a = jnp.where(both > 7, skip3 - 1, COLS - 1)
    no_next = jnp.where(straddles == 1, mask_a, 0)
    limit_a = jnp.where(both > 7, span2, span3)
    mask_b = jnp.where(both > 7, COLS - skip3, 0)
    chunk = 128
    stepped[1024:1032] = jnp.zeros((8, 128), F32)

    def lane_part(i, carry):
        row = pl.multiple_of(i * chunk, chunk)
        x = stepped[pl.ds(row, chunk), :]
        beyond = stepped[pl.ds(pl.multiple_of(row + 8, 8), chunk), :]
        col = jnp.right_shift(row + lax.broadcasted_iota(I32, (chunk, 128), 0), 3)
        beyond = jnp.where((col & no_next) != no_next, beyond, 0.0)
        lanes_done[pl.ds(row, chunk), :] = dot_exact(x, here) + dot_exact(beyond, after)
        return carry

    lax.fori_loop(0, 1024 // chunk, lane_part, 0)

    def neighbours(c, mask):
        j = c & mask
        off = j & (-j)
        has_up = (j != 0) & (j + off <= mask)
        weight = jnp.where(j != 0, 0.5, 0.0)
        weight_up = jnp.where(has_up, 0.5, 0.0)
        return c - off, jnp.where(has_up, c + off, c), weight, weight_up

    inside = lane < limit_a

    def columns_a(c, carry):
        lower, upper, weight, weight_up = neighbours(c, mask_a)
        for t in range(2):
            at = t * COLS
            update = weight * lanes_done[tile(at + lower), :]
            update = update + weight_up * lanes_done[tile(at + upper), :]
            rows_done[tile(at + c), :] = lanes_done[tile(at + c), :] - jnp.where(
                inside, update, 0.0
            )
        return carry

    lax.fori_loop(0, COLS, columns_a, 0)

    def columns_b(c, carry):
        lower, upper, weight, weight_up = neighbours(c, mask_b)
        for t in range(2):
            at = t * COLS
            update = weight * rows_done[tile(at + lower), :]
            update = update + weight_up * rows_done[tile(at + upper), :]
            lanes_done[tile(at + c), :] = rows_done[tile(at + c), :] - update
        return carry

    lax.fori_loop(0, COLS, columns_b, 0)

    lead[...] = lanes_done[node_rows(0, 0), :]

    def lead_copy(slot, target, sent):
        return pltpu.make_async_remote_copy(
            src_ref=lead, dst_ref=lead_in.at[slot], send_sem=lead_send.at[sent],
            recv_sem=lead_recv.at[slot], device_id=(g, target), device_id_type=MESH,
        )

    routes = [(0, d > 0, lax.rem(d + 7, 8)), (1, lax.rem(d, 2) == 0, lax.rem(d + 1, 8))]
    routes += [(1, d == 0, 2), (1, d == 0, 4), (1, d == 4, 6), (2, d == 4, 2)]
    for sent, (slot, condition, target) in enumerate(routes):

        @pl.when(condition)
        def _():
            lead_copy(slot, target, sent).start()

    zero_lead = jnp.zeros((64, 128), F32)

    @pl.when(d == 7)
    def _():
        lead_in[0] = zero_lead

    @pl.when(d == 0)
    def _():
        lead_in[1] = zero_lead

    @pl.when(d != 2)
    def _():
        lead_in[2] = zero_lead

    @pl.when(d < 7)
    def _():
        lead_copy(0, lax.rem(d + 7, 8), 0).wait_recv()

    @pl.when(d > 0)
    def _():
        lead_copy(1, lax.rem(d + 1, 8), 0).wait_recv()

    @pl.when(d == 2)
    def _():
        lead_copy(2, lax.rem(d + 1, 8), 0).wait_recv()

    use_next = jnp.where(lax.rem(d, 2) == 1, 1.0, 0.0)
    odd = (sub & 1) == 1
    two = (sub & 3) == 2
    four = sub == 4

    def fourth(c, carry):
        x0 = lanes_done[tile(c), :]
        x1 = lanes_done[tile(COLS + c), :]
        following = jnp.broadcast_to(lead_in[0, pl.ds(c, 1), :], (8, 128))
        lower = jnp.broadcast_to(lead_in[1, pl.ds(c, 1), :], (8, 128))
        upper = jnp.broadcast_to(lead_in[2, pl.ds(c, 1), :], (8, 128)) + use_next * following
        upper = jnp.where(d > 0, upper, 0.0)
        for t, x, beyond, special in ((0, x0, x1, lower + upper), (1, x1, following, x0 + following)):
            y = jnp.where(sub == 0, beyond, x)
            near1 = pltpu.roll(y, 7, 0) + pltpu.roll(x, 1, 0)
            near2 = pltpu.roll(y, 6, 0) + pltpu.roll(x, 2, 0)
            near4 = pltpu.roll(y, 4, 0) + pltpu.roll(x, 4, 0)
            near = jnp.where(odd, near1, jnp.where(two, near2, jnp.where(four, near4, special)))
            s_ref[tile(t * COLS + c), :] = x - 0.5 * near
        return carry

    lax.fori_loop(0, COLS, fourth, 0)

    @pl.when(d > 0)
    def _():
        down().wait_send()

    @pl.when(d < 7)
    def _():
        upward().wait_send()

    for sent, (slot, condition, target) in enumerate(routes):

        @pl.when(condition)
        def _():
            lead_copy(slot, target, sent).wait_send()


def block_rows(block):
    node = lax.div(block, 8)
    at = (lax.div(node, 8) * COLS + lax.rem(block, 8) * 8) * 8 + lax.rem(node, 8)
    return pl.ds(at, 8, stride=8)


def exchange_kernel(
    s_ref, own_ref, slot_ref, out_ref,
    outgoing, arrived, returned, back, slots_out, slots_in, index_v, index_s,
    index_sem, send_sem, recv_sem,
):
    g = lax.axis_index("grid")
    d = lax.axis_index("dom")
    me = g * 8 + d
    x, y = lax.div(g, 4), lax.rem(g, 4)
    z, core = lax.div(d, 2), lax.rem(d, 2)
    barrier = pltpu.get_barrier_semaphore()

    def peer(k):
        px = lax.rem(x + lax.div(k, 32), 4)
        py = lax.rem(y + lax.rem(lax.div(k, 8), 4), 4)
        pz = lax.rem(z + lax.rem(lax.div(k, 2), 4), 4)
        pc = lax.rem(core + lax.rem(k, 2), 2)
        return px * 4 + py, pz * 2 + pc

    def greet(k, carry):
        pl.semaphore_signal(barrier, inc=1, device_id=peer(k), device_id_type=MESH)
        return carry

    lax.fori_loop(1, 128, greet, 0)

    owners = own_ref[...]
    slot_ids = slot_ref[...]
    own_row = jnp.broadcast_to(owners, (128, 128))
    own_col = own_row.T
    row = lax.broadcasted_iota(I32, (128, 128), 0)
    col = lax.broadcasted_iota(I32, (128, 128), 1)
    earlier = jnp.where((own_row == own_col) & (row < col), 1, 0)
    rank = jnp.sum(earlier, axis=0, keepdims=True)
    rank_row = jnp.broadcast_to(rank, (128, 128))
    rank_col = rank_row.T
    slot_row = jnp.broadcast_to(slot_ids, (128, 128))
    table = jnp.full((128, 128), -1, I32)
    index_v[...] = jnp.zeros((8, 128), I32)
    index_v[0:1] = 2 * owners + rank
    for r in range(2):
        to_owner = (own_col == col) & (rank_col == r)
        index_v[1 + r : 2 + r] = jnp.sum(jnp.where(to_owner, row, 0), axis=0, keepdims=True)
        of_block = (own_row == row) & (rank_row == r)
        ids = jnp.sum(jnp.where(of_block, slot_row + 1, 0), axis=1, keepdims=True) - 1
        table = jnp.where(col == r, ids, table)
    slots_out[:, 0, :] = table
    fetch = pltpu.make_async_copy(index_v, index_s, index_sem)
    fetch.start()
    fetch.wait()

    def pack(o, carry):
        for r in range(2):
            outgoing[tile(2 * o + r), :] = s_ref[block_rows(index_s[1 + r, o]), :]
        return carry

    lax.fori_loop(0, 128, pack, 0)
    pl.semaphore_wait(barrier, 127)

    def share(at):
        return pl.ds(pl.multiple_of(at * 16, 16), 16)

    def send(k, carry):
        pg, pd = peer(k)
        to = pg * 8 + pd
        pltpu.make_async_remote_copy(
            src_ref=slots_out.at[to], dst_ref=slots_in.at[me], send_sem=send_sem.at[0],
            recv_sem=recv_sem.at[0], device_id=(pg, pd), device_id_type=MESH,
        ).start()
        pltpu.make_async_remote_copy(
            src_ref=outgoing.at[share(to)], dst_ref=arrived.at[share(me)], send_sem=send_sem.at[1],
            recv_sem=recv_sem.at[1], device_id=(pg, pd), device_id_type=MESH,
        ).start()
        return carry

    lax.fori_loop(1, 128, send, 0)
    slots_in[me] = slots_out[me]
    arrived[share(me), :] = outgoing[share(me), :]
    anyone = (g, lax.rem(d + 1, 8))

    def all_of(source, target, which):
        size = 127 * (source.shape[0] // 128)
        return pltpu.make_async_remote_copy(
            src_ref=source.at[pl.ds(0, size)], dst_ref=target.at[pl.ds(0, size)],
            send_sem=send_sem.at[which], recv_sem=recv_sem.at[which],
            device_id=anyone, device_id_type=MESH,
        )

    all_of(slots_out, slots_in, 0).wait_recv()
    ids_col = slots_in[:, 0, :]
    ids_row = ids_col.T
    equal = jnp.concatenate(
        [
            jnp.concatenate(
                [
                    jnp.where(
                        jnp.broadcast_to(ids_col[:, r : r + 1], (128, 128))
                        == jnp.broadcast_to(ids_row[s : s + 1, :], (128, 128)),
                        1.0,
                        0.0,
                    )
                    for s in range(2)
                ],
                axis=1,
            )
            for r in range(2)
        ],
        axis=0,
    ).astype(BF16)
    all_of(outgoing, arrived, 1).wait_recv()
    for j in range(8):
        block = jnp.concatenate(
            [arrived[pl.ds(r * 8 + j, 128, stride=16), :] for r in range(2)], axis=0
        )
        first = block.astype(BF16)
        rest = block - first.astype(F32)
        second = rest.astype(BF16)
        third = (rest - second.astype(F32)).astype(BF16)
        total = jnp.dot(equal, third, preferred_element_type=F32)
        total = total + jnp.dot(equal, second, preferred_element_type=F32)
        total = total + jnp.dot(equal, first, preferred_element_type=F32)
        for r in range(2):
            returned[pl.ds(r * 8 + j, 128, stride=16), :] = total[r * 128 : (r + 1) * 128]

    def send_back(k, carry):
        pg, pd = peer(k)
        to = pg * 8 + pd
        pltpu.make_async_remote_copy(
            src_ref=returned.at[share(to)], dst_ref=back.at[share(me)], send_sem=send_sem.at[2],
            recv_sem=recv_sem.at[2], device_id=(pg, pd), device_id_type=MESH,
        ).start()
        return carry

    lax.fori_loop(1, 128, send_back, 0)
    back[share(me), :] = returned[share(me), :]
    all_of(returned, back, 2).wait_recv()

    def unpack(b, carry):
        out_ref[block_rows(b), :] = back[tile(index_s[0, b]), :]
        return carry

    lax.fori_loop(0, 128, unpack, 0)
    all_of(slots_out, slots_in, 0).wait_send()
    all_of(outgoing, arrived, 1).wait_send()
    all_of(returned, back, 2).wait_send()


def body(concentration, diffusion, velocity, levels, grid_signs, owner_list, slot_list):
    def tiled(block):
        return block.reshape(2, 8, COLS, 128).transpose(0, 2, 1, 3).reshape(1024, 128)

    smem = pl.BlockSpec(memory_space=pltpu.SMEM)
    vmem = pl.BlockSpec(memory_space=pltpu.VMEM)
    anywhere = pl.BlockSpec(memory_space=pl.ANY)
    total_rows = (TILE_HALO + COLS + PAD) * 8
    surplus = pl.pallas_call(
        surplus_kernel,
        out_shape=jax.ShapeDtypeStruct((1032, 128), F32),
        in_specs=[smem, smem, smem, anywhere, anywhere],
        out_specs=vmem,
        scratch_shapes=[
            pltpu.VMEM((total_rows, 128), F32),
            pltpu.VMEM((total_rows, 128), F32),
            pltpu.VMEM((1552, 128), F32),
            pltpu.VMEM((1032, 128), F32),
            pltpu.VMEM((1024, 128), F32),
            pltpu.VMEM((1024, 128), F32),
            pltpu.VMEM((2, 192, 128), F32),
            pltpu.VMEM((192, 128), F32),
            pltpu.VMEM((192, 128), F32),
            pltpu.VMEM((64, 128), F32),
            pltpu.VMEM((3, 64, 128), F32),
            pltpu.SemaphoreType.DMA((2,)),
            pltpu.SemaphoreType.DMA((2,)),
            pltpu.SemaphoreType.DMA((2,)),
            pltpu.SemaphoreType.DMA((6,)),
            pltpu.SemaphoreType.DMA((3,)),
        ],
        compiler_params=pltpu.CompilerParams(collective_id=0, has_side_effects=True),
        name="surplus",
    )(levels, velocity, grid_signs, tiled(concentration), tiled(diffusion))
    combined = pl.pallas_call(
        exchange_kernel,
        out_shape=jax.ShapeDtypeStruct((1032, 128), F32),
        in_specs=[vmem, vmem, vmem],
        out_specs=vmem,
        scratch_shapes=[
            pltpu.VMEM((2048, 128), F32),
            pltpu.VMEM((2064, 128), F32),
            pltpu.VMEM((2064, 128), F32),
            pltpu.VMEM((2048, 128), F32),
            pltpu.VMEM((128, 1, 128), I32),
            pltpu.VMEM((128, 1, 128), I32),
            pltpu.VMEM((8, 128), I32),
            pltpu.SMEM((8, 128), I32),
            pltpu.SemaphoreType.DMA,
            pltpu.SemaphoreType.DMA((3,)),
            pltpu.SemaphoreType.DMA((3,)),
        ],
        compiler_params=pltpu.CompilerParams(collective_id=1, has_side_effects=True),
        name="exchange",
    )(surplus, owner_list, slot_list)
    return combined[:1024].reshape(2, COLS, 8, 128).transpose(0, 2, 1, 3).reshape(1, 16, COLS * 128)


def solution(mesh):
    return jax.shard_map(
        body,
        mesh=mesh,
        in_specs=(
            P("grid", "dom", None),
            P("grid", "dom", None),
            P(),
            P("grid", None),
            P("grid"),
            P(("grid", "dom"), None),
            P(("grid", "dom"), None),
        ),
        out_specs=P("grid", "dom", None),
        check_vma=False,
    )
```

```python
import jax
import jax.numpy as jnp
from jax import lax
from jax.experimental import pallas as pl
from jax.experimental.pallas import tpu as pltpu
from jax.sharding import PartitionSpec as P

MESH = pl.DeviceIdType.MESH
F32 = jnp.float32
BF16 = jnp.bfloat16
I32 = jnp.int32

COLS = 64
PAD = 8
TILE_HALO = PAD + 2 * COLS


def tile(at):
    return pl.ds(at * 8, 8)


def node_rows(base, node):
    return pl.ds(base + (node // 8) * COLS * 8 + node % 8, COLS, stride=8)


def dot_exact(left, right):
    first = left.astype(BF16)
    rest = left - first.astype(F32)
    second = rest.astype(BF16)
    third = (rest - second.astype(F32)).astype(BF16)
    total = jnp.dot(third, right, preferred_element_type=F32)
    total = total + jnp.dot(second, right, preferred_element_type=F32)
    return total + jnp.dot(first, right, preferred_element_type=F32)


def lane_matrices(l1, l2, sign):
    source = lax.broadcasted_iota(I32, (128, 128), 0)
    target = lax.broadcasted_iota(I32, (128, 128), 1)
    both = l1 + l2
    low = [0, l1, both]
    top = [jnp.minimum(l1, 7), jnp.minimum(both, 7), 7]
    here = jnp.full((128, 128), sign, F32)
    after = jnp.full((128, 128), sign, F32)
    for field in range(3):
        width = jnp.maximum(top[field] - jnp.minimum(low[field], 7), 0)
        mask = jnp.left_shift(1, width) - 1
        shift = jnp.minimum(low[field], 7)
        fro = jnp.right_shift(source, shift) & mask
        to = jnp.right_shift(target, shift) & mask
        bit = to & (-to)
        same = jnp.where(fro == to, 1.0, 0.0)
        near = jnp.where((to != 0) & ((fro == to - bit) | (fro == to + bit)), -0.5, 0.0)
        plain = same + near
        wraps = (to != 0) & (to + bit == mask + 1) & (fro == 0)
        carry = jnp.where(wraps, -0.5, 0.0)
        here = here * plain
        if field == 0:
            after = after * plain
        elif field == 1:
            after = after * jnp.where(both > 6, jnp.where(width > 0, carry, 0.0), plain)
        else:
            after = after * jnp.where(both > 6, 1.0, carry)
    return here, after


def peer_offsets():
    offsets = [(k // 32, k // 8 % 4, k // 2 % 4, k % 2) for k in range(1, 128)]
    return sorted(offsets, key=lambda o: -sum(min(v, 4 - v) for v in o[:3]))


def unrolled(count, factor, step):
    def some(i, carry):
        for k in range(factor):
            step(i * factor + k)
        return carry

    lax.fori_loop(0, count // factor, some, 0)


def combine_kernel(
    lev_ref, vel_ref, sign_ref, own_ref, slot_ref, u_hbm, k_hbm, out_ref,
    start, mid, coef, stepped, lanes_done, rows_done, surplus, packs, low_in, high_in, lead, lead_in,
    out_a, out_b, in_a, in_b, ret_a, ret_b, back_a, back_b, slots_out, slots_in, index_v, index_s,
    load_sem, send_sem, recv_sem, lead_send, lead_recv, slot_sems, out_sems, back_sems,
):
    g = lax.axis_index("grid")
    d = lax.axis_index("dom")
    me = g * 8 + d
    x_at, y_at = lax.div(g, 4), lax.rem(g, 4)
    z_at, core = lax.div(d, 2), lax.rem(d, 2)
    barrier = pltpu.get_barrier_semaphore()

    load_u = pltpu.make_async_copy(u_hbm, start.at[pl.ds(PAD * 8, 1024)], load_sem.at[0])
    load_k = pltpu.make_async_copy(k_hbm, coef.at[pl.ds(0, 1024)], load_sem.at[1])
    load_u.start()
    load_k.start()

    def peer(offset):
        px = lax.rem(x_at + offset[0], 4)
        py = lax.rem(y_at + offset[1], 4)
        pz = lax.rem(z_at + offset[2], 4)
        return px * 4 + py, pz * 2 + lax.rem(core + offset[3], 2)

    offsets = peer_offsets()
    for offset in offsets:
        pl.semaphore_signal(barrier, inc=1, device_id=peer(offset), device_id_type=MESH)

    owners = own_ref[...]
    own_row = jnp.broadcast_to(owners, (128, 128))
    own_col = own_row.T
    row = lax.broadcasted_iota(I32, (128, 128), 0)
    col = lax.broadcasted_iota(I32, (128, 128), 1)
    earlier = jnp.where((own_row == own_col) & (row < col), 1, 0)
    rank = jnp.sum(earlier, axis=0, keepdims=True)
    rank_row = jnp.broadcast_to(rank, (128, 128))
    rank_col = rank_row.T
    slot_row = jnp.broadcast_to(slot_ref[...], (128, 128))
    table = jnp.full((128, 128), -1, I32)
    index_v[...] = jnp.zeros((8, 128), I32)
    index_v[0:1] = 2 * owners + rank
    for r in range(2):
        to_owner = (own_col == col) & (rank_col == r)
        index_v[1 + r : 2 + r] = jnp.sum(jnp.where(to_owner, row, 0), axis=0, keepdims=True)
        of_block = (own_row == row) & (rank_row == r)
        ids = jnp.sum(jnp.where(of_block, slot_row + 1, 0), axis=1, keepdims=True) - 1
        table = jnp.where(col == r, ids, table)
    slots_out[:, 0, :] = table
    fetch = pltpu.make_async_copy(index_v, index_s, load_sem.at[2])
    fetch.start()

    zero_pad = jnp.zeros((PAD * 8, 128), F32)
    for buffer in (start, mid):
        buffer[0 : PAD * 8] = zero_pad
        buffer[(TILE_HALO + COLS) * 8 : (TILE_HALO + COLS + PAD) * 8] = zero_pad
    halo = TILE_HALO * 8
    start[halo : halo + COLS * 8] = jnp.zeros((COLS * 8, 128), F32)
    coef[1024:1536] = jnp.zeros((512, 128), F32)
    stepped[1024:1032] = jnp.zeros((8, 128), F32)

    def halo_rows(s):
        return pl.ds(halo + s, COLS, stride=8)

    def halo_coef(s):
        return pl.ds(1024 + s, COLS, stride=8)

    base = PAD * 8
    load_u.wait()
    load_k.wait()
    packs[0, 0:64] = start[node_rows(base, 0), :]
    packs[0, 64:128] = start[node_rows(base, 1), :]
    packs[0, 128:192] = coef[node_rows(0, 0), :]
    packs[1, 0:64] = start[node_rows(base, 14), :]
    packs[1, 64:128] = start[node_rows(base, 15), :]
    packs[1, 128:192] = coef[node_rows(0, 15), :]
    start[halo_rows(2), :] = packs[0, 0:64]
    start[halo_rows(3), :] = packs[0, 64:128]
    start[halo_rows(4), :] = packs[1, 0:64]
    start[halo_rows(5), :] = packs[1, 64:128]
    coef[halo_coef(2), :] = packs[0, 128:192]
    coef[halo_coef(5), :] = packs[1, 128:192]

    l1 = lev_ref[0, 0]
    l2 = lev_ref[0, 1]
    l3 = lev_ref[0, 2]
    both = l1 + l2
    lane = lax.broadcasted_iota(I32, (8, 128), 1)
    sub = lax.broadcasted_iota(I32, (8, 128), 0)
    span2 = jnp.left_shift(1, l1)
    span3 = jnp.minimum(jnp.left_shift(1, both), 128)
    skip3 = jnp.where(both == 8, 2, jnp.where(both == 9, 4, jnp.where(both == 10, 8, 1)))
    last1 = jnp.left_shift(1, l1) - 1
    last2 = jnp.left_shift(1, l2) - 1
    last3 = jnp.left_shift(1, l3) - 1
    drift1 = 0.1 * vel_ref[0]
    drift2 = 0.1 * vel_ref[1]
    drift3 = 0.1 * vel_ref[2]
    drift4 = 0.1 * vel_ref[3]
    from_next2 = lane < span2
    from_last2 = lane >= 128 - span2
    from_next3 = lane < span3
    from_last3 = lane >= 128 - span3
    ahead2 = (128 - span2) & 127
    behind2 = span2 & 127
    ahead3 = (128 - span3) & 127
    behind3 = span3 & 127

    def masks(c):
        cell = c * 128 + lane
        i1 = cell & last1
        i2 = jnp.right_shift(cell, l1) & last2
        i3 = jnp.right_shift(cell, both) & last3
        return (i1 != last1, i1 != 0, i2 != last2, i2 != 0, i3 != last3, i3 != 0)

    def advance(ref, at, x, ahead4, behind4, diff, ok):
        p1 = jnp.where(ok[0], pltpu.roll(x, 127, 1), 0.0)
        m1 = jnp.where(ok[1], pltpu.roll(x, 1, 1), 0.0)
        p2 = pltpu.roll(jnp.where(from_next2, ref[tile(at + 1), :], x), ahead2, 1)
        p2 = jnp.where(ok[2], p2, 0.0)
        m2 = pltpu.roll(jnp.where(from_last2, ref[tile(at - 1), :], x), behind2, 1)
        m2 = jnp.where(ok[3], m2, 0.0)
        p3 = pltpu.roll(jnp.where(from_next3, ref[tile(at + skip3), :], x), ahead3, 1)
        p3 = jnp.where(ok[4], p3, 0.0)
        m3 = pltpu.roll(jnp.where(from_last3, ref[tile(at - skip3), :], x), behind3, 1)
        m3 = jnp.where(ok[5], m3, 0.0)
        second = ((p1 + m1) + (p2 + m2)) + ((p3 + m3) + (ahead4 + behind4)) - 8.0 * x
        drift = (drift1 * (p1 - m1) + drift2 * (p2 - m2)) + (
            drift3 * (p3 - m3) + drift4 * (ahead4 - behind4)
        )
        return x + 0.1 * diff * second - drift

    def both_groups(ref, c, target, offset, with_halo):
        ok = masks(c)
        x0 = ref[tile(PAD + c), :]
        x1 = ref[tile(PAD + COLS + c), :]
        down0, up1 = x0, x1
        if with_halo:
            xh = ref[tile(TILE_HALO + c), :]
            down0 = jnp.where(sub == 7, pltpu.roll(xh, 6, 0), x0)
            up1 = jnp.where(sub == 0, pltpu.roll(xh, 2, 0), x1)
        value0 = advance(
            ref, PAD + c, x0, pltpu.roll(jnp.where(sub == 0, x1, x0), 7, 0),
            pltpu.roll(down0, 1, 0), coef[tile(c), :], ok,
        )
        value1 = advance(
            ref, PAD + COLS + c, x1, pltpu.roll(up1, 7, 0),
            pltpu.roll(jnp.where(sub == 7, x0, x1), 1, 0), coef[tile(COLS + c), :], ok,
        )
        target[tile(offset + c), :] = value0
        target[tile(offset + COLS + c), :] = value1

    unrolled(COLS, 2, lambda c: both_groups(start, c, mid, PAD, False))

    pl.semaphore_wait(barrier, 127)

    def down():
        return pltpu.make_async_remote_copy(
            src_ref=packs.at[0], dst_ref=high_in, send_sem=send_sem.at[0], recv_sem=recv_sem.at[0],
            device_id=(g, lax.rem(d + 7, 8)), device_id_type=MESH,
        )

    def upward():
        return pltpu.make_async_remote_copy(
            src_ref=packs.at[1], dst_ref=low_in, send_sem=send_sem.at[1], recv_sem=recv_sem.at[1],
            device_id=(g, lax.rem(d + 1, 8)), device_id_type=MESH,
        )

    @pl.when(d > 0)
    def _():
        down().start()

    @pl.when(d < 7)
    def _():
        upward().start()

    def send_all(sources, targets, sems, size):
        for offset in offsets:
            pg, pd = peer(offset)
            pltpu.make_async_remote_copy(
                src_ref=sources.at[pl.ds((pg * 8 + pd) * size, size)],
                dst_ref=targets.at[pl.ds(me * size, size)],
                send_sem=sems.at[0], recv_sem=sems.at[1],
                device_id=(pg, pd), device_id_type=MESH,
            ).start()
        targets[pl.ds(me * size, size)] = sources[pl.ds(me * size, size)]

    def all_of(sources, targets, sems, size):
        return pltpu.make_async_remote_copy(
            src_ref=sources.at[pl.ds(0, 127 * size)], dst_ref=targets.at[pl.ds(0, 127 * size)],
            send_sem=sems.at[0], recv_sem=sems.at[1],
            device_id=(g, lax.rem(d + 1, 8)), device_id_type=MESH,
        )

    send_all(slots_out, slots_in, slot_sems, 1)
    fetch.wait()

    zero_rows = jnp.zeros((192, 128), F32)

    @pl.when(d == 0)
    def _():
        low_in[...] = zero_rows

    @pl.when(d == 7)
    def _():
        high_in[...] = zero_rows

    here, after = lane_matrices(l1, l2, sign_ref[0].astype(F32))
    here = here.astype(BF16)
    after = after.astype(BF16)

    @pl.when(d < 7)
    def _():
        down().wait_recv()

    @pl.when(d > 0)
    def _():
        upward().wait_recv()

    start[halo_rows(0), :] = low_in[0:64]
    start[halo_rows(1), :] = low_in[64:128]
    start[halo_rows(6), :] = high_in[0:64]
    start[halo_rows(7), :] = high_in[64:128]
    coef[halo_coef(1), :] = low_in[128:192]
    coef[halo_coef(6), :] = high_in[128:192]
    outside = jnp.where(d == 0, 1, jnp.where(d == 7, 6, -1))

    def first_halo(c):
        xh = start[tile(TILE_HALO + c), :]
        value = advance(
            start, TILE_HALO + c, xh, pltpu.roll(xh, 7, 0), pltpu.roll(xh, 1, 0),
            coef[tile(2 * COLS + c), :], masks(c),
        )
        mid[tile(TILE_HALO + c), :] = jnp.where(sub == outside, 0.0, value)

    unrolled(COLS, 4, first_halo)
    mid[node_rows(base, 0), :] = mid[halo_rows(2), :]
    mid[node_rows(base, 15), :] = mid[halo_rows(5), :]
    unrolled(COLS, 2, lambda c: both_groups(mid, c, stepped, 0, True))

    straddles = jnp.where(both > 7, jnp.where(l1 < 7, 1, 0), jnp.where(both == 6, 1, 0))
    mask_a = jnp.where(both > 7, skip3 - 1, COLS - 1)
    no_next = jnp.where(straddles == 1, mask_a, 0)
    limit_a = jnp.where(both > 7, span2, span3)
    mask_b = jnp.where(both > 7, COLS - skip3, 0)
    inside = lane < limit_a
    chunk = 128

    def lane_part(i):
        at = i * chunk
        x = stepped[pl.ds(at, chunk), :]
        beyond = stepped[pl.ds(at + 8, chunk), :]
        column = jnp.right_shift(at + lax.broadcasted_iota(I32, (chunk, 128), 0), 3)
        beyond = jnp.where((column & no_next) != no_next, beyond, 0.0)
        lanes_done[pl.ds(at, chunk), :] = dot_exact(x, here) + dot_exact(beyond, after)

    def columns(source, target, t, mask, chosen):
        def step(c):
            j = c & mask
            off = j & (-j)
            has_up = (j != 0) & (j + off <= mask)
            weight = jnp.where(j != 0, 0.5, 0.0)
            weight_up = jnp.where(has_up, 0.5, 0.0)
            at = t * COLS + c
            update = weight * source[tile(at - off), :]
            update = update + weight_up * source[tile(jnp.where(has_up, at + off, at)), :]
            if chosen is not None:
                update = jnp.where(chosen, update, 0.0)
            target[tile(at), :] = source[tile(at), :] - update

        unrolled(COLS, 4, step)

    def lead_copy(slot, target, sent):
        return pltpu.make_async_remote_copy(
            src_ref=lead, dst_ref=lead_in.at[slot], send_sem=lead_send.at[sent],
            recv_sem=lead_recv.at[slot], device_id=(g, target), device_id_type=MESH,
        )

    routes = [(0, d > 0, lax.rem(d + 7, 8)), (1, lax.rem(d, 2) == 0, lax.rem(d + 1, 8))]
    routes += [(1, d == 0, 2), (1, d == 0, 4), (1, d == 4, 6), (2, d == 4, 2)]
    for t in range(2):
        for i in range(512 // chunk):
            lane_part(t * (512 // chunk) + i)
        columns(lanes_done, rows_done, t, mask_a, inside)
        columns(rows_done, lanes_done, t, mask_b, None)
        if t == 0:
            lead[...] = lanes_done[node_rows(0, 0), :]
            for sent, (slot, condition, target) in enumerate(routes):

                @pl.when(condition)
                def _():
                    lead_copy(slot, target, sent).start()

    odd = (sub & 1) == 1
    two = (sub & 3) == 2
    four = sub == 4

    def fourth(c):
        x0 = lanes_done[tile(c), :]
        x1 = lanes_done[tile(COLS + c), :]
        for t, x, y, special in ((0, x0, jnp.where(sub == 0, x1, x0), 0.0), (1, x1, jnp.where(sub == 0, 0.0, x1), x0)):
            near1 = pltpu.roll(y, 7, 0) + pltpu.roll(x, 1, 0)
            near2 = pltpu.roll(y, 6, 0) + pltpu.roll(x, 2, 0)
            near4 = pltpu.roll(y, 4, 0) + pltpu.roll(x, 4, 0)
            near = jnp.where(odd, near1, jnp.where(two, near2, jnp.where(four, near4, special)))
            surplus[tile(t * COLS + c), :] = x - 0.5 * near

    unrolled(COLS, 2, fourth)

    zero_lead = jnp.zeros((64, 128), F32)

    @pl.when(d == 7)
    def _():
        lead_in[0] = zero_lead

    @pl.when(d == 0)
    def _():
        lead_in[1] = zero_lead

    @pl.when(d != 2)
    def _():
        lead_in[2] = zero_lead

    @pl.when(d < 7)
    def _():
        lead_copy(0, lax.rem(d + 7, 8), 0).wait_recv()

    @pl.when(d > 0)
    def _():
        lead_copy(1, lax.rem(d + 1, 8), 0).wait_recv()

    @pl.when(d == 2)
    def _():
        lead_copy(2, lax.rem(d + 1, 8), 0).wait_recv()

    following = 0.5 * lead_in[0]
    use_next = jnp.where(lax.rem(d, 2) == 1, 1.0, 0.0)
    around = 0.5 * (lead_in[1] + lead_in[2]) + use_next * following
    surplus[node_rows(0, 0), :] = surplus[node_rows(0, 0), :] - around
    for node in (8, 12, 14, 15):
        surplus[node_rows(0, node), :] = surplus[node_rows(0, node), :] - following

    def block_rows(block, half):
        node = lax.div(block, 8)
        at = (lax.div(node, 8) * COLS + lax.rem(block, 8) * 8) * 8 + lax.rem(node, 8)
        return pl.ds(at + half * 32, 4, stride=8)

    def pack(half, target):
        def step(o):
            for r in range(2):
                target[pl.ds(o * 8 + r * 4, 4), :] = surplus[block_rows(index_s[1 + r, o], half), :]

        unrolled(128, 4, step)

    halves = ((out_a, in_a, ret_a, back_a), (out_b, in_b, ret_b, back_b))
    for half, (outgoing, arrived, _, _) in enumerate(halves):
        pack(half, outgoing)
        send_all(outgoing, arrived, out_sems.at[half], 8)

    all_of(slots_out, slots_in, slot_sems, 1).wait_recv()
    ids_col = slots_in[:, 0, :]
    ids_row = ids_col.T
    equal = []
    for r in range(2):
        of_r = jnp.broadcast_to(ids_col[:, r : r + 1], (128, 128))
        parts = [
            jnp.where(of_r == jnp.broadcast_to(ids_row[s : s + 1, :], (128, 128)), 1.0, 0.0)
            for s in range(2)
        ]
        equal.append(jnp.concatenate(parts, axis=1))
    equal = jnp.concatenate(equal, axis=0).astype(BF16)

    for half, (outgoing, arrived, returned, back) in enumerate(halves):
        all_of(outgoing, arrived, out_sems.at[half], 8).wait_recv()
        for j in range(4):
            block = jnp.concatenate(
                [arrived[pl.ds(r * 4 + j, 128, stride=8), :] for r in range(2)], axis=0
            )
            first = block.astype(BF16)
            rest = block - first.astype(F32)
            second = rest.astype(BF16)
            third = (rest - second.astype(F32)).astype(BF16)
            total = jnp.dot(equal, third, preferred_element_type=F32)
            total = total + jnp.dot(equal, second, preferred_element_type=F32)
            total = total + jnp.dot(equal, first, preferred_element_type=F32)
            for r in range(2):
                returned[pl.ds(r * 4 + j, 128, stride=8), :] = total[r * 128 : (r + 1) * 128]
        send_all(returned, back, back_sems.at[half], 8)

    for half, (_, _, returned, back) in enumerate(halves):
        all_of(returned, back, back_sems.at[half], 8).wait_recv()

        def unpack(b):
            out_ref[block_rows(b, half), :] = back[pl.ds(index_s[0, b] * 4, 4), :]

        unrolled(128, 4, unpack)

    @pl.when(d > 0)
    def _():
        down().wait_send()

    @pl.when(d < 7)
    def _():
        upward().wait_send()

    for sent, (slot, condition, target) in enumerate(routes):

        @pl.when(condition)
        def _():
            lead_copy(slot, target, sent).wait_send()

    all_of(slots_out, slots_in, slot_sems, 1).wait_send()
    for half, (outgoing, arrived, returned, back) in enumerate(halves):
        all_of(outgoing, arrived, out_sems.at[half], 8).wait_send()
        all_of(returned, back, back_sems.at[half], 8).wait_send()


def body(concentration, diffusion, velocity, levels, grid_signs, owner_list, slot_list):
    def tiled(block):
        return block.reshape(2, 8, COLS, 128).transpose(0, 2, 1, 3).reshape(1024, 128)

    smem = pl.BlockSpec(memory_space=pltpu.SMEM)
    vmem = pl.BlockSpec(memory_space=pltpu.VMEM)
    anywhere = pl.BlockSpec(memory_space=pl.ANY)
    total_rows = (TILE_HALO + COLS + PAD) * 8
    rows = [total_rows, total_rows, 1552, 1032, 1032, 1032, 1032]
    combined = pl.pallas_call(
        combine_kernel,
        out_shape=jax.ShapeDtypeStruct((1032, 128), F32),
        in_specs=[smem, smem, smem, vmem, vmem, anywhere, anywhere],
        out_specs=vmem,
        scratch_shapes=[pltpu.VMEM((n, 128), F32) for n in rows]
        + [
            pltpu.VMEM((2, 192, 128), F32),
            pltpu.VMEM((192, 128), F32),
            pltpu.VMEM((192, 128), F32),
            pltpu.VMEM((64, 128), F32),
            pltpu.VMEM((3, 64, 128), F32),
        ]
        + [pltpu.VMEM((1032, 128), F32) for _ in range(8)]
        + [
            pltpu.VMEM((128, 1, 128), I32),
            pltpu.VMEM((128, 1, 128), I32),
            pltpu.VMEM((8, 128), I32),
            pltpu.SMEM((8, 128), I32),
            pltpu.SemaphoreType.DMA((3,)),
            pltpu.SemaphoreType.DMA((2,)),
            pltpu.SemaphoreType.DMA((2,)),
            pltpu.SemaphoreType.DMA((6,)),
            pltpu.SemaphoreType.DMA((3,)),
            pltpu.SemaphoreType.DMA((2,)),
            pltpu.SemaphoreType.DMA((2, 2)),
            pltpu.SemaphoreType.DMA((2, 2)),
        ],
        compiler_params=pltpu.CompilerParams(collective_id=0, has_side_effects=True),
        name="combine",
    )(levels, velocity, grid_signs, owner_list, slot_list, tiled(concentration), tiled(diffusion))
    return combined[:1024].reshape(2, COLS, 8, 128).transpose(0, 2, 1, 3).reshape(1, 16, COLS * 128)


def solution(mesh):
    return jax.shard_map(
        body,
        mesh=mesh,
        in_specs=(
            P("grid", "dom", None),
            P("grid", "dom", None),
            P(),
            P("grid", None),
            P("grid"),
            P(("grid", "dom"), None),
            P(("grid", "dom"), None),
        ),
        out_specs=P("grid", "dom", None),
        check_vma=False,
    )
```

```python
import jax
import jax.numpy as jnp
from jax import lax
from jax.experimental import pallas as pl
from jax.experimental.pallas import tpu as pltpu
from jax.sharding import PartitionSpec as P

MESH = pl.DeviceIdType.MESH
F32 = jnp.float32
BF16 = jnp.bfloat16
I32 = jnp.int32

COLS = 64
PAD = 8
TILE_HALO = PAD + 2 * COLS


def tile(at):
    return pl.ds(at * 8, 8)


def node_rows(base, node):
    return pl.ds(base + (node // 8) * COLS * 8 + node % 8, COLS, stride=8)


def dot_split(left, right):
    first = left.astype(BF16)
    second = (left - first.astype(F32)).astype(BF16)
    total = jnp.dot(second, right, preferred_element_type=F32)
    return total + jnp.dot(first, right, preferred_element_type=F32)


def lane_matrices(l1, l2, sign):
    source = lax.broadcasted_iota(I32, (128, 128), 0)
    target = lax.broadcasted_iota(I32, (128, 128), 1)
    both = l1 + l2
    low = [0, l1, both]
    top = [jnp.minimum(l1, 7), jnp.minimum(both, 7), 7]
    here = jnp.full((128, 128), sign, F32)
    after = jnp.full((128, 128), sign, F32)
    for field in range(3):
        width = jnp.maximum(top[field] - jnp.minimum(low[field], 7), 0)
        mask = jnp.left_shift(1, width) - 1
        shift = jnp.minimum(low[field], 7)
        fro = jnp.right_shift(source, shift) & mask
        to = jnp.right_shift(target, shift) & mask
        bit = to & (-to)
        same = jnp.where(fro == to, 1.0, 0.0)
        near = jnp.where((to != 0) & ((fro == to - bit) | (fro == to + bit)), -0.5, 0.0)
        plain = same + near
        wraps = (to != 0) & (to + bit == mask + 1) & (fro == 0)
        carry = jnp.where(wraps, -0.5, 0.0)
        here = here * plain
        if field == 0:
            after = after * plain
        elif field == 1:
            after = after * jnp.where(both > 6, jnp.where(width > 0, carry, 0.0), plain)
        else:
            after = after * jnp.where(both > 6, 1.0, carry)
    return here, after


def peer_offsets():
    offsets = [(k // 32, k // 8 % 4, k // 2 % 4, k % 2) for k in range(1, 128)]
    return sorted(offsets, key=lambda o: -sum(min(v, 4 - v) for v in o[:3]))


def unrolled(count, factor, step):
    def some(i, carry):
        for k in range(factor):
            step(i * factor + k)
        return carry

    lax.fori_loop(0, count // factor, some, 0)


def combine_kernel(
    lev_ref, vel_ref, sign_ref, own_ref, slot_ref, u_hbm, k_hbm, out_ref,
    start, mid, coef, stepped, lanes_done, rows_done, surplus, packs, low_in, high_in, lead, lead_in,
    out_a, out_b, in_a, in_b, ret_a, ret_b, back_a, back_b, slots_out, slots_in, index_v, index_s,
    load_sem, send_sem, recv_sem, lead_send, lead_recv, slot_sems, out_sems, back_sems,
):
    g = lax.axis_index("grid")
    d = lax.axis_index("dom")
    me = g * 8 + d
    x_at, y_at = g // 4, g % 4
    z_at, core = d // 2, d % 2
    grids = [((x_at + i) % 4) * 4 + (y_at + j) % 4 for i in range(4) for j in range(4)]
    doms = [((z_at + i) % 4) * 2 + (core + j) % 2 for i in range(4) for j in range(2)]
    barrier = pltpu.get_barrier_semaphore()

    load_u = pltpu.make_async_copy(u_hbm, start.at[pl.ds(PAD * 8, 1024)], load_sem.at[0])
    load_k = pltpu.make_async_copy(k_hbm, coef.at[pl.ds(0, 1024)], load_sem.at[1])
    load_u.start()
    load_k.start()

    def peer(offset):
        return grids[offset[0] * 4 + offset[1]], doms[offset[2] * 2 + offset[3]]

    offsets = peer_offsets()
    for offset in offsets:
        pl.semaphore_signal(barrier, inc=1, device_id=peer(offset), device_id_type=MESH)

    owners = own_ref[...]
    own_row = jnp.broadcast_to(owners, (128, 128))
    own_col = own_row.T
    row = lax.broadcasted_iota(I32, (128, 128), 0)
    col = lax.broadcasted_iota(I32, (128, 128), 1)
    earlier = jnp.where((own_row == own_col) & (row < col), 1, 0)
    rank = jnp.sum(earlier, axis=0, keepdims=True)
    rank_row = jnp.broadcast_to(rank, (128, 128))
    rank_col = rank_row.T
    slot_row = jnp.broadcast_to(slot_ref[...], (128, 128))
    table = jnp.full((128, 128), -1, I32)
    index_v[...] = jnp.zeros((8, 128), I32)
    second_one = jnp.minimum(rank, 1)
    index_v[0:1] = 8 * owners + 4 * second_one
    index_v[3:4] = 8 * owners + 4 * (1 - second_one)
    first_row = (row // 64) * (8 * COLS) + (row % 8) * 64 + (row // 8) % 8
    for r in range(2):
        to_owner = (own_col == col) & (rank_col == r)
        index_v[1 + r : 2 + r] = jnp.sum(
            jnp.where(to_owner, first_row, 0), axis=0, keepdims=True
        )
        of_block = (own_row == row) & (rank_row == r)
        ids = jnp.sum(jnp.where(of_block, slot_row + 1, 0), axis=1, keepdims=True) - 1
        table = jnp.where(col == r, ids, table)
    slots_out[:, 0, :] = table
    fetch = pltpu.make_async_copy(index_v, index_s, load_sem.at[2])
    fetch.start()

    lanes_done[1024:1032] = jnp.zeros((8, 128), F32)
    rows_done[1024:1032] = jnp.zeros((8, 128), F32)
    halo = TILE_HALO * 8

    def halo_rows(s):
        return pl.ds(halo + s, COLS, stride=8)

    def halo_coef(s):
        return pl.ds(1024 + s, COLS, stride=8)

    base = PAD * 8
    load_u.wait()
    load_k.wait()
    packs[0, 0:64] = start[node_rows(base, 0), :]
    packs[0, 64:128] = start[node_rows(base, 1), :]
    packs[0, 128:192] = coef[node_rows(0, 0), :]
    packs[1, 0:64] = start[node_rows(base, 14), :]
    packs[1, 64:128] = start[node_rows(base, 15), :]
    packs[1, 128:192] = coef[node_rows(0, 15), :]
    start[halo_rows(2), :] = packs[0, 0:64]
    start[halo_rows(3), :] = packs[0, 64:128]
    start[halo_rows(4), :] = packs[1, 0:64]
    start[halo_rows(5), :] = packs[1, 64:128]
    coef[halo_coef(2), :] = packs[0, 128:192]
    coef[halo_coef(5), :] = packs[1, 128:192]

    l1 = lev_ref[0, 0]
    l2 = lev_ref[0, 1]
    l3 = lev_ref[0, 2]
    both = l1 + l2
    lane = lax.broadcasted_iota(I32, (8, 128), 1)
    sub = lax.broadcasted_iota(I32, (8, 128), 0)
    span2 = jnp.left_shift(1, l1)
    span3 = jnp.minimum(jnp.left_shift(1, both), 128)
    skip3 = jnp.where(both == 8, 2, jnp.where(both == 9, 4, jnp.where(both == 10, 8, 1)))
    last1 = jnp.left_shift(1, l1) - 1
    last2 = jnp.left_shift(1, l2) - 1
    last3 = jnp.left_shift(1, l3) - 1
    drift1 = 0.1 * vel_ref[0]
    drift2 = 0.1 * vel_ref[1]
    drift3 = 0.1 * vel_ref[2]
    drift4 = 0.1 * vel_ref[3]
    from_next2 = lane < span2
    from_last2 = lane >= 128 - span2
    from_next3 = lane < span3
    from_last3 = lane >= 128 - span3
    ahead2 = (128 - span2) & 127
    behind2 = span2 & 127
    ahead3 = (128 - span3) & 127
    behind3 = span3 & 127

    i1 = lane & last1
    not_last1 = i1 != last1
    not_first1 = i1 != 0

    def masks(c):
        cell = c * 128 + lane
        i2 = jnp.right_shift(cell, l1) & last2
        i3 = jnp.right_shift(cell, both) & last3
        return (not_last1, not_first1, i2 != last2, i2 != 0, i3 != last3, i3 != 0)

    def advance(ref, at, x, ahead4, behind4, diff, ok):
        p1 = jnp.where(ok[0], pltpu.roll(x, 127, 1), 0.0)
        m1 = jnp.where(ok[1], pltpu.roll(x, 1, 1), 0.0)
        p2 = pltpu.roll(jnp.where(from_next2, ref[tile(at + 1), :], x), ahead2, 1)
        p2 = jnp.where(ok[2], p2, 0.0)
        m2 = pltpu.roll(jnp.where(from_last2, ref[tile(at - 1), :], x), behind2, 1)
        m2 = jnp.where(ok[3], m2, 0.0)
        p3 = pltpu.roll(jnp.where(from_next3, ref[tile(at + skip3), :], x), ahead3, 1)
        p3 = jnp.where(ok[4], p3, 0.0)
        m3 = pltpu.roll(jnp.where(from_last3, ref[tile(at - skip3), :], x), behind3, 1)
        m3 = jnp.where(ok[5], m3, 0.0)
        second = ((p1 + m1) + (p2 + m2)) + ((p3 + m3) + (ahead4 + behind4)) - 8.0 * x
        drift = (drift1 * (p1 - m1) + drift2 * (p2 - m2)) + (
            drift3 * (p3 - m3) + drift4 * (ahead4 - behind4)
        )
        return x + 0.1 * diff * second - drift

    def both_groups(ref, c, target, offset, with_halo):
        ok = masks(c)
        x0 = ref[tile(PAD + c), :]
        x1 = ref[tile(PAD + COLS + c), :]
        down0, up1 = x0, x1
        if with_halo:
            xh = ref[tile(TILE_HALO + c), :]
            down0 = jnp.where(sub == 7, pltpu.roll(xh, 6, 0), x0)
            up1 = jnp.where(sub == 0, pltpu.roll(xh, 2, 0), x1)
        value0 = advance(
            ref, PAD + c, x0, pltpu.roll(jnp.where(sub == 0, x1, x0), 7, 0),
            pltpu.roll(down0, 1, 0), coef[tile(c), :], ok,
        )
        value1 = advance(
            ref, PAD + COLS + c, x1, pltpu.roll(up1, 7, 0),
            pltpu.roll(jnp.where(sub == 7, x0, x1), 1, 0), coef[tile(COLS + c), :], ok,
        )
        target[tile(offset + c), :] = value0
        target[tile(offset + COLS + c), :] = value1

    unrolled(COLS, 2, lambda c: both_groups(start, c, mid, PAD, False))

    pl.semaphore_wait(barrier, 127)

    def down():
        return pltpu.make_async_remote_copy(
            src_ref=packs.at[0], dst_ref=high_in, send_sem=send_sem.at[0], recv_sem=recv_sem.at[0],
            device_id=(g, lax.rem(d + 7, 8)), device_id_type=MESH,
        )

    def upward():
        return pltpu.make_async_remote_copy(
            src_ref=packs.at[1], dst_ref=low_in, send_sem=send_sem.at[1], recv_sem=recv_sem.at[1],
            device_id=(g, lax.rem(d + 1, 8)), device_id_type=MESH,
        )

    @pl.when(d > 0)
    def _():
        down().start()

    @pl.when(d < 7)
    def _():
        upward().start()

    def send_all(sources, targets, sems, size):
        for offset in offsets:
            pg, pd = peer(offset)
            pltpu.make_async_remote_copy(
                src_ref=sources.at[pl.ds((pg * 8 + pd) * size, size)],
                dst_ref=targets.at[pl.ds(me * size, size)],
                send_sem=sems.at[0], recv_sem=sems.at[1],
                device_id=(pg, pd), device_id_type=MESH,
            ).start()
        targets[pl.ds(me * size, size)] = sources[pl.ds(me * size, size)]

    def all_of(sources, targets, sems, size):
        return pltpu.make_async_remote_copy(
            src_ref=sources.at[pl.ds(0, 127 * size)], dst_ref=targets.at[pl.ds(0, 127 * size)],
            send_sem=sems.at[0], recv_sem=sems.at[1],
            device_id=(g, lax.rem(d + 1, 8)), device_id_type=MESH,
        )

    send_all(slots_out, slots_in, slot_sems, 1)
    fetch.wait()

    zero_rows = jnp.zeros((192, 128), F32)

    @pl.when(d == 0)
    def _():
        low_in[...] = zero_rows

    @pl.when(d == 7)
    def _():
        high_in[...] = zero_rows

    here, after = lane_matrices(l1, l2, sign_ref[0].astype(F32))
    here = here.astype(BF16)
    after = after.astype(BF16)

    @pl.when(d < 7)
    def _():
        down().wait_recv()

    @pl.when(d > 0)
    def _():
        upward().wait_recv()

    start[halo_rows(0), :] = low_in[0:64]
    start[halo_rows(1), :] = low_in[64:128]
    start[halo_rows(6), :] = high_in[0:64]
    start[halo_rows(7), :] = high_in[64:128]
    coef[halo_coef(1), :] = low_in[128:192]
    coef[halo_coef(6), :] = high_in[128:192]
    outside = jnp.where(d == 0, 1, jnp.where(d == 7, 6, -1))

    def first_halo(c):
        xh = start[tile(TILE_HALO + c), :]
        value = advance(
            start, TILE_HALO + c, xh, pltpu.roll(xh, 7, 0), pltpu.roll(xh, 1, 0),
            coef[tile(2 * COLS + c), :], masks(c),
        )
        mid[tile(TILE_HALO + c), :] = jnp.where(sub == outside, 0.0, value)

    unrolled(COLS, 4, first_halo)
    mid[node_rows(base, 0), :] = mid[halo_rows(2), :]
    mid[node_rows(base, 15), :] = mid[halo_rows(5), :]
    unrolled(COLS, 2, lambda c: both_groups(mid, c, stepped, 0, True))

    straddles = jnp.where(both > 7, jnp.where(l1 < 7, 1, 0), jnp.where(both == 6, 1, 0))
    mask_a = jnp.where(both > 7, skip3 - 1, COLS - 1)
    no_next = jnp.where(straddles == 1, mask_a, 0)
    limit_a = jnp.where(both > 7, span2, span3)
    mask_b = jnp.where(both > 7, COLS - skip3, 0)
    inside = lane < limit_a
    chunk = 128

    def lane_part(i):
        at = i * chunk
        x = stepped[pl.ds(at, chunk), :]
        beyond = stepped[pl.ds(at + 8, chunk), :]
        column = jnp.right_shift(at + lax.broadcasted_iota(I32, (chunk, 128), 0), 3)
        beyond = jnp.where((column & no_next) != no_next, beyond, 0.0)
        lanes_done[pl.ds(at, chunk), :] = dot_split(x, here) + dot_split(beyond, after)

    nothing = 2 * COLS

    def columns(source, target, mask, chosen):
        def step(c):
            j = c & mask
            off = j & (-j)
            has_up = (j != 0) & (j + off <= mask)
            for t in range(2):
                lower = jnp.where(j != 0, t * COLS + c - off, nothing)
                upper = jnp.where(has_up, t * COLS + c + off, nothing)
                update = 0.5 * (source[tile(lower), :] + source[tile(upper), :])
                if chosen is not None:
                    update = jnp.where(chosen, update, 0.0)
                target[tile(t * COLS + c), :] = source[tile(t * COLS + c), :] - update

        unrolled(COLS, 4, step)

    def lead_copy(slot, target, sent):
        return pltpu.make_async_remote_copy(
            src_ref=lead, dst_ref=lead_in.at[slot], send_sem=lead_send.at[sent],
            recv_sem=lead_recv.at[slot], device_id=(g, target), device_id_type=MESH,
        )

    routes = [(0, d > 0, lax.rem(d + 7, 8)), (1, lax.rem(d, 2) == 0, lax.rem(d + 1, 8))]
    routes += [(1, d == 0, 2), (1, d == 0, 4), (1, d == 4, 6), (2, d == 4, 2)]
    for i in range(1024 // chunk):
        lane_part(i)
    columns(lanes_done, rows_done, mask_a, inside)
    columns(rows_done, lanes_done, mask_b, None)
    lead[...] = lanes_done[node_rows(0, 0), :]
    for sent, (slot, condition, target) in enumerate(routes):

        @pl.when(condition)
        def _():
            lead_copy(slot, target, sent).start()

    odd = (sub & 1) == 1
    two = (sub & 3) == 2
    four = sub == 4

    def fourth(c):
        x0 = lanes_done[tile(c), :]
        x1 = lanes_done[tile(COLS + c), :]
        for t, x, y, special in ((0, x0, jnp.where(sub == 0, x1, x0), 0.0), (1, x1, jnp.where(sub == 0, 0.0, x1), x0)):
            near1 = pltpu.roll(y, 7, 0) + pltpu.roll(x, 1, 0)
            near2 = pltpu.roll(y, 6, 0) + pltpu.roll(x, 2, 0)
            near4 = pltpu.roll(y, 4, 0) + pltpu.roll(x, 4, 0)
            near = jnp.where(odd, near1, jnp.where(two, near2, jnp.where(four, near4, special)))
            surplus[tile(t * COLS + c), :] = x - 0.5 * near

    unrolled(COLS, 2, fourth)

    all_of(slots_out, slots_in, slot_sems, 1).wait_recv()
    ids_col = slots_in[:, 0, :]
    ids_row = ids_col.T
    equal = []
    for r in range(2):
        of_r = jnp.broadcast_to(ids_col[:, r : r + 1], (128, 128))
        parts = [
            jnp.where(of_r == jnp.broadcast_to(ids_row[s : s + 1, :], (128, 128)), 1.0, 0.0)
            for s in range(2)
        ]
        equal.append(jnp.concatenate(parts, axis=1))
    equal = jnp.concatenate(equal, axis=0).astype(BF16)

    zero_lead = jnp.zeros((64, 128), F32)

    @pl.when(d == 7)
    def _():
        lead_in[0] = zero_lead

    @pl.when(d == 0)
    def _():
        lead_in[1] = zero_lead

    @pl.when(d != 2)
    def _():
        lead_in[2] = zero_lead

    @pl.when(d < 7)
    def _():
        lead_copy(0, lax.rem(d + 7, 8), 0).wait_recv()

    @pl.when(d > 0)
    def _():
        lead_copy(1, lax.rem(d + 1, 8), 0).wait_recv()

    @pl.when(d == 2)
    def _():
        lead_copy(2, lax.rem(d + 1, 8), 0).wait_recv()

    following = 0.5 * lead_in[0]
    use_next = jnp.where(lax.rem(d, 2) == 1, 1.0, 0.0)
    around = 0.5 * (lead_in[1] + lead_in[2]) + use_next * following
    surplus[node_rows(0, 0), :] = surplus[node_rows(0, 0), :] - around
    for node in (8, 12, 14, 15):
        surplus[node_rows(0, node), :] = surplus[node_rows(0, node), :] - following

    for o in range(128):
        of_rank = [surplus[pl.ds(index_s[1 + r, o], 8, stride=8), :] for r in range(2)]
        turned = pltpu.roll(of_rank[1], 4, 0)
        out_a[o * 8 : o * 8 + 8, :] = jnp.where(sub < 4, of_rank[0], turned)
        out_b[o * 8 : o * 8 + 8, :] = jnp.where(sub < 4, turned, of_rank[0])

    halves = ((out_a, in_a, ret_a, back_a), (out_b, in_b, ret_b, back_b))
    for half, (outgoing, arrived, _, _) in enumerate(halves):
        send_all(outgoing, arrived, out_sems.at[half], 8)

    for half, (outgoing, arrived, returned, back) in enumerate(halves):
        all_of(outgoing, arrived, out_sems.at[half], 8).wait_recv()
        for j in range(4):
            block = jnp.concatenate(
                [arrived[pl.ds((r ^ half) * 4 + j, 128, stride=8), :] for r in range(2)], axis=0
            )
            first = block.astype(BF16)
            second = (block - first.astype(F32)).astype(BF16)
            total = jnp.dot(equal, second, preferred_element_type=F32)
            total = total + jnp.dot(equal, first, preferred_element_type=F32)
            for r in range(2):
                returned[pl.ds((r ^ half) * 4 + j, 128, stride=8), :] = total[
                    r * 128 : (r + 1) * 128
                ]
        send_all(returned, back, back_sems.at[half], 8)

    for half, (_, _, returned, back) in enumerate(halves):
        all_of(returned, back, back_sems.at[half], 8).wait_recv()

        for block in range(128):
            at = (block // 64) * (8 * COLS) + (block % 8) * 64 + (block // 8) % 8 + half * 32
            out_ref[pl.ds(at, 4, stride=8), :] = back[pl.ds(index_s[3 * half, block], 4), :]

    @pl.when(d > 0)
    def _():
        down().wait_send()

    @pl.when(d < 7)
    def _():
        upward().wait_send()

    for sent, (slot, condition, target) in enumerate(routes):

        @pl.when(condition)
        def _():
            lead_copy(slot, target, sent).wait_send()

    all_of(slots_out, slots_in, slot_sems, 1).wait_send()
    for half, (outgoing, arrived, returned, back) in enumerate(halves):
        all_of(outgoing, arrived, out_sems.at[half], 8).wait_send()
        all_of(returned, back, back_sems.at[half], 8).wait_send()


def body(concentration, diffusion, velocity, levels, grid_signs, owner_list, slot_list):
    def in_hbm(array):
        return pltpu.with_memory_space_constraint(array, pltpu.HBM)

    def tiled(block):
        rows = block.reshape(2, 8, COLS, 128).transpose(0, 2, 1, 3).reshape(1024, 128)
        return in_hbm(rows)

    smem = pl.BlockSpec(memory_space=pltpu.SMEM)
    vmem = pl.BlockSpec(memory_space=pltpu.VMEM)
    anywhere = pl.BlockSpec(memory_space=pltpu.HBM)
    total_rows = (TILE_HALO + COLS + PAD) * 8
    rows = [total_rows, total_rows, 1552, 1032, 1032, 1032, 1032]
    combined = pl.pallas_call(
        combine_kernel,
        out_shape=jax.ShapeDtypeStruct((1032, 128), F32),
        in_specs=[smem, smem, smem, vmem, vmem, anywhere, anywhere],
        out_specs=vmem,
        scratch_shapes=[pltpu.VMEM((n, 128), F32) for n in rows]
        + [
            pltpu.VMEM((2, 192, 128), F32),
            pltpu.VMEM((192, 128), F32),
            pltpu.VMEM((192, 128), F32),
            pltpu.VMEM((64, 128), F32),
            pltpu.VMEM((3, 64, 128), F32),
        ]
        + [pltpu.VMEM((1032, 128), F32) for _ in range(8)]
        + [
            pltpu.VMEM((128, 1, 128), I32),
            pltpu.VMEM((128, 1, 128), I32),
            pltpu.VMEM((8, 128), I32),
            pltpu.SMEM((8, 128), I32),
            pltpu.SemaphoreType.DMA((3,)),
            pltpu.SemaphoreType.DMA((2,)),
            pltpu.SemaphoreType.DMA((2,)),
            pltpu.SemaphoreType.DMA((6,)),
            pltpu.SemaphoreType.DMA((3,)),
            pltpu.SemaphoreType.DMA((2,)),
            pltpu.SemaphoreType.DMA((2, 2)),
            pltpu.SemaphoreType.DMA((2, 2)),
        ],
        compiler_params=pltpu.CompilerParams(
            collective_id=0, has_side_effects=True, vmem_limit_bytes=24 << 20
        ),
        name="combine",
    )(
        in_hbm(levels), in_hbm(velocity), grid_signs, in_hbm(owner_list), in_hbm(slot_list),
        tiled(concentration), tiled(diffusion),
    )
    return combined[:1024].reshape(2, COLS, 8, 128).transpose(0, 2, 1, 3).reshape(1, 16, COLS * 128)


def solution(mesh):
    return jax.shard_map(
        body,
        mesh=mesh,
        in_specs=(
            P("grid", "dom", None),
            P("grid", "dom", None),
            P(),
            P("grid", None),
            P("grid"),
            P(("grid", "dom"), None),
            P(("grid", "dom"), None),
        ),
        out_specs=P("grid", "dom", None),
        check_vma=False,
    )
```

```python
import jax
import jax.numpy as jnp
from jax import lax
from jax.experimental import pallas as pl
from jax.experimental.pallas import tpu as pltpu
from jax.sharding import PartitionSpec as P

MESH = pl.DeviceIdType.MESH
F32 = jnp.float32
BF16 = jnp.bfloat16
I32 = jnp.int32

COLS = 64
PAD = 8
TILE_HALO = PAD + 2 * COLS


def tile(at):
    return pl.ds(at * 8, 8)


def node_rows(base, node):
    return pl.ds(base + (node // 8) * COLS * 8 + node % 8, COLS, stride=8)


def dot_split(left, right):
    first = left.astype(BF16)
    second = (left - first.astype(F32)).astype(BF16)
    total = jnp.dot(second, right, preferred_element_type=F32)
    return total + jnp.dot(first, right, preferred_element_type=F32)


def lane_matrices(l1, l2, sign):
    source = lax.broadcasted_iota(I32, (128, 128), 0)
    target = lax.broadcasted_iota(I32, (128, 128), 1)
    both = l1 + l2
    low = [0, l1, both]
    top = [jnp.minimum(l1, 7), jnp.minimum(both, 7), 7]
    here = jnp.full((128, 128), sign, F32)
    after = jnp.full((128, 128), sign, F32)
    for field in range(3):
        width = jnp.maximum(top[field] - jnp.minimum(low[field], 7), 0)
        mask = jnp.left_shift(1, width) - 1
        shift = jnp.minimum(low[field], 7)
        fro = jnp.right_shift(source, shift) & mask
        to = jnp.right_shift(target, shift) & mask
        bit = to & (-to)
        same = jnp.where(fro == to, 1.0, 0.0)
        near = jnp.where((to != 0) & ((fro == to - bit) | (fro == to + bit)), -0.5, 0.0)
        plain = same + near
        wraps = (to != 0) & (to + bit == mask + 1) & (fro == 0)
        carry = jnp.where(wraps, -0.5, 0.0)
        here = here * plain
        if field == 0:
            after = after * plain
        elif field == 1:
            after = after * jnp.where(both > 6, jnp.where(width > 0, carry, 0.0), plain)
        else:
            after = after * jnp.where(both > 6, 1.0, carry)
    return here, after


def peer_offsets():
    offsets = [(k // 32, k // 8 % 4, k // 2 % 4, k % 2) for k in range(1, 128)]
    return sorted(offsets, key=lambda o: -sum(min(v, 4 - v) for v in o[:3]))


def unrolled(count, factor, step):
    def some(i, carry):
        for k in range(factor):
            step(i * factor + k)
        return carry

    lax.fori_loop(0, count // factor, some, 0)


def combine_kernel(
    lev_ref, vel_ref, sign_ref, own_ref, slot_ref, u_hbm, k_hbm, out_ref,
    start, mid, coef, stepped, lanes_done, rows_done, surplus, packs, low_in, high_in, lead, lead_in,
    sums, diffs, forth, back2, turned3,
    out_a, out_b, in_a, in_b, ret_a, ret_b, back_a, back_b, slots_out, slots_in, index_v, index_s,
    load_sem, send_sem, recv_sem, lead_send, lead_recv, slot_sems, out_sems, back_sems,
):
    g = lax.axis_index("grid")
    d = lax.axis_index("dom")
    me = g * 8 + d
    x_at, y_at = g // 4, g % 4
    z_at, core = d // 2, d % 2
    grids = [((x_at + i) % 4) * 4 + (y_at + j) % 4 for i in range(4) for j in range(4)]
    doms = [((z_at + i) % 4) * 2 + (core + j) % 2 for i in range(4) for j in range(2)]
    barrier = pltpu.get_barrier_semaphore()

    load_u = pltpu.make_async_copy(u_hbm, start.at[pl.ds(PAD * 8, 1024)], load_sem.at[0])
    load_k = pltpu.make_async_copy(k_hbm, coef.at[pl.ds(0, 1024)], load_sem.at[1])
    load_u.start()
    load_k.start()

    def peer(offset):
        return grids[offset[0] * 4 + offset[1]], doms[offset[2] * 2 + offset[3]]

    offsets = peer_offsets()
    for offset in offsets:
        pl.semaphore_signal(barrier, inc=1, device_id=peer(offset), device_id_type=MESH)

    owners = own_ref[...]
    own_row = jnp.broadcast_to(owners, (128, 128))
    own_col = own_row.T
    row = lax.broadcasted_iota(I32, (128, 128), 0)
    col = lax.broadcasted_iota(I32, (128, 128), 1)
    earlier = jnp.where((own_row == own_col) & (row < col), 1, 0)
    rank = jnp.sum(earlier, axis=0, keepdims=True)
    rank_row = jnp.broadcast_to(rank, (128, 128))
    rank_col = rank_row.T
    slot_row = jnp.broadcast_to(slot_ref[...], (128, 128))
    table = jnp.full((128, 128), -1, I32)
    index_v[...] = jnp.zeros((8, 128), I32)
    second_one = jnp.minimum(rank, 1)
    index_v[0:1] = 8 * owners + 4 * second_one
    index_v[3:4] = 8 * owners + 4 * (1 - second_one)
    first_row = (row // 64) * (8 * COLS) + (row % 8) * 64 + (row // 8) % 8
    for r in range(2):
        to_owner = (own_col == col) & (rank_col == r)
        index_v[1 + r : 2 + r] = jnp.sum(
            jnp.where(to_owner, first_row, 0), axis=0, keepdims=True
        )
        of_block = (own_row == row) & (rank_row == r)
        ids = jnp.sum(jnp.where(of_block, slot_row + 1, 0), axis=1, keepdims=True) - 1
        table = jnp.where(col == r, ids, table)
    slots_out[:, 0, :] = table
    fetch = pltpu.make_async_copy(index_v, index_s, load_sem.at[2])
    fetch.start()

    lanes_done[1024:1032] = jnp.zeros((8, 128), F32)
    rows_done[1024:1032] = jnp.zeros((8, 128), F32)
    halo = TILE_HALO * 8

    def halo_rows(s):
        return pl.ds(halo + s, COLS, stride=8)

    def halo_coef(s):
        return pl.ds(1024 + s, COLS, stride=8)

    base = PAD * 8
    load_u.wait()
    load_k.wait()
    packs[0, 0:64] = start[node_rows(base, 0), :]
    packs[0, 64:128] = start[node_rows(base, 1), :]
    packs[0, 128:192] = coef[node_rows(0, 0), :]
    packs[1, 0:64] = start[node_rows(base, 14), :]
    packs[1, 64:128] = start[node_rows(base, 15), :]
    packs[1, 128:192] = coef[node_rows(0, 15), :]
    start[halo_rows(2), :] = packs[0, 0:64]
    start[halo_rows(3), :] = packs[0, 64:128]
    start[halo_rows(4), :] = packs[1, 0:64]
    start[halo_rows(5), :] = packs[1, 64:128]
    coef[halo_coef(2), :] = packs[0, 128:192]
    coef[halo_coef(5), :] = packs[1, 128:192]

    l1 = lev_ref[0, 0]
    l2 = lev_ref[0, 1]
    l3 = lev_ref[0, 2]
    both = l1 + l2
    lane = lax.broadcasted_iota(I32, (8, 128), 1)
    sub = lax.broadcasted_iota(I32, (8, 128), 0)
    span2 = jnp.left_shift(1, l1)
    span3 = jnp.minimum(jnp.left_shift(1, both), 128)
    skip3 = jnp.where(both == 8, 2, jnp.where(both == 9, 4, jnp.where(both == 10, 8, 1)))
    last1 = jnp.left_shift(1, l1) - 1
    last2 = jnp.left_shift(1, l2) - 1
    last3 = jnp.left_shift(1, l3) - 1
    drift1 = 0.1 * vel_ref[0]
    drift2 = 0.1 * vel_ref[1]
    drift3 = 0.1 * vel_ref[2]
    drift4 = 0.1 * vel_ref[3]
    stays2 = lane < 128 - span2
    comes2 = lane >= span2
    stays3 = lane < 128 - span3
    comes3 = lane >= span3

    source = lax.broadcasted_iota(I32, (128, 128), 0)
    target = lax.broadcasted_iota(I32, (128, 128), 1)
    at1 = target & last1
    from_up = jnp.where((source == target + 1) & (at1 != last1), 1.0, 0.0)
    from_down = jnp.where((source == target - 1) & (at1 != 0), 1.0, 0.0)
    turn2 = span2 & 127
    turn3 = span3 & 127
    forms = [
        from_up + from_down,
        from_up - from_down,
        jnp.where(source == ((target + turn2) & 127), 1.0, 0.0),
        jnp.where(source == ((target - turn2) & 127), 1.0, 0.0),
        jnp.where(source == ((target + turn3) & 127), 1.0, 0.0),
    ]
    forms = jnp.concatenate([jnp.concatenate([form, form], axis=0).astype(BF16) for form in forms], axis=1)
    shift_chunk = 128

    def shift_lanes(ref, at):
        x = ref[at : at + shift_chunk, :]
        high = x.astype(BF16)
        low = (x - high.astype(F32)).astype(BF16)
        shifted = jnp.dot(
            jnp.concatenate([high, low], axis=1), forms, preferred_element_type=F32
        )
        for form, scratch in enumerate((sums, diffs, forth, back2, turned3)):
            scratch[at : at + shift_chunk, :] = shifted[:, form * 128 : (form + 1) * 128]

    def masks(c):
        cell = c * 128 + lane
        i2 = jnp.right_shift(cell, l1) & last2
        i3 = jnp.right_shift(cell, both) & last3
        return (i2 != last2, i2 != 0, i3 != last3, i3 != 0)

    def advance(at, x, ahead4, behind4, diff, ok):
        here = tile(at)
        p2 = jnp.where(stays2, forth[here, :], forth[tile(at + 1), :])
        p2 = jnp.where(ok[0], p2, 0.0)
        m2 = jnp.where(comes2, back2[here, :], back2[tile(at - 1), :])
        m2 = jnp.where(ok[1], m2, 0.0)
        half = turned3[here, :]
        p3 = jnp.where(stays3, half, turned3[tile(at + skip3), :])
        p3 = jnp.where(ok[2], p3, 0.0)
        m3 = jnp.where(comes3, half, turned3[tile(at - skip3), :])
        m3 = jnp.where(ok[3], m3, 0.0)
        second = (sums[here, :] + (p2 + m2)) + ((p3 + m3) + (ahead4 + behind4)) - 8.0 * x
        drift = (drift1 * diffs[here, :] + drift2 * (p2 - m2)) + (
            drift3 * (p3 - m3) + drift4 * (ahead4 - behind4)
        )
        return x + 0.1 * diff * second - drift

    def both_groups(ref, c, target, offset, with_halo):
        ok = masks(c)
        x0 = ref[tile(PAD + c), :]
        x1 = ref[tile(PAD + COLS + c), :]
        down0, up1 = x0, x1
        if with_halo:
            xh = ref[tile(TILE_HALO + c), :]
            down0 = jnp.where(sub == 7, pltpu.roll(xh, 6, 0), x0)
            up1 = jnp.where(sub == 0, pltpu.roll(xh, 2, 0), x1)
        value0 = advance(
            PAD + c, x0, pltpu.roll(jnp.where(sub == 0, x1, x0), 7, 0),
            pltpu.roll(down0, 1, 0), coef[tile(c), :], ok,
        )
        value1 = advance(
            PAD + COLS + c, x1, pltpu.roll(up1, 7, 0),
            pltpu.roll(jnp.where(sub == 7, x0, x1), 1, 0), coef[tile(COLS + c), :], ok,
        )
        target[tile(offset + c), :] = value0
        target[tile(offset + COLS + c), :] = value1

    for i in range(1024 // shift_chunk):
        shift_lanes(start, PAD * 8 + i * shift_chunk)
    unrolled(COLS, 2, lambda c: both_groups(start, c, mid, PAD, False))

    pl.semaphore_wait(barrier, 127)

    def down():
        return pltpu.make_async_remote_copy(
            src_ref=packs.at[0], dst_ref=high_in, send_sem=send_sem.at[0], recv_sem=recv_sem.at[0],
            device_id=(g, lax.rem(d + 7, 8)), device_id_type=MESH,
        )

    def upward():
        return pltpu.make_async_remote_copy(
            src_ref=packs.at[1], dst_ref=low_in, send_sem=send_sem.at[1], recv_sem=recv_sem.at[1],
            device_id=(g, lax.rem(d + 1, 8)), device_id_type=MESH,
        )

    @pl.when(d > 0)
    def _():
        down().start()

    @pl.when(d < 7)
    def _():
        upward().start()

    def send_all(sources, targets, sems, size):
        for offset in offsets:
            pg, pd = peer(offset)
            pltpu.make_async_remote_copy(
                src_ref=sources.at[pl.ds((pg * 8 + pd) * size, size)],
                dst_ref=targets.at[pl.ds(me * size, size)],
                send_sem=sems.at[0], recv_sem=sems.at[1],
                device_id=(pg, pd), device_id_type=MESH,
            ).start()
        targets[pl.ds(me * size, size)] = sources[pl.ds(me * size, size)]

    def all_of(sources, targets, sems, size):
        return pltpu.make_async_remote_copy(
            src_ref=sources.at[pl.ds(0, 127 * size)], dst_ref=targets.at[pl.ds(0, 127 * size)],
            send_sem=sems.at[0], recv_sem=sems.at[1],
            device_id=(g, lax.rem(d + 1, 8)), device_id_type=MESH,
        )

    send_all(slots_out, slots_in, slot_sems, 1)
    fetch.wait()

    zero_rows = jnp.zeros((192, 128), F32)

    @pl.when(d == 0)
    def _():
        low_in[...] = zero_rows

    @pl.when(d == 7)
    def _():
        high_in[...] = zero_rows

    here, after = lane_matrices(l1, l2, sign_ref[0].astype(F32))
    here = here.astype(BF16)
    after = after.astype(BF16)

    @pl.when(d < 7)
    def _():
        down().wait_recv()

    @pl.when(d > 0)
    def _():
        upward().wait_recv()

    start[halo_rows(0), :] = low_in[0:64]
    start[halo_rows(1), :] = low_in[64:128]
    start[halo_rows(6), :] = high_in[0:64]
    start[halo_rows(7), :] = high_in[64:128]
    coef[halo_coef(1), :] = low_in[128:192]
    coef[halo_coef(6), :] = high_in[128:192]
    outside = jnp.where(d == 0, 1, jnp.where(d == 7, 6, -1))

    def first_halo(c):
        xh = start[tile(TILE_HALO + c), :]
        value = advance(
            TILE_HALO + c, xh, pltpu.roll(xh, 7, 0), pltpu.roll(xh, 1, 0),
            coef[tile(2 * COLS + c), :], masks(c),
        )
        mid[tile(TILE_HALO + c), :] = jnp.where(sub == outside, 0.0, value)

    for i in range(512 // shift_chunk):
        shift_lanes(start, halo + i * shift_chunk)
    unrolled(COLS, 4, first_halo)
    mid[node_rows(base, 0), :] = mid[halo_rows(2), :]
    mid[node_rows(base, 15), :] = mid[halo_rows(5), :]
    for i in range(1024 // shift_chunk):
        shift_lanes(mid, PAD * 8 + i * shift_chunk)
    unrolled(COLS, 2, lambda c: both_groups(mid, c, stepped, 0, True))

    straddles = jnp.where(both > 7, jnp.where(l1 < 7, 1, 0), jnp.where(both == 6, 1, 0))
    mask_a = jnp.where(both > 7, skip3 - 1, COLS - 1)
    no_next = jnp.where(straddles == 1, mask_a, 0)
    limit_a = jnp.where(both > 7, span2, span3)
    mask_b = jnp.where(both > 7, COLS - skip3, 0)
    inside = lane < limit_a
    chunk = 128

    def lane_part(i):
        at = i * chunk
        x = stepped[pl.ds(at, chunk), :]
        beyond = stepped[pl.ds(at + 8, chunk), :]
        column = jnp.right_shift(at + lax.broadcasted_iota(I32, (chunk, 128), 0), 3)
        beyond = jnp.where((column & no_next) != no_next, beyond, 0.0)
        lanes_done[pl.ds(at, chunk), :] = dot_split(x, here) + dot_split(beyond, after)

    nothing = 2 * COLS

    def columns(source, target, mask, chosen):
        def step(c):
            j = c & mask
            off = j & (-j)
            has_up = (j != 0) & (j + off <= mask)
            for t in range(2):
                lower = jnp.where(j != 0, t * COLS + c - off, nothing)
                upper = jnp.where(has_up, t * COLS + c + off, nothing)
                update = 0.5 * (source[tile(lower), :] + source[tile(upper), :])
                if chosen is not None:
                    update = jnp.where(chosen, update, 0.0)
                target[tile(t * COLS + c), :] = source[tile(t * COLS + c), :] - update

        unrolled(COLS, 4, step)

    def lead_copy(slot, target, sent):
        return pltpu.make_async_remote_copy(
            src_ref=lead, dst_ref=lead_in.at[slot], send_sem=lead_send.at[sent],
            recv_sem=lead_recv.at[slot], device_id=(g, target), device_id_type=MESH,
        )

    routes = [(0, d > 0, lax.rem(d + 7, 8)), (1, lax.rem(d, 2) == 0, lax.rem(d + 1, 8))]
    routes += [(1, d == 0, 2), (1, d == 0, 4), (1, d == 4, 6), (2, d == 4, 2)]
    for i in range(1024 // chunk):
        lane_part(i)
    columns(lanes_done, rows_done, mask_a, inside)
    columns(rows_done, lanes_done, mask_b, None)
    lead[...] = lanes_done[node_rows(0, 0), :]
    for sent, (slot, condition, target) in enumerate(routes):

        @pl.when(condition)
        def _():
            lead_copy(slot, target, sent).start()

    odd = (sub & 1) == 1
    two = (sub & 3) == 2
    four = sub == 4

    def fourth(c):
        x0 = lanes_done[tile(c), :]
        x1 = lanes_done[tile(COLS + c), :]
        for t, x, y, special in ((0, x0, jnp.where(sub == 0, x1, x0), 0.0), (1, x1, jnp.where(sub == 0, 0.0, x1), x0)):
            near1 = pltpu.roll(y, 7, 0) + pltpu.roll(x, 1, 0)
            near2 = pltpu.roll(y, 6, 0) + pltpu.roll(x, 2, 0)
            near4 = pltpu.roll(y, 4, 0) + pltpu.roll(x, 4, 0)
            near = jnp.where(odd, near1, jnp.where(two, near2, jnp.where(four, near4, special)))
            surplus[tile(t * COLS + c), :] = x - 0.5 * near

    unrolled(COLS, 2, fourth)

    all_of(slots_out, slots_in, slot_sems, 1).wait_recv()
    ids_col = slots_in[:, 0, :]
    ids_row = ids_col.T
    equal = []
    for r in range(2):
        of_r = jnp.broadcast_to(ids_col[:, r : r + 1], (128, 128))
        parts = [
            jnp.where(of_r == jnp.broadcast_to(ids_row[s : s + 1, :], (128, 128)), 1.0, 0.0)
            for s in range(2)
        ]
        equal.append(jnp.concatenate(parts, axis=1))
    equal = jnp.concatenate(equal, axis=0).astype(BF16)

    zero_lead = jnp.zeros((64, 128), F32)

    @pl.when(d == 7)
    def _():
        lead_in[0] = zero_lead

    @pl.when(d == 0)
    def _():
        lead_in[1] = zero_lead

    @pl.when(d != 2)
    def _():
        lead_in[2] = zero_lead

    @pl.when(d < 7)
    def _():
        lead_copy(0, lax.rem(d + 7, 8), 0).wait_recv()

    @pl.when(d > 0)
    def _():
        lead_copy(1, lax.rem(d + 1, 8), 0).wait_recv()

    @pl.when(d == 2)
    def _():
        lead_copy(2, lax.rem(d + 1, 8), 0).wait_recv()

    following = 0.5 * lead_in[0]
    use_next = jnp.where(lax.rem(d, 2) == 1, 1.0, 0.0)
    around = 0.5 * (lead_in[1] + lead_in[2]) + use_next * following
    surplus[node_rows(0, 0), :] = surplus[node_rows(0, 0), :] - around
    for node in (8, 12, 14, 15):
        surplus[node_rows(0, node), :] = surplus[node_rows(0, node), :] - following

    for o in range(128):
        of_rank = [surplus[pl.ds(index_s[1 + r, o], 8, stride=8), :] for r in range(2)]
        turned = pltpu.roll(of_rank[1], 4, 0)
        out_a[o * 8 : o * 8 + 8, :] = jnp.where(sub < 4, of_rank[0], turned)
        out_b[o * 8 : o * 8 + 8, :] = jnp.where(sub < 4, turned, of_rank[0])

    halves = ((out_a, in_a, ret_a, back_a), (out_b, in_b, ret_b, back_b))
    for half, (outgoing, arrived, _, _) in enumerate(halves):
        send_all(outgoing, arrived, out_sems.at[half], 8)

    for half, (outgoing, arrived, returned, back) in enumerate(halves):
        all_of(outgoing, arrived, out_sems.at[half], 8).wait_recv()
        for j in range(4):
            block = jnp.concatenate(
                [arrived[pl.ds((r ^ half) * 4 + j, 128, stride=8), :] for r in range(2)], axis=0
            )
            first = block.astype(BF16)
            second = (block - first.astype(F32)).astype(BF16)
            total = jnp.dot(equal, second, preferred_element_type=F32)
            total = total + jnp.dot(equal, first, preferred_element_type=F32)
            for r in range(2):
                returned[pl.ds((r ^ half) * 4 + j, 128, stride=8), :] = total[
                    r * 128 : (r + 1) * 128
                ]
        send_all(returned, back, back_sems.at[half], 8)

    for half, (_, _, returned, back) in enumerate(halves):
        all_of(returned, back, back_sems.at[half], 8).wait_recv()

        for block in range(128):
            at = (block // 64) * (8 * COLS) + (block % 8) * 64 + (block // 8) % 8 + half * 32
            out_ref[pl.ds(at, 4, stride=8), :] = back[pl.ds(index_s[3 * half, block], 4), :]

    @pl.when(d > 0)
    def _():
        down().wait_send()

    @pl.when(d < 7)
    def _():
        upward().wait_send()

    for sent, (slot, condition, target) in enumerate(routes):

        @pl.when(condition)
        def _():
            lead_copy(slot, target, sent).wait_send()

    all_of(slots_out, slots_in, slot_sems, 1).wait_send()
    for half, (outgoing, arrived, returned, back) in enumerate(halves):
        all_of(outgoing, arrived, out_sems.at[half], 8).wait_send()
        all_of(returned, back, back_sems.at[half], 8).wait_send()


def body(concentration, diffusion, velocity, levels, grid_signs, owner_list, slot_list):
    def in_hbm(array):
        return pltpu.with_memory_space_constraint(array, pltpu.HBM)

    def tiled(block):
        rows = block.reshape(2, 8, COLS, 128).transpose(0, 2, 1, 3).reshape(1024, 128)
        return in_hbm(rows)

    smem = pl.BlockSpec(memory_space=pltpu.SMEM)
    vmem = pl.BlockSpec(memory_space=pltpu.VMEM)
    anywhere = pl.BlockSpec(memory_space=pltpu.HBM)
    total_rows = (TILE_HALO + COLS + PAD) * 8
    rows = [total_rows, total_rows, 1552, 1032, 1032, 1032, 1032]
    combined = pl.pallas_call(
        combine_kernel,
        out_shape=jax.ShapeDtypeStruct((1032, 128), F32),
        in_specs=[smem, smem, smem, vmem, vmem, anywhere, anywhere],
        out_specs=vmem,
        scratch_shapes=[pltpu.VMEM((n, 128), F32) for n in rows]
        + [
            pltpu.VMEM((2, 192, 128), F32),
            pltpu.VMEM((192, 128), F32),
            pltpu.VMEM((192, 128), F32),
            pltpu.VMEM((64, 128), F32),
            pltpu.VMEM((3, 64, 128), F32),
        ]
        + [pltpu.VMEM((total_rows, 128), F32) for _ in range(5)]
        + [pltpu.VMEM((1032, 128), F32) for _ in range(8)]
        + [
            pltpu.VMEM((128, 1, 128), I32),
            pltpu.VMEM((128, 1, 128), I32),
            pltpu.VMEM((8, 128), I32),
            pltpu.SMEM((8, 128), I32),
            pltpu.SemaphoreType.DMA((3,)),
            pltpu.SemaphoreType.DMA((2,)),
            pltpu.SemaphoreType.DMA((2,)),
            pltpu.SemaphoreType.DMA((6,)),
            pltpu.SemaphoreType.DMA((3,)),
            pltpu.SemaphoreType.DMA((2,)),
            pltpu.SemaphoreType.DMA((2, 2)),
            pltpu.SemaphoreType.DMA((2, 2)),
        ],
        compiler_params=pltpu.CompilerParams(
            collective_id=0, has_side_effects=True, vmem_limit_bytes=24 << 20
        ),
        name="combine",
    )(
        in_hbm(levels), in_hbm(velocity), grid_signs, in_hbm(owner_list), in_hbm(slot_list),
        tiled(concentration), tiled(diffusion),
    )
    return combined[:1024].reshape(2, COLS, 8, 128).transpose(0, 2, 1, 3).reshape(1, 16, COLS * 128)


def solution(mesh):
    return jax.shard_map(
        body,
        mesh=mesh,
        in_specs=(
            P("grid", "dom", None),
            P("grid", "dom", None),
            P(),
            P("grid", None),
            P("grid"),
            P(("grid", "dom"), None),
            P(("grid", "dom"), None),
        ),
        out_specs=P("grid", "dom", None),
        check_vma=False,
    )
```

```python
import jax
import jax.numpy as jnp
from jax import lax
from jax.experimental import pallas as pl
from jax.experimental.pallas import tpu as pltpu
from jax.sharding import PartitionSpec as P

MESH = pl.DeviceIdType.MESH
F32 = jnp.float32
BF16 = jnp.bfloat16
I32 = jnp.int32

COLS = 64
PAD = 8
EDGE_COEF = 194
EDGE = 129
TILE_HALO = PAD + 2 * COLS


def tile(at):
    return pl.ds(at * 8, 8)


def node_rows(base, node):
    return pl.ds(base + (node // 8) * COLS * 8 + node % 8, COLS, stride=8)


def dot_split(left, right):
    first = left.astype(BF16)
    second = (left - first.astype(F32)).astype(BF16)
    total = jnp.dot(second, right, preferred_element_type=F32)
    return total + jnp.dot(first, right, preferred_element_type=F32)


def lane_matrices(l1, l2, sign):
    source = lax.broadcasted_iota(I32, (128, 128), 0)
    target = lax.broadcasted_iota(I32, (128, 128), 1)
    both = l1 + l2
    low = [0, l1, both]
    top = [jnp.minimum(l1, 7), jnp.minimum(both, 7), 7]
    here = jnp.full((128, 128), sign, F32)
    after = jnp.full((128, 128), sign, F32)
    for field in range(3):
        width = jnp.maximum(top[field] - jnp.minimum(low[field], 7), 0)
        mask = jnp.left_shift(1, width) - 1
        shift = jnp.minimum(low[field], 7)
        fro = jnp.right_shift(source, shift) & mask
        to = jnp.right_shift(target, shift) & mask
        bit = to & (-to)
        same = jnp.where(fro == to, 1.0, 0.0)
        near = jnp.where((to != 0) & ((fro == to - bit) | (fro == to + bit)), -0.5, 0.0)
        plain = same + near
        wraps = (to != 0) & (to + bit == mask + 1) & (fro == 0)
        carry = jnp.where(wraps, -0.5, 0.0)
        here = here * plain
        if field == 0:
            after = after * plain
        elif field == 1:
            after = after * jnp.where(both > 6, jnp.where(width > 0, carry, 0.0), plain)
        else:
            after = after * jnp.where(both > 6, 1.0, carry)
    return here, after


def peer_offsets():
    offsets = [(k // 32, k // 8 % 4, k // 2 % 4, k % 2) for k in range(1, 128)]
    return sorted(offsets, key=lambda o: -sum(min(v, 4 - v) for v in o[:3]))


def unrolled(count, factor, step):
    def some(i, carry):
        for k in range(factor):
            step(i * factor + k)
        return carry

    lax.fori_loop(0, count // factor, some, 0)


def combine_kernel(
    lev_ref, vel_ref, sign_ref, own_ref, slot_ref, u_hbm, k_hbm, out_ref,
    start, mid, coef, stepped, lanes_done, rows_done, surplus, packs, low_in, high_in, lead, lead_in,
    sums, diffs, forth, back2, turned3,
    out_a, out_b, in_a, in_b, ret_a, ret_b, back_a, back_b, slots_out, slots_in, index_v, index_s,
    load_sem, send_sem, recv_sem, lead_send, lead_recv, slot_sems, out_sems, back_sems,
):
    g = lax.axis_index("grid")
    d = lax.axis_index("dom")
    me = g * 8 + d
    x_at, y_at = g // 4, g % 4
    z_at, core = d // 2, d % 2
    grids = [((x_at + i) % 4) * 4 + (y_at + j) % 4 for i in range(4) for j in range(4)]
    doms = [((z_at + i) % 4) * 2 + (core + j) % 2 for i in range(4) for j in range(2)]
    barrier = pltpu.get_barrier_semaphore()

    load_u = pltpu.make_async_copy(u_hbm, start.at[pl.ds(PAD * 8, 1024)], load_sem.at[0])
    load_k = pltpu.make_async_copy(k_hbm, coef.at[pl.ds(0, 1024)], load_sem.at[1])
    load_u.start()
    load_k.start()

    def peer(offset):
        return grids[offset[0] * 4 + offset[1]], doms[offset[2] * 2 + offset[3]]

    offsets = peer_offsets()
    for offset in offsets:
        pl.semaphore_signal(barrier, inc=1, device_id=peer(offset), device_id_type=MESH)

    owners = own_ref[...]
    own_row = jnp.broadcast_to(owners, (128, 128))
    own_col = own_row.T
    row = lax.broadcasted_iota(I32, (128, 128), 0)
    col = lax.broadcasted_iota(I32, (128, 128), 1)
    earlier = jnp.where((own_row == own_col) & (row < col), 1, 0)
    rank = jnp.sum(earlier, axis=0, keepdims=True)
    rank_row = jnp.broadcast_to(rank, (128, 128))
    rank_col = rank_row.T
    slot_row = jnp.broadcast_to(slot_ref[...], (128, 128))
    table = jnp.full((128, 128), -1, I32)
    index_v[...] = jnp.zeros((8, 128), I32)
    second_one = jnp.minimum(rank, 1)
    index_v[0:1] = 8 * owners + 4 * second_one
    index_v[3:4] = 8 * owners + 4 * (1 - second_one)
    first_row = (row // 64) * (8 * COLS) + (row % 8) * 64 + (row // 8) % 8
    for r in range(2):
        to_owner = (own_col == col) & (rank_col == r)
        index_v[1 + r : 2 + r] = jnp.sum(
            jnp.where(to_owner, first_row, 0), axis=0, keepdims=True
        )
        of_block = (own_row == row) & (rank_row == r)
        ids = jnp.sum(jnp.where(of_block, slot_row + 1, 0), axis=1, keepdims=True) - 1
        table = jnp.where(col == r, ids, table)
    slots_out[:, 0, :] = table
    fetch = pltpu.make_async_copy(index_v, index_s, load_sem.at[2])
    fetch.start()

    lanes_done[1024:1032] = jnp.zeros((8, 128), F32)
    rows_done[1024:1032] = jnp.zeros((8, 128), F32)
    halo = TILE_HALO * 8

    def halo_rows(s):
        return pl.ds(halo + s, COLS, stride=8)

    def halo_coef(s):
        return pl.ds(1024 + s, COLS, stride=8)

    base = PAD * 8
    load_u.wait()
    load_k.wait()
    packs[0, 0:64] = start[node_rows(base, 0), :]
    packs[0, 64:128] = start[node_rows(base, 1), :]
    packs[0, 128:192] = coef[node_rows(0, 0), :]
    packs[1, 0:64] = start[node_rows(base, 14), :]
    packs[1, 64:128] = start[node_rows(base, 15), :]
    packs[1, 128:192] = coef[node_rows(0, 15), :]
    start[halo_rows(2), :] = packs[0, 0:64]
    start[halo_rows(3), :] = packs[0, 64:128]
    start[halo_rows(4), :] = packs[1, 0:64]
    start[halo_rows(5), :] = packs[1, 64:128]
    coef[halo_coef(2), :] = packs[0, 128:192]
    coef[halo_coef(5), :] = packs[1, 128:192]
    for s, node in ((1, 0), (2, 1), (5, 14), (6, 15)):
        coef[pl.ds(EDGE_COEF * 8 + s, COLS, stride=8), :] = coef[node_rows(0, node), :]

    l1 = lev_ref[0, 0]
    l2 = lev_ref[0, 1]
    l3 = lev_ref[0, 2]
    both = l1 + l2
    lane = lax.broadcasted_iota(I32, (8, 128), 1)
    sub = lax.broadcasted_iota(I32, (8, 128), 0)
    span2 = jnp.left_shift(1, l1)
    span3 = jnp.minimum(jnp.left_shift(1, both), 128)
    skip3 = jnp.where(both == 8, 2, jnp.where(both == 9, 4, jnp.where(both == 10, 8, 1)))
    last1 = jnp.left_shift(1, l1) - 1
    last2 = jnp.left_shift(1, l2) - 1
    last3 = jnp.left_shift(1, l3) - 1
    drift1 = 0.1 * vel_ref[0]
    drift2 = 0.1 * vel_ref[1]
    drift3 = 0.1 * vel_ref[2]
    drift4 = 0.1 * vel_ref[3]
    stays2 = lane < 128 - span2
    comes2 = lane >= span2
    stays3 = lane < 128 - span3
    comes3 = lane >= span3

    source = lax.broadcasted_iota(I32, (128, 128), 0)
    target = lax.broadcasted_iota(I32, (128, 128), 1)
    at1 = target & last1
    from_up = jnp.where((source == target + 1) & (at1 != last1), 1.0, 0.0)
    from_down = jnp.where((source == target - 1) & (at1 != 0), 1.0, 0.0)
    turn2 = span2 & 127
    turn3 = span3 & 127
    forms = [
        from_up + from_down,
        from_up - from_down,
        jnp.where(source == ((target + turn2) & 127), 1.0, 0.0),
        jnp.where(source == ((target - turn2) & 127), 1.0, 0.0),
        jnp.where(source == ((target + turn3) & 127), 1.0, 0.0),
    ]
    forms = jnp.concatenate([jnp.concatenate([form, form], axis=0).astype(BF16) for form in forms], axis=1)
    shift_chunk = 128

    def shift_lanes(ref, at):
        x = ref[at : at + shift_chunk, :]
        high = x.astype(BF16)
        low = (x - high.astype(F32)).astype(BF16)
        shifted = jnp.dot(
            jnp.concatenate([high, low], axis=1), forms, preferred_element_type=F32
        )
        for form, scratch in enumerate((sums, diffs, forth, back2, turned3)):
            scratch[at : at + shift_chunk, :] = shifted[:, form * 128 : (form + 1) * 128]

    def masks(c):
        cell = c * 128 + lane
        i2 = jnp.right_shift(cell, l1) & last2
        i3 = jnp.right_shift(cell, both) & last3
        return (i2 != last2, i2 != 0, i3 != last3, i3 != 0)

    def advance(at, x, ahead4, behind4, diff, ok):
        here = tile(at)
        p2 = jnp.where(stays2, forth[here, :], forth[tile(at + 1), :])
        p2 = jnp.where(ok[0], p2, 0.0)
        m2 = jnp.where(comes2, back2[here, :], back2[tile(at - 1), :])
        m2 = jnp.where(ok[1], m2, 0.0)
        half = turned3[here, :]
        p3 = jnp.where(stays3, half, turned3[tile(at + skip3), :])
        p3 = jnp.where(ok[2], p3, 0.0)
        m3 = jnp.where(comes3, half, turned3[tile(at - skip3), :])
        m3 = jnp.where(ok[3], m3, 0.0)
        second = (sums[here, :] + (p2 + m2)) + ((p3 + m3) + (ahead4 + behind4)) - 8.0 * x
        drift = (drift1 * diffs[here, :] + drift2 * (p2 - m2)) + (
            drift3 * (p3 - m3) + drift4 * (ahead4 - behind4)
        )
        return x + 0.1 * diff * second - drift

    def both_groups(ref, c, target, offset):
        ok = masks(c)
        x0 = ref[tile(PAD + c), :]
        x1 = ref[tile(PAD + COLS + c), :]
        value0 = advance(
            PAD + c, x0, pltpu.roll(jnp.where(sub == 0, x1, x0), 7, 0),
            pltpu.roll(x0, 1, 0), coef[tile(c), :], ok,
        )
        value1 = advance(
            PAD + COLS + c, x1, pltpu.roll(x1, 7, 0),
            pltpu.roll(jnp.where(sub == 7, x0, x1), 1, 0), coef[tile(COLS + c), :], ok,
        )
        target[tile(offset + c), :] = value0
        target[tile(offset + COLS + c), :] = value1

    for i in range(1024 // shift_chunk):
        shift_lanes(start, PAD * 8 + i * shift_chunk)
    unrolled(COLS, 2, lambda c: both_groups(start, c, mid, PAD))
    for i in range(1024 // shift_chunk):
        shift_lanes(mid, PAD * 8 + i * shift_chunk)
    unrolled(COLS, 2, lambda c: both_groups(mid, c, stepped, 0))

    pl.semaphore_wait(barrier, 127)

    def down():
        return pltpu.make_async_remote_copy(
            src_ref=packs.at[0], dst_ref=high_in, send_sem=send_sem.at[0], recv_sem=recv_sem.at[0],
            device_id=(g, lax.rem(d + 7, 8)), device_id_type=MESH,
        )

    def upward():
        return pltpu.make_async_remote_copy(
            src_ref=packs.at[1], dst_ref=low_in, send_sem=send_sem.at[1], recv_sem=recv_sem.at[1],
            device_id=(g, lax.rem(d + 1, 8)), device_id_type=MESH,
        )

    @pl.when(d > 0)
    def _():
        down().start()

    @pl.when(d < 7)
    def _():
        upward().start()

    def send_all(sources, targets, sems, size):
        for offset in offsets:
            pg, pd = peer(offset)
            pltpu.make_async_remote_copy(
                src_ref=sources.at[pl.ds((pg * 8 + pd) * size, size)],
                dst_ref=targets.at[pl.ds(me * size, size)],
                send_sem=sems.at[0], recv_sem=sems.at[1],
                device_id=(pg, pd), device_id_type=MESH,
            ).start()
        targets[pl.ds(me * size, size)] = sources[pl.ds(me * size, size)]

    def all_of(sources, targets, sems, size):
        return pltpu.make_async_remote_copy(
            src_ref=sources.at[pl.ds(0, 127 * size)], dst_ref=targets.at[pl.ds(0, 127 * size)],
            send_sem=sems.at[0], recv_sem=sems.at[1],
            device_id=(g, lax.rem(d + 1, 8)), device_id_type=MESH,
        )

    send_all(slots_out, slots_in, slot_sems, 1)
    fetch.wait()

    zero_rows = jnp.zeros((192, 128), F32)

    @pl.when(d == 0)
    def _():
        low_in[...] = zero_rows

    @pl.when(d == 7)
    def _():
        high_in[...] = zero_rows

    here, after = lane_matrices(l1, l2, sign_ref[0].astype(F32))
    here = here.astype(BF16)
    after = after.astype(BF16)

    straddles = jnp.where(both > 7, jnp.where(l1 < 7, 1, 0), jnp.where(both == 6, 1, 0))
    mask_a = jnp.where(both > 7, skip3 - 1, COLS - 1)
    no_next = jnp.where(straddles == 1, mask_a, 0)
    limit_a = jnp.where(both > 7, span2, span3)
    mask_b = jnp.where(both > 7, COLS - skip3, 0)
    inside = lane < limit_a
    chunk = 128

    def lane_part(base_row, i):
        at = base_row + i * chunk
        x = stepped[pl.ds(at, chunk), :]
        beyond = stepped[pl.ds(at + 8, chunk), :]
        column = jnp.right_shift(i * chunk + lax.broadcasted_iota(I32, (chunk, 128), 0), 3) & (COLS - 1)
        beyond = jnp.where((column & no_next) != no_next, beyond, 0.0)
        lanes_done[pl.ds(at, chunk), :] = dot_split(x, here) + dot_split(beyond, after)

    for i in range(1024 // chunk):
        lane_part(0, i)

    @pl.when(d < 7)
    def _():
        down().wait_recv()

    @pl.when(d > 0)
    def _():
        upward().wait_recv()

    start[halo_rows(0), :] = low_in[0:64]
    start[halo_rows(1), :] = low_in[64:128]
    start[halo_rows(6), :] = high_in[0:64]
    start[halo_rows(7), :] = high_in[64:128]
    coef[halo_coef(1), :] = low_in[128:192]
    coef[halo_coef(6), :] = high_in[128:192]
    outside = jnp.where(d == 0, 1, jnp.where(d == 7, 6, -1))

    def first_halo(c):
        xh = start[tile(TILE_HALO + c), :]
        value = advance(
            TILE_HALO + c, xh, pltpu.roll(xh, 7, 0), pltpu.roll(xh, 1, 0),
            coef[tile(2 * COLS + c), :], masks(c),
        )
        mid[tile(TILE_HALO + c), :] = jnp.where(sub == outside, 0.0, value)

    for i in range(512 // shift_chunk):
        shift_lanes(start, halo + i * shift_chunk)
    unrolled(COLS, 4, first_halo)
    for s, source_rows in enumerate(
        (
            halo_rows(1), halo_rows(2), node_rows(base, 1), node_rows(base, 2),
            node_rows(base, 13), node_rows(base, 14), halo_rows(5), halo_rows(6),
        )
    ):
        start[halo_rows(s), :] = mid[source_rows, :]
    for i in range(512 // shift_chunk):
        shift_lanes(start, halo + i * shift_chunk)

    def second_edge(c):
        xh = start[tile(TILE_HALO + c), :]
        stepped[tile(EDGE + c), :] = advance(
            TILE_HALO + c, xh, pltpu.roll(xh, 7, 0), pltpu.roll(xh, 1, 0),
            coef[tile(EDGE_COEF + c), :], masks(c),
        )

    unrolled(COLS, 4, second_edge)
    for i in range(512 // chunk):
        lane_part(EDGE * 8, i)
    for s, node in ((1, 0), (2, 1), (5, 14), (6, 15)):
        lanes_done[node_rows(0, node), :] = lanes_done[pl.ds(EDGE * 8 + s, COLS, stride=8), :]

    nothing = 2 * COLS

    def columns(source, target, mask, chosen):
        def step(c):
            j = c & mask
            off = j & (-j)
            has_up = (j != 0) & (j + off <= mask)
            for t in range(2):
                lower = jnp.where(j != 0, t * COLS + c - off, nothing)
                upper = jnp.where(has_up, t * COLS + c + off, nothing)
                update = 0.5 * (source[tile(lower), :] + source[tile(upper), :])
                if chosen is not None:
                    update = jnp.where(chosen, update, 0.0)
                target[tile(t * COLS + c), :] = source[tile(t * COLS + c), :] - update

        unrolled(COLS, 4, step)

    def lead_copy(slot, target, sent):
        return pltpu.make_async_remote_copy(
            src_ref=lead, dst_ref=lead_in.at[slot], send_sem=lead_send.at[sent],
            recv_sem=lead_recv.at[slot], device_id=(g, target), device_id_type=MESH,
        )

    routes = [(0, d > 0, lax.rem(d + 7, 8)), (1, lax.rem(d, 2) == 0, lax.rem(d + 1, 8))]
    routes += [(1, d == 0, 2), (1, d == 0, 4), (1, d == 4, 6), (2, d == 4, 2)]
    def column_matrix(mask):
        to_col = lax.broadcasted_iota(I32, (COLS, COLS), 0)
        from_col = lax.broadcasted_iota(I32, (COLS, COLS), 1)
        j = to_col & mask
        off = j & (-j)
        lower = from_col == to_col - off
        upper = (j + off <= mask) & (from_col == to_col + off)
        return jnp.where((j != 0) & (lower | upper), -0.5, 0.0).astype(BF16)

    def times_rows(matrix, rows):
        high = rows.astype(BF16)
        low = (rows - high.astype(F32)).astype(BF16)
        total = jnp.dot(matrix, low, preferred_element_type=F32)
        return total + jnp.dot(matrix, high, preferred_element_type=F32)

    first_node = lanes_done[node_rows(0, 0), :]
    lane_of_row = lax.broadcasted_iota(I32, (COLS, 128), 1)
    change = times_rows(column_matrix(mask_a), first_node)
    first_node = first_node + jnp.where(lane_of_row < limit_a, change, 0.0)
    lead[...] = first_node + times_rows(column_matrix(mask_b), first_node)
    for sent, (slot, condition, target) in enumerate(routes):

        @pl.when(condition)
        def _():
            lead_copy(slot, target, sent).start()

    columns(lanes_done, rows_done, mask_a, inside)
    columns(rows_done, lanes_done, mask_b, None)

    odd = (sub & 1) == 1
    two = (sub & 3) == 2
    four = sub == 4

    def fourth(c):
        x0 = lanes_done[tile(c), :]
        x1 = lanes_done[tile(COLS + c), :]
        for t, x, y, special in ((0, x0, jnp.where(sub == 0, x1, x0), 0.0), (1, x1, jnp.where(sub == 0, 0.0, x1), x0)):
            near1 = pltpu.roll(y, 7, 0) + pltpu.roll(x, 1, 0)
            near2 = pltpu.roll(y, 6, 0) + pltpu.roll(x, 2, 0)
            near4 = pltpu.roll(y, 4, 0) + pltpu.roll(x, 4, 0)
            near = jnp.where(odd, near1, jnp.where(two, near2, jnp.where(four, near4, special)))
            surplus[tile(t * COLS + c), :] = x - 0.5 * near

    unrolled(COLS, 2, fourth)

    all_of(slots_out, slots_in, slot_sems, 1).wait_recv()
    ids_col = slots_in[:, 0, :]
    ids_row = ids_col.T
    equal = []
    for r in range(2):
        of_r = jnp.broadcast_to(ids_col[:, r : r + 1], (128, 128))
        parts = [
            jnp.where(of_r == jnp.broadcast_to(ids_row[s : s + 1, :], (128, 128)), 1.0, 0.0)
            for s in range(2)
        ]
        equal.append(jnp.concatenate(parts, axis=1))
    equal = jnp.concatenate(equal, axis=0).astype(BF16)

    zero_lead = jnp.zeros((64, 128), F32)

    @pl.when(d == 7)
    def _():
        lead_in[0] = zero_lead

    @pl.when(d == 0)
    def _():
        lead_in[1] = zero_lead

    @pl.when(d != 2)
    def _():
        lead_in[2] = zero_lead

    @pl.when(d < 7)
    def _():
        lead_copy(0, lax.rem(d + 7, 8), 0).wait_recv()

    @pl.when(d > 0)
    def _():
        lead_copy(1, lax.rem(d + 1, 8), 0).wait_recv()

    @pl.when(d == 2)
    def _():
        lead_copy(2, lax.rem(d + 1, 8), 0).wait_recv()

    following = 0.5 * lead_in[0]
    use_next = jnp.where(lax.rem(d, 2) == 1, 1.0, 0.0)
    around = 0.5 * (lead_in[1] + lead_in[2]) + use_next * following
    surplus[node_rows(0, 0), :] = surplus[node_rows(0, 0), :] - around
    for node in (8, 12, 14, 15):
        surplus[node_rows(0, node), :] = surplus[node_rows(0, node), :] - following

    for o in range(128):
        of_rank = [surplus[pl.ds(index_s[1 + r, o], 8, stride=8), :] for r in range(2)]
        turned = pltpu.roll(of_rank[1], 4, 0)
        out_a[o * 8 : o * 8 + 8, :] = jnp.where(sub < 4, of_rank[0], turned)
        out_b[o * 8 : o * 8 + 8, :] = jnp.where(sub < 4, turned, of_rank[0])

    halves = ((out_a, in_a, ret_a, back_a), (out_b, in_b, ret_b, back_b))
    for half, (outgoing, arrived, _, _) in enumerate(halves):
        send_all(outgoing, arrived, out_sems.at[half], 8)

    for half, (outgoing, arrived, returned, back) in enumerate(halves):
        all_of(outgoing, arrived, out_sems.at[half], 8).wait_recv()
        for j in range(4):
            block = jnp.concatenate(
                [arrived[pl.ds((r ^ half) * 4 + j, 128, stride=8), :] for r in range(2)], axis=0
            )
            first = block.astype(BF16)
            second = (block - first.astype(F32)).astype(BF16)
            total = jnp.dot(equal, second, preferred_element_type=F32)
            total = total + jnp.dot(equal, first, preferred_element_type=F32)
            for r in range(2):
                returned[pl.ds((r ^ half) * 4 + j, 128, stride=8), :] = total[
                    r * 128 : (r + 1) * 128
                ]
        send_all(returned, back, back_sems.at[half], 8)

    for half, (_, _, returned, back) in enumerate(halves):
        all_of(returned, back, back_sems.at[half], 8).wait_recv()

        for block in range(128):
            at = (block // 64) * (8 * COLS) + (block % 8) * 64 + (block // 8) % 8 + half * 32
            out_ref[pl.ds(at, 4, stride=8), :] = back[pl.ds(index_s[3 * half, block], 4), :]

    @pl.when(d > 0)
    def _():
        down().wait_send()

    @pl.when(d < 7)
    def _():
        upward().wait_send()

    for sent, (slot, condition, target) in enumerate(routes):

        @pl.when(condition)
        def _():
            lead_copy(slot, target, sent).wait_send()

    all_of(slots_out, slots_in, slot_sems, 1).wait_send()
    for half, (outgoing, arrived, returned, back) in enumerate(halves):
        all_of(outgoing, arrived, out_sems.at[half], 8).wait_send()
        all_of(returned, back, back_sems.at[half], 8).wait_send()


def body(concentration, diffusion, velocity, levels, grid_signs, owner_list, slot_list):
    def in_hbm(array):
        return pltpu.with_memory_space_constraint(array, pltpu.HBM)

    def tiled(block):
        rows = block.reshape(2, 8, COLS, 128).transpose(0, 2, 1, 3).reshape(1024, 128)
        return in_hbm(rows)

    smem = pl.BlockSpec(memory_space=pltpu.SMEM)
    vmem = pl.BlockSpec(memory_space=pltpu.VMEM)
    anywhere = pl.BlockSpec(memory_space=pltpu.HBM)
    total_rows = (TILE_HALO + COLS + PAD) * 8
    rows = [total_rows, total_rows, 2080, 1560, 1560, 1032, 1032]
    combined = pl.pallas_call(
        combine_kernel,
        out_shape=jax.ShapeDtypeStruct((1032, 128), F32),
        in_specs=[smem, smem, smem, vmem, vmem, anywhere, anywhere],
        out_specs=vmem,
        scratch_shapes=[pltpu.VMEM((n, 128), F32) for n in rows]
        + [
            pltpu.VMEM((2, 192, 128), F32),
            pltpu.VMEM((192, 128), F32),
            pltpu.VMEM((192, 128), F32),
            pltpu.VMEM((64, 128), F32),
            pltpu.VMEM((3, 64, 128), F32),
        ]
        + [pltpu.VMEM((total_rows, 128), F32) for _ in range(5)]
        + [pltpu.VMEM((1032, 128), F32) for _ in range(8)]
        + [
            pltpu.VMEM((128, 1, 128), I32),
            pltpu.VMEM((128, 1, 128), I32),
            pltpu.VMEM((8, 128), I32),
            pltpu.SMEM((8, 128), I32),
            pltpu.SemaphoreType.DMA((3,)),
            pltpu.SemaphoreType.DMA((2,)),
            pltpu.SemaphoreType.DMA((2,)),
            pltpu.SemaphoreType.DMA((6,)),
            pltpu.SemaphoreType.DMA((3,)),
            pltpu.SemaphoreType.DMA((2,)),
            pltpu.SemaphoreType.DMA((2, 2)),
            pltpu.SemaphoreType.DMA((2, 2)),
        ],
        compiler_params=pltpu.CompilerParams(
            collective_id=0, has_side_effects=True, vmem_limit_bytes=24 << 20
        ),
        name="combine",
    )(
        in_hbm(levels), in_hbm(velocity), grid_signs, in_hbm(owner_list), in_hbm(slot_list),
        tiled(concentration), tiled(diffusion),
    )
    return combined[:1024].reshape(2, COLS, 8, 128).transpose(0, 2, 1, 3).reshape(1, 16, COLS * 128)


def solution(mesh):
    return jax.shard_map(
        body,
        mesh=mesh,
        in_specs=(
            P("grid", "dom", None),
            P("grid", "dom", None),
            P(),
            P("grid", None),
            P("grid"),
            P(("grid", "dom"), None),
            P(("grid", "dom"), None),
        ),
        out_specs=P("grid", "dom", None),
        check_vma=False,
    )
```

```python
import jax
import jax.numpy as jnp
from jax import lax
from jax.experimental import pallas as pl
from jax.experimental.pallas import tpu as pltpu
from jax.sharding import PartitionSpec as P

MESH = pl.DeviceIdType.MESH
F32 = jnp.float32
BF16 = jnp.bfloat16
I32 = jnp.int32

COLS = 64
PAD = 8
EDGE = 1032
TILE_HALO = PAD + 2 * COLS


def tile(at):
    return pl.ds(at * 8, 8)


def node_rows(base, node):
    return pl.ds(base + (node // 8) * COLS * 8 + node % 8, COLS, stride=8)


def dot_split(left, right):
    first = left.astype(BF16)
    second = (left - first.astype(F32)).astype(BF16)
    total = jnp.dot(second, right, preferred_element_type=F32)
    return total + jnp.dot(first, right, preferred_element_type=F32)


def lane_matrices(l1, l2, sign):
    source = lax.broadcasted_iota(I32, (128, 128), 0)
    target = lax.broadcasted_iota(I32, (128, 128), 1)
    both = l1 + l2
    low = [0, l1, both]
    top = [jnp.minimum(l1, 7), jnp.minimum(both, 7), 7]
    here = jnp.full((128, 128), sign, F32)
    after = jnp.full((128, 128), sign, F32)
    for field in range(3):
        width = jnp.maximum(top[field] - jnp.minimum(low[field], 7), 0)
        mask = jnp.left_shift(1, width) - 1
        shift = jnp.minimum(low[field], 7)
        fro = jnp.right_shift(source, shift) & mask
        to = jnp.right_shift(target, shift) & mask
        bit = to & (-to)
        same = jnp.where(fro == to, 1.0, 0.0)
        near = jnp.where((to != 0) & ((fro == to - bit) | (fro == to + bit)), -0.5, 0.0)
        plain = same + near
        wraps = (to != 0) & (to + bit == mask + 1) & (fro == 0)
        carry = jnp.where(wraps, -0.5, 0.0)
        here = here * plain
        if field == 0:
            after = after * plain
        elif field == 1:
            after = after * jnp.where(both > 6, jnp.where(width > 0, carry, 0.0), plain)
        else:
            after = after * jnp.where(both > 6, 1.0, carry)
    return here, after


def peer_offsets():
    offsets = [(k // 32, k // 8 % 4, k // 2 % 4, k % 2) for k in range(1, 128)]
    return sorted(offsets, key=lambda o: -sum(min(v, 4 - v) for v in o[:3]))


def unrolled(count, factor, step):
    def some(i, carry):
        for k in range(factor):
            step(i * factor + k)
        return carry

    lax.fori_loop(0, count // factor, some, 0)


def combine_kernel(
    lev_ref, vel_ref, sign_ref, own_ref, slot_ref, u_hbm, k_hbm, out_ref,
    start, mid, coef, stepped, lanes_done, rows_done, surplus, packs, low_in, high_in, lead, lead_in,
    sums, diffs, forth, back2, turned3,
    out_a, out_b, in_a, in_b, ret_a, ret_b, back_a, back_b, slots_out, slots_in, index_v, index_s,
    load_sem, send_sem, recv_sem, lead_send, lead_recv, slot_sems, out_sems, back_sems,
):
    g = lax.axis_index("grid")
    d = lax.axis_index("dom")
    me = g * 8 + d
    x_at, y_at = g // 4, g % 4
    z_at, core = d // 2, d % 2
    grids = [((x_at + i) % 4) * 4 + (y_at + j) % 4 for i in range(4) for j in range(4)]
    doms = [((z_at + i) % 4) * 2 + (core + j) % 2 for i in range(4) for j in range(2)]
    barrier = pltpu.get_barrier_semaphore()

    load_u = pltpu.make_async_copy(u_hbm, start.at[pl.ds(PAD * 8, 1024)], load_sem.at[0])
    load_k = pltpu.make_async_copy(k_hbm, coef.at[pl.ds(0, 1024)], load_sem.at[1])
    load_u.start()
    load_k.start()

    def peer(offset):
        return grids[offset[0] * 4 + offset[1]], doms[offset[2] * 2 + offset[3]]

    offsets = peer_offsets()
    for offset in offsets:
        pl.semaphore_signal(barrier, inc=1, device_id=peer(offset), device_id_type=MESH)

    owners = own_ref[...]
    own_row = jnp.broadcast_to(owners, (128, 128))
    own_col = own_row.T
    row = lax.broadcasted_iota(I32, (128, 128), 0)
    col = lax.broadcasted_iota(I32, (128, 128), 1)
    earlier = jnp.where((own_row == own_col) & (row < col), 1, 0)
    rank = jnp.sum(earlier, axis=0, keepdims=True)
    rank_row = jnp.broadcast_to(rank, (128, 128))
    rank_col = rank_row.T
    slot_row = jnp.broadcast_to(slot_ref[...], (128, 128))
    table = jnp.full((128, 128), -1, I32)
    index_v[...] = jnp.zeros((8, 128), I32)
    second_one = jnp.minimum(rank, 1)
    index_v[0:1] = 8 * owners + 4 * second_one
    index_v[3:4] = 8 * owners + 4 * (1 - second_one)
    for r in range(2):
        to_owner = (own_col == col) & (rank_col == r)
        index_v[1 + r : 2 + r] = jnp.sum(jnp.where(to_owner, row, 0), axis=0, keepdims=True)
        of_block = (own_row == row) & (rank_row == r)
        ids = jnp.sum(jnp.where(of_block, slot_row + 1, 0), axis=1, keepdims=True) - 1
        table = jnp.where(col == r, ids, table)
    slots_out[:, 0, :] = table
    fetch = pltpu.make_async_copy(index_v, index_s, load_sem.at[2])
    fetch.start()

    halo = TILE_HALO * 8

    def slot_rows(slot, count=1):
        return pl.ds(halo + slot * COLS, count * COLS)

    base = PAD * 8
    load_u.wait()
    load_k.wait()
    packs[0, 0:64] = start[node_rows(base, 0), :]
    packs[0, 64:128] = start[node_rows(base, 1), :]
    packs[0, 128:192] = coef[node_rows(0, 0), :]
    packs[1, 0:64] = start[node_rows(base, 14), :]
    packs[1, 64:128] = start[node_rows(base, 15), :]
    packs[1, 128:192] = coef[node_rows(0, 15), :]
    start[slot_rows(2, 2), :] = packs[0, 0:128]
    start[slot_rows(4, 2), :] = packs[1, 0:128]
    coef[1024:1088] = coef[node_rows(0, 1), :]
    coef[1088:1152] = coef[node_rows(0, 14), :]

    l1 = lev_ref[0, 0]
    l2 = lev_ref[0, 1]
    l3 = lev_ref[0, 2]
    both = l1 + l2
    lane = lax.broadcasted_iota(I32, (8, 128), 1)
    sub = lax.broadcasted_iota(I32, (8, 128), 0)
    span2 = jnp.left_shift(1, l1)
    span3 = jnp.minimum(jnp.left_shift(1, both), 128)
    skip3 = jnp.where(both == 8, 2, jnp.where(both == 9, 4, jnp.where(both == 10, 8, 1)))
    last1 = jnp.left_shift(1, l1) - 1
    last2 = jnp.left_shift(1, l2) - 1
    last3 = jnp.left_shift(1, l3) - 1
    drift1 = 0.1 * vel_ref[0]
    drift2 = 0.1 * vel_ref[1]
    drift3 = 0.1 * vel_ref[2]
    drift4 = 0.1 * vel_ref[3]
    stays2 = lane < 128 - span2
    comes2 = lane >= span2
    stays3 = lane < 128 - span3
    comes3 = lane >= span3

    source = lax.broadcasted_iota(I32, (128, 128), 0)
    target = lax.broadcasted_iota(I32, (128, 128), 1)
    at1 = target & last1
    from_up = jnp.where((source == target + 1) & (at1 != last1), 1.0, 0.0)
    from_down = jnp.where((source == target - 1) & (at1 != 0), 1.0, 0.0)
    turn2 = span2 & 127
    turn3 = span3 & 127
    forms = [
        from_up + from_down,
        from_up - from_down,
        jnp.where(source == ((target + turn2) & 127), 1.0, 0.0),
        jnp.where(source == ((target - turn2) & 127), 1.0, 0.0),
        jnp.where(source == ((target + turn3) & 127), 1.0, 0.0),
    ]
    forms = jnp.concatenate([jnp.concatenate([form, form], axis=0).astype(BF16) for form in forms], axis=1)
    shift_chunk = 128

    def shift_lanes(ref, at):
        x = ref[at : at + shift_chunk, :]
        high = x.astype(BF16)
        low = (x - high.astype(F32)).astype(BF16)
        shifted = jnp.dot(
            jnp.concatenate([high, low], axis=1), forms, preferred_element_type=F32
        )
        for form, scratch in enumerate((sums, diffs, forth, back2, turned3)):
            scratch[at : at + shift_chunk, :] = shifted[:, form * 128 : (form + 1) * 128]

    def masks(c):
        cell = c * 128 + lane
        i2 = jnp.right_shift(cell, l1) & last2
        i3 = jnp.right_shift(cell, both) & last3
        return (i2 != last2, i2 != 0, i3 != last3, i3 != 0)

    def advance(rows_at, x, ahead4, behind4, diff, ok):
        here = rows_at(0)
        p2 = jnp.where(stays2, forth[here, :], forth[rows_at(1), :])
        p2 = jnp.where(ok[0], p2, 0.0)
        m2 = jnp.where(comes2, back2[here, :], back2[rows_at(-1), :])
        m2 = jnp.where(ok[1], m2, 0.0)
        half = turned3[here, :]
        p3 = jnp.where(stays3, half, turned3[rows_at(skip3), :])
        p3 = jnp.where(ok[2], p3, 0.0)
        m3 = jnp.where(comes3, half, turned3[rows_at(-skip3), :])
        m3 = jnp.where(ok[3], m3, 0.0)
        second = (sums[here, :] + (p2 + m2)) + ((p3 + m3) + (ahead4 + behind4)) - 8.0 * x
        drift = (drift1 * diffs[here, :] + drift2 * (p2 - m2)) + (
            drift3 * (p3 - m3) + drift4 * (ahead4 - behind4)
        )
        return x + 0.1 * diff * second - drift

    def both_groups(ref, c, target, offset):
        ok = masks(c)
        x0 = ref[tile(PAD + c), :]
        x1 = ref[tile(PAD + COLS + c), :]
        value0 = advance(
            lambda k: tile(PAD + c + k), x0, pltpu.roll(jnp.where(sub == 0, x1, x0), 7, 0),
            pltpu.roll(x0, 1, 0), coef[tile(c), :], ok,
        )
        value1 = advance(
            lambda k: tile(PAD + COLS + c + k), x1, pltpu.roll(x1, 7, 0),
            pltpu.roll(jnp.where(sub == 7, x0, x1), 1, 0), coef[tile(COLS + c), :], ok,
        )
        target[tile(offset + c), :] = value0
        target[tile(offset + COLS + c), :] = value1

    for i in range(1024 // shift_chunk):
        shift_lanes(start, PAD * 8 + i * shift_chunk)
    unrolled(COLS, 2, lambda c: both_groups(start, c, mid, PAD))
    for i in range(1024 // shift_chunk):
        shift_lanes(mid, PAD * 8 + i * shift_chunk)
    unrolled(COLS, 2, lambda c: both_groups(mid, c, stepped, 0))
    for slot, node in ((2, 1), (3, 2), (4, 13), (5, 14)):
        mid[slot_rows(slot), :] = mid[node_rows(base, node), :]

    pl.semaphore_wait(barrier, 127)

    def down():
        return pltpu.make_async_remote_copy(
            src_ref=packs.at[0], dst_ref=high_in, send_sem=send_sem.at[0], recv_sem=recv_sem.at[0],
            device_id=(g, lax.rem(d + 7, 8)), device_id_type=MESH,
        )

    def upward():
        return pltpu.make_async_remote_copy(
            src_ref=packs.at[1], dst_ref=low_in, send_sem=send_sem.at[1], recv_sem=recv_sem.at[1],
            device_id=(g, lax.rem(d + 1, 8)), device_id_type=MESH,
        )

    @pl.when(d > 0)
    def _():
        down().start()

    @pl.when(d < 7)
    def _():
        upward().start()

    def send_all(sources, targets, sems, size):
        for offset in offsets:
            pg, pd = peer(offset)
            pltpu.make_async_remote_copy(
                src_ref=sources.at[pl.ds((pg * 8 + pd) * size, size)],
                dst_ref=targets.at[pl.ds(me * size, size)],
                send_sem=sems.at[0], recv_sem=sems.at[1],
                device_id=(pg, pd), device_id_type=MESH,
            ).start()
        targets[pl.ds(me * size, size)] = sources[pl.ds(me * size, size)]

    def all_of(sources, targets, sems, size):
        return pltpu.make_async_remote_copy(
            src_ref=sources.at[pl.ds(0, 127 * size)], dst_ref=targets.at[pl.ds(0, 127 * size)],
            send_sem=sems.at[0], recv_sem=sems.at[1],
            device_id=(g, lax.rem(d + 1, 8)), device_id_type=MESH,
        )

    send_all(slots_out, slots_in, slot_sems, 1)
    fetch.wait()

    zero_rows = jnp.zeros((192, 128), F32)

    @pl.when(d == 0)
    def _():
        low_in[...] = zero_rows

    @pl.when(d == 7)
    def _():
        high_in[...] = zero_rows

    here, after = lane_matrices(l1, l2, sign_ref[0].astype(F32))
    here = here.astype(BF16)
    after = after.astype(BF16)

    straddles = jnp.where(both > 7, jnp.where(l1 < 7, 1, 0), jnp.where(both == 6, 1, 0))
    mask_a = jnp.where(both > 7, skip3 - 1, COLS - 1)
    no_next = jnp.where(straddles == 1, mask_a, 0)
    limit_a = jnp.where(both > 7, span2, span3)
    mask_b = jnp.where(both > 7, COLS - skip3, 0)
    inside = lane < limit_a
    chunk = 128

    def lane_part(base_row, i):
        at = base_row + i * chunk
        x = stepped[pl.ds(at, chunk), :]
        beyond = stepped[pl.ds(at + 8, chunk), :]
        column = jnp.right_shift(i * chunk + lax.broadcasted_iota(I32, (chunk, 128), 0), 3) & (COLS - 1)
        beyond = jnp.where((column & no_next) != no_next, beyond, 0.0)
        lanes_done[pl.ds(at, chunk), :] = dot_split(x, here) + dot_split(beyond, after)

    for i in range(1024 // chunk):
        lane_part(0, i)

    to_col = lax.broadcasted_iota(I32, (128, 128), 0)
    from_col = lax.broadcasted_iota(I32, (128, 128), 1) & (COLS - 1)
    upper_half = to_col < COLS
    to_col = to_col & (COLS - 1)

    def column_field(mask):
        to_field, from_field = to_col & mask, from_col & mask
        bit = to_field & (-to_field)
        near = (from_field == to_field - bit) | (from_field == to_field + bit)
        near = jnp.where((to_field != 0) & near, -0.5, 0.0)
        return jnp.where(to_field == from_field, 1.0, near)

    same_a = jnp.where((to_col & mask_a) == (from_col & mask_a), 1.0, 0.0)
    columns_matrix = jnp.where(upper_half, column_field(mask_a), same_a) * column_field(mask_b)
    columns_matrix = columns_matrix.astype(BF16)

    def columns(rows):
        high = rows.astype(BF16)
        low = (rows - high.astype(F32)).astype(BF16)
        terms = jnp.concatenate([high, low], axis=0)
        done = jnp.dot(columns_matrix, terms, preferred_element_type=F32)
        lane_of_row = lax.broadcasted_iota(I32, (COLS, rows.shape[1]), 1) & 127
        return jnp.where(lane_of_row < limit_a, done[:COLS], done[COLS:])

    def edge_step(ref, moves):
        for i in range(8):
            ok = masks(i * 8 + sub)
            for slot, diff, write in moves:
                at = halo + slot * COLS + i * 8
                value = advance(
                    lambda k: pl.ds(at + k, 8), ref[at : at + 8, :],
                    ref[at + COLS : at + COLS + 8, :], ref[at - COLS : at - COLS + 8, :],
                    diff(i * 8), ok,
                )
                write(i * 8, value)

    def to_mid(slot, zero_at):
        def write(i, value):
            if zero_at is not None:
                value = jnp.where(d == zero_at, 0.0, value)
            mid[halo + slot * COLS + i : halo + slot * COLS + i + 8, :] = value

        return write

    def to_stepped(place):
        def write(i, value):
            stepped[EDGE + place * COLS + i : EDGE + place * COLS + i + 8, :] = value

        return write

    def lane_edge(place):
        at = EDGE + place * COLS
        x = stepped[at : at + 128, :]
        beyond = stepped[at + 1 : at + 129, :]
        column = lax.broadcasted_iota(I32, (128, 128), 0) & (COLS - 1)
        beyond = jnp.where((column & no_next) != no_next, beyond, 0.0)
        lanes_done[at : at + 128, :] = dot_split(x, here) + dot_split(beyond, after)

    coef0 = lambda i: packs[0, 128 + i : 136 + i, :]
    coef15 = lambda i: packs[1, 128 + i : 136 + i, :]

    @pl.when(d > 0)
    def _():
        upward().wait_recv()

    start[slot_rows(0, 2), :] = low_in[0:128]
    shift_lanes(start, halo + COLS)
    below = lambda i: low_in[128 + i : 136 + i, :]
    edge_step(start, ((1, below, to_mid(0, 0)), (2, coef0, to_mid(1, None))))
    shift_lanes(mid, halo + COLS)
    coef1 = lambda i: coef[1024 + i : 1032 + i, :]
    edge_step(mid, ((1, coef0, to_stepped(0)), (2, coef1, to_stepped(1))))
    lane_edge(0)

    def lead_copy(slot, target, sent):
        return pltpu.make_async_remote_copy(
            src_ref=lead, dst_ref=lead_in.at[slot], send_sem=lead_send.at[sent],
            recv_sem=lead_recv.at[slot], device_id=(g, target), device_id_type=MESH,
        )

    routes = [(0, d > 0, lax.rem(d + 7, 8)), (1, lax.rem(d, 2) == 0, lax.rem(d + 1, 8))]
    routes += [(1, d == 0, 2), (1, d == 0, 4), (1, d == 4, 6), (2, d == 4, 2)]
    lead[...] = columns(lanes_done[EDGE : EDGE + COLS, :])
    for sent, (slot, condition, target) in enumerate(routes):

        @pl.when(condition)
        def _():
            lead_copy(slot, target, sent).start()

    @pl.when(d < 7)
    def _():
        down().wait_recv()

    start[slot_rows(6, 2), :] = high_in[0:128]
    shift_lanes(start, halo + 5 * COLS)
    above = lambda i: high_in[128 + i : 136 + i, :]
    edge_step(start, ((5, coef15, to_mid(6, None)), (6, above, to_mid(7, 7))))
    shift_lanes(mid, halo + 5 * COLS)
    coef14 = lambda i: coef[1088 + i : 1096 + i, :]
    edge_step(mid, ((5, coef14, to_stepped(2)), (6, coef15, to_stepped(3))))
    lane_edge(2)

    places = {0: 0, 1: 1, 14: 2, 15: 3}

    def lanes_of(node):
        if node in places:
            at = EDGE + places[node] * COLS
            return lanes_done[at : at + COLS, :]
        return lanes_done[node_rows(0, node), :]

    for node in range(0, 16, 2):
        pair = columns(jnp.concatenate([lanes_of(node), lanes_of(node + 1)], axis=1))
        rows_done[node * COLS : (node + 1) * COLS, :] = pair[:, :128]
        rows_done[(node + 1) * COLS : (node + 2) * COLS, :] = pair[:, 128:]

    for i in range(0, COLS, 8):
        nodes = [rows_done[n * COLS + i : n * COLS + i + 8, :] for n in range(16)]
        for n in range(16):
            value = nodes[n]
            bit = n & (-n)
            if n:
                near = nodes[n - bit]
                if n + bit < 16:
                    near = near + nodes[n + bit]
                value = value - 0.5 * near
            surplus[n * COLS + i : n * COLS + i + 8, :] = value

    all_of(slots_out, slots_in, slot_sems, 1).wait_recv()
    ids_col = slots_in[:, 0, :]
    ids_row = ids_col.T
    equal = []
    for r in range(2):
        of_r = jnp.broadcast_to(ids_col[:, r : r + 1], (128, 128))
        parts = [
            jnp.where(of_r == jnp.broadcast_to(ids_row[s : s + 1, :], (128, 128)), 1.0, 0.0)
            for s in range(2)
        ]
        equal.append(jnp.concatenate(parts, axis=1))
    equal = jnp.concatenate(equal, axis=0).astype(BF16)

    zero_lead = jnp.zeros((64, 128), F32)

    @pl.when(d == 7)
    def _():
        lead_in[0] = zero_lead

    @pl.when(d == 0)
    def _():
        lead_in[1] = zero_lead

    @pl.when(d != 2)
    def _():
        lead_in[2] = zero_lead

    @pl.when(d < 7)
    def _():
        lead_copy(0, lax.rem(d + 7, 8), 0).wait_recv()

    @pl.when(d > 0)
    def _():
        lead_copy(1, lax.rem(d + 1, 8), 0).wait_recv()

    @pl.when(d == 2)
    def _():
        lead_copy(2, lax.rem(d + 1, 8), 0).wait_recv()

    following = 0.5 * lead_in[0]
    use_next = jnp.where(lax.rem(d, 2) == 1, 1.0, 0.0)
    around = 0.5 * (lead_in[1] + lead_in[2]) + use_next * following
    surplus[0:COLS] = surplus[0:COLS] - around
    for node in (8, 12, 14, 15):
        at = node * COLS
        surplus[at : at + COLS] = surplus[at : at + COLS] - following

    for o in range(128):
        of_rank = [surplus[tile(index_s[1 + r, o]), :] for r in range(2)]
        turned = pltpu.roll(of_rank[1], 4, 0)
        out_a[o * 8 : o * 8 + 8, :] = jnp.where(sub < 4, of_rank[0], turned)
        out_b[o * 8 : o * 8 + 8, :] = jnp.where(sub < 4, turned, of_rank[0])

    halves = ((out_a, in_a, ret_a, back_a), (out_b, in_b, ret_b, back_b))
    for half, (outgoing, arrived, _, _) in enumerate(halves):
        send_all(outgoing, arrived, out_sems.at[half], 8)

    for half, (outgoing, arrived, returned, back) in enumerate(halves):
        all_of(outgoing, arrived, out_sems.at[half], 8).wait_recv()
        for j in range(4):
            block = jnp.concatenate(
                [arrived[pl.ds((r ^ half) * 4 + j, 128, stride=8), :] for r in range(2)], axis=0
            )
            first = block.astype(BF16)
            second = (block - first.astype(F32)).astype(BF16)
            total = jnp.dot(equal, second, preferred_element_type=F32)
            total = total + jnp.dot(equal, first, preferred_element_type=F32)
            for r in range(2):
                returned[pl.ds((r ^ half) * 4 + j, 128, stride=8), :] = total[
                    r * 128 : (r + 1) * 128
                ]
        send_all(returned, back, back_sems.at[half], 8)

    for half, (_, _, returned, back) in enumerate(halves):
        all_of(returned, back, back_sems.at[half], 8).wait_recv()

        for block in range(128):
            at = (block // 64) * (8 * COLS) + (block % 8) * 64 + (block // 8) % 8 + half * 32
            out_ref[pl.ds(at, 4, stride=8), :] = back[pl.ds(index_s[3 * half, block], 4), :]

    @pl.when(d > 0)
    def _():
        down().wait_send()

    @pl.when(d < 7)
    def _():
        upward().wait_send()

    for sent, (slot, condition, target) in enumerate(routes):

        @pl.when(condition)
        def _():
            lead_copy(slot, target, sent).wait_send()

    all_of(slots_out, slots_in, slot_sems, 1).wait_send()
    for half, (outgoing, arrived, returned, back) in enumerate(halves):
        all_of(outgoing, arrived, out_sems.at[half], 8).wait_send()
        all_of(returned, back, back_sems.at[half], 8).wait_send()


def body(concentration, diffusion, velocity, levels, grid_signs, owner_list, slot_list):
    def in_hbm(array):
        return pltpu.with_memory_space_constraint(array, pltpu.HBM)

    def tiled(block):
        rows = block.reshape(2, 8, COLS, 128).transpose(0, 2, 1, 3).reshape(1024, 128)
        return in_hbm(rows)

    smem = pl.BlockSpec(memory_space=pltpu.SMEM)
    vmem = pl.BlockSpec(memory_space=pltpu.VMEM)
    anywhere = pl.BlockSpec(memory_space=pltpu.HBM)
    total_rows = (TILE_HALO + COLS + PAD) * 8
    rows = [total_rows, total_rows, 1152, 1296, 1296, 1032, 1032]
    combined = pl.pallas_call(
        combine_kernel,
        out_shape=jax.ShapeDtypeStruct((1032, 128), F32),
        in_specs=[smem, smem, smem, vmem, vmem, anywhere, anywhere],
        out_specs=vmem,
        scratch_shapes=[pltpu.VMEM((n, 128), F32) for n in rows]
        + [
            pltpu.VMEM((2, 192, 128), F32),
            pltpu.VMEM((192, 128), F32),
            pltpu.VMEM((192, 128), F32),
            pltpu.VMEM((64, 128), F32),
            pltpu.VMEM((3, 64, 128), F32),
        ]
        + [pltpu.VMEM((total_rows, 128), F32) for _ in range(5)]
        + [pltpu.VMEM((1032, 128), F32) for _ in range(8)]
        + [
            pltpu.VMEM((128, 1, 128), I32),
            pltpu.VMEM((128, 1, 128), I32),
            pltpu.VMEM((8, 128), I32),
            pltpu.SMEM((8, 128), I32),
            pltpu.SemaphoreType.DMA((3,)),
            pltpu.SemaphoreType.DMA((2,)),
            pltpu.SemaphoreType.DMA((2,)),
            pltpu.SemaphoreType.DMA((6,)),
            pltpu.SemaphoreType.DMA((3,)),
            pltpu.SemaphoreType.DMA((2,)),
            pltpu.SemaphoreType.DMA((2, 2)),
            pltpu.SemaphoreType.DMA((2, 2)),
        ],
        compiler_params=pltpu.CompilerParams(
            collective_id=0, has_side_effects=True, vmem_limit_bytes=24 << 20
        ),
        name="combine",
    )(
        in_hbm(levels), in_hbm(velocity), grid_signs, in_hbm(owner_list), in_hbm(slot_list),
        tiled(concentration), tiled(diffusion),
    )
    return combined[:1024].reshape(2, COLS, 8, 128).transpose(0, 2, 1, 3).reshape(1, 16, COLS * 128)


def solution(mesh):
    return jax.shard_map(
        body,
        mesh=mesh,
        in_specs=(
            P("grid", "dom", None),
            P("grid", "dom", None),
            P(),
            P("grid", None),
            P("grid"),
            P(("grid", "dom"), None),
            P(("grid", "dom"), None),
        ),
        out_specs=P("grid", "dom", None),
        check_vma=False,
    )
```

```python
import jax
import jax.numpy as jnp
from jax import lax
from jax.experimental import pallas as pl
from jax.experimental.pallas import tpu as pltpu
from jax.sharding import PartitionSpec as P

MESH = pl.DeviceIdType.MESH
F32 = jnp.float32
BF16 = jnp.bfloat16
I32 = jnp.int32

COLS = 64
PAD = 8
EDGE = 1032
TILE_HALO = PAD + 2 * COLS


def tile(at):
    return pl.ds(at * 8, 8)


def node_rows(base, node):
    return pl.ds(base + (node // 8) * COLS * 8 + node % 8, COLS, stride=8)


def dot_split(left, right):
    first = left.astype(BF16)
    second = (left - first.astype(F32)).astype(BF16)
    total = jnp.dot(second, right, preferred_element_type=F32)
    return total + jnp.dot(first, right, preferred_element_type=F32)


def lane_matrices(l1, l2, sign):
    source = lax.broadcasted_iota(I32, (128, 128), 0)
    target = lax.broadcasted_iota(I32, (128, 128), 1)
    both = l1 + l2
    low = [0, l1, both]
    top = [jnp.minimum(l1, 7), jnp.minimum(both, 7), 7]
    here = jnp.full((128, 128), sign, F32)
    after = jnp.full((128, 128), sign, F32)
    for field in range(3):
        width = jnp.maximum(top[field] - jnp.minimum(low[field], 7), 0)
        mask = jnp.left_shift(1, width) - 1
        shift = jnp.minimum(low[field], 7)
        fro = jnp.right_shift(source, shift) & mask
        to = jnp.right_shift(target, shift) & mask
        bit = to & (-to)
        same = jnp.where(fro == to, 1.0, 0.0)
        near = jnp.where((to != 0) & ((fro == to - bit) | (fro == to + bit)), -0.5, 0.0)
        plain = same + near
        wraps = (to != 0) & (to + bit == mask + 1) & (fro == 0)
        carry = jnp.where(wraps, -0.5, 0.0)
        here = here * plain
        if field == 0:
            after = after * plain
        elif field == 1:
            after = after * jnp.where(both > 6, jnp.where(width > 0, carry, 0.0), plain)
        else:
            after = after * jnp.where(both > 6, 1.0, carry)
    return here, after


def peer_offsets():
    offsets = [(k // 32, k // 8 % 4, k // 2 % 4, k % 2) for k in range(1, 128)]
    return sorted(offsets, key=lambda o: -sum(min(v, 4 - v) for v in o[:3]))


def unrolled(count, factor, step):
    def some(i, carry):
        for k in range(factor):
            step(i * factor + k)
        return carry

    lax.fori_loop(0, count // factor, some, 0)


def combine_kernel(
    lev_ref, vel_ref, sign_ref, own_ref, slot_ref, u_hbm, k_hbm, out_ref,
    start, mid, coef, stepped, lanes_done, rows_done, surplus, packs, low_in, high_in, lead, lead_in,
    sums, diffs, forth, back2, turned3,
    out_a, out_b, in_a, in_b, ret_a, ret_b, back_a, back_b, slots_out, slots_in, index_v, index_s,
    load_sem, send_sem, recv_sem, lead_send, lead_recv, slot_sems, out_sems, back_sems,
):
    g = lax.axis_index("grid")
    d = lax.axis_index("dom")
    me = g * 8 + d
    x_at, y_at = g // 4, g % 4
    z_at, core = d // 2, d % 2
    grids = [((x_at + i) % 4) * 4 + (y_at + j) % 4 for i in range(4) for j in range(4)]
    doms = [((z_at + i) % 4) * 2 + (core + j) % 2 for i in range(4) for j in range(2)]
    barrier = pltpu.get_barrier_semaphore()

    load_u = pltpu.make_async_copy(u_hbm, start.at[pl.ds(PAD * 8, 1024)], load_sem.at[0])
    load_k = pltpu.make_async_copy(k_hbm, coef.at[pl.ds(0, 1024)], load_sem.at[1])
    load_u.start()
    load_k.start()

    def peer(offset):
        return grids[offset[0] * 4 + offset[1]], doms[offset[2] * 2 + offset[3]]

    offsets = peer_offsets()
    for offset in offsets:
        pl.semaphore_signal(barrier, inc=1, device_id=peer(offset), device_id_type=MESH)

    owners = own_ref[...]
    own_row = jnp.broadcast_to(owners, (128, 128))
    own_col = own_row.T
    row = lax.broadcasted_iota(I32, (128, 128), 0)
    col = lax.broadcasted_iota(I32, (128, 128), 1)
    earlier = jnp.where((own_row == own_col) & (row < col), 1, 0)
    rank = jnp.sum(earlier, axis=0, keepdims=True)
    rank_row = jnp.broadcast_to(rank, (128, 128))
    rank_col = rank_row.T
    slot_row = jnp.broadcast_to(slot_ref[...], (128, 128))
    table = jnp.full((128, 128), -1, I32)
    index_v[...] = jnp.zeros((8, 128), I32)
    second_one = jnp.minimum(rank, 1)
    index_v[0:1] = 8 * owners + 4 * second_one
    index_v[3:4] = 8 * owners + 4 * (1 - second_one)
    for r in range(2):
        to_owner = (own_col == col) & (rank_col == r)
        index_v[1 + r : 2 + r] = jnp.sum(jnp.where(to_owner, row, 0), axis=0, keepdims=True)
        of_block = (own_row == row) & (rank_row == r)
        ids = jnp.sum(jnp.where(of_block, slot_row + 1, 0), axis=1, keepdims=True) - 1
        table = jnp.where(col == r, ids, table)
    slots_out[:, 0, :] = table
    fetch = pltpu.make_async_copy(index_v, index_s, load_sem.at[2])
    fetch.start()

    halo = TILE_HALO * 8

    def slot_rows(slot, count=1):
        return pl.ds(halo + slot * COLS, count * COLS)

    base = PAD * 8
    load_u.wait()
    load_k.wait()
    packs[0, 0:64] = start[node_rows(base, 0), :]
    packs[0, 64:128] = start[node_rows(base, 1), :]
    packs[0, 128:192] = coef[node_rows(0, 0), :]
    packs[1, 0:64] = start[node_rows(base, 14), :]
    packs[1, 64:128] = start[node_rows(base, 15), :]
    packs[1, 128:192] = coef[node_rows(0, 15), :]
    start[slot_rows(2, 2), :] = packs[0, 0:128]
    start[slot_rows(4, 2), :] = packs[1, 0:128]
    coef[1024:1088] = coef[node_rows(0, 1), :]
    coef[1088:1152] = coef[node_rows(0, 14), :]

    l1 = lev_ref[0, 0]
    l2 = lev_ref[0, 1]
    l3 = lev_ref[0, 2]
    both = l1 + l2
    lane = lax.broadcasted_iota(I32, (8, 128), 1)
    sub = lax.broadcasted_iota(I32, (8, 128), 0)
    span2 = jnp.left_shift(1, l1)
    span3 = jnp.minimum(jnp.left_shift(1, both), 128)
    skip3 = jnp.where(both == 8, 2, jnp.where(both == 9, 4, jnp.where(both == 10, 8, 1)))
    last1 = jnp.left_shift(1, l1) - 1
    last2 = jnp.left_shift(1, l2) - 1
    last3 = jnp.left_shift(1, l3) - 1
    drift1 = 0.1 * vel_ref[0]
    drift2 = 0.1 * vel_ref[1]
    drift3 = 0.1 * vel_ref[2]
    drift4 = 0.1 * vel_ref[3]
    stays2 = lane < 128 - span2
    comes2 = lane >= span2
    stays3 = lane < 128 - span3
    comes3 = lane >= span3

    source = lax.broadcasted_iota(I32, (128, 128), 0)
    target = lax.broadcasted_iota(I32, (128, 128), 1)
    at1 = target & last1
    from_up = jnp.where((source == target + 1) & (at1 != last1), 1.0, 0.0)
    from_down = jnp.where((source == target - 1) & (at1 != 0), 1.0, 0.0)
    turn2 = span2 & 127
    turn3 = span3 & 127
    forms = [
        from_up + from_down,
        from_up - from_down,
        jnp.where(source == ((target + turn2) & 127), 1.0, 0.0),
        jnp.where(source == ((target - turn2) & 127), 1.0, 0.0),
        jnp.where(source == ((target + turn3) & 127), 1.0, 0.0),
    ]
    forms = jnp.concatenate([jnp.concatenate([form, form], axis=0).astype(BF16) for form in forms], axis=1)
    shift_chunk = 128

    def shift_lanes(ref, at):
        x = ref[at : at + shift_chunk, :]
        high = x.astype(BF16)
        low = (x - high.astype(F32)).astype(BF16)
        shifted = jnp.dot(
            jnp.concatenate([high, low], axis=1), forms, preferred_element_type=F32
        )
        for form, scratch in enumerate((sums, diffs, forth, back2, turned3)):
            scratch[at : at + shift_chunk, :] = shifted[:, form * 128 : (form + 1) * 128]

    def masks(c):
        cell = c * 128 + lane
        i2 = jnp.right_shift(cell, l1) & last2
        i3 = jnp.right_shift(cell, both) & last3
        return (i2 != last2, i2 != 0, i3 != last3, i3 != 0)

    def advance(rows_at, x, ahead4, behind4, diff, ok):
        here = rows_at(0)
        p2 = jnp.where(stays2, forth[here, :], forth[rows_at(1), :])
        p2 = jnp.where(ok[0], p2, 0.0)
        m2 = jnp.where(comes2, back2[here, :], back2[rows_at(-1), :])
        m2 = jnp.where(ok[1], m2, 0.0)
        half = turned3[here, :]
        p3 = jnp.where(stays3, half, turned3[rows_at(skip3), :])
        p3 = jnp.where(ok[2], p3, 0.0)
        m3 = jnp.where(comes3, half, turned3[rows_at(-skip3), :])
        m3 = jnp.where(ok[3], m3, 0.0)
        second = (sums[here, :] + (p2 + m2)) + ((p3 + m3) + (ahead4 + behind4)) - 8.0 * x
        drift = (drift1 * diffs[here, :] + drift2 * (p2 - m2)) + (
            drift3 * (p3 - m3) + drift4 * (ahead4 - behind4)
        )
        return x + 0.1 * diff * second - drift

    def both_groups(ref, c, target, offset):
        ok = masks(c)
        x0 = ref[tile(PAD + c), :]
        x1 = ref[tile(PAD + COLS + c), :]
        value0 = advance(
            lambda k: tile(PAD + c + k), x0, pltpu.roll(jnp.where(sub == 0, x1, x0), 7, 0),
            pltpu.roll(x0, 1, 0), coef[tile(c), :], ok,
        )
        value1 = advance(
            lambda k: tile(PAD + COLS + c + k), x1, pltpu.roll(x1, 7, 0),
            pltpu.roll(jnp.where(sub == 7, x0, x1), 1, 0), coef[tile(COLS + c), :], ok,
        )
        target[tile(offset + c), :] = value0
        target[tile(offset + COLS + c), :] = value1

    for i in range(1024 // shift_chunk):
        shift_lanes(start, PAD * 8 + i * shift_chunk)
    unrolled(COLS, 2, lambda c: both_groups(start, c, mid, PAD))
    for i in range(1024 // shift_chunk):
        shift_lanes(mid, PAD * 8 + i * shift_chunk)
    pl.semaphore_wait(barrier, 127)

    def down():
        return pltpu.make_async_remote_copy(
            src_ref=packs.at[0], dst_ref=high_in, send_sem=send_sem.at[0], recv_sem=recv_sem.at[0],
            device_id=(g, lax.rem(d + 7, 8)), device_id_type=MESH,
        )

    def upward():
        return pltpu.make_async_remote_copy(
            src_ref=packs.at[1], dst_ref=low_in, send_sem=send_sem.at[1], recv_sem=recv_sem.at[1],
            device_id=(g, lax.rem(d + 1, 8)), device_id_type=MESH,
        )

    @pl.when(d > 0)
    def _():
        down().start()

    @pl.when(d < 7)
    def _():
        upward().start()

    def send_all(sources, targets, sems, size):
        for offset in offsets:
            pg, pd = peer(offset)
            pltpu.make_async_remote_copy(
                src_ref=sources.at[pl.ds((pg * 8 + pd) * size, size)],
                dst_ref=targets.at[pl.ds(me * size, size)],
                send_sem=sems.at[0], recv_sem=sems.at[1],
                device_id=(pg, pd), device_id_type=MESH,
            ).start()
        targets[pl.ds(me * size, size)] = sources[pl.ds(me * size, size)]

    def all_of(sources, targets, sems, size):
        return pltpu.make_async_remote_copy(
            src_ref=sources.at[pl.ds(0, 127 * size)], dst_ref=targets.at[pl.ds(0, 127 * size)],
            send_sem=sems.at[0], recv_sem=sems.at[1],
            device_id=(g, lax.rem(d + 1, 8)), device_id_type=MESH,
        )

    unrolled(COLS, 2, lambda c: both_groups(mid, c, stepped, 0))
    for slot, node in ((2, 1), (3, 2), (4, 13), (5, 14)):
        mid[slot_rows(slot), :] = mid[node_rows(base, node), :]
    fetch.wait()

    zero_rows = jnp.zeros((192, 128), F32)

    @pl.when(d == 0)
    def _():
        low_in[...] = zero_rows

    @pl.when(d == 7)
    def _():
        high_in[...] = zero_rows

    here, after = lane_matrices(l1, l2, sign_ref[0].astype(F32))
    here = here.astype(BF16)
    after = after.astype(BF16)

    straddles = jnp.where(both > 7, jnp.where(l1 < 7, 1, 0), jnp.where(both == 6, 1, 0))
    mask_a = jnp.where(both > 7, skip3 - 1, COLS - 1)
    no_next = jnp.where(straddles == 1, mask_a, 0)
    limit_a = jnp.where(both > 7, span2, span3)
    mask_b = jnp.where(both > 7, COLS - skip3, 0)
    inside = lane < limit_a
    chunk = 128

    def lane_part(base_row, i):
        at = base_row + i * chunk
        x = stepped[pl.ds(at, chunk), :]
        beyond = stepped[pl.ds(at + 8, chunk), :]
        column = jnp.right_shift(i * chunk + lax.broadcasted_iota(I32, (chunk, 128), 0), 3) & (COLS - 1)
        beyond = jnp.where((column & no_next) != no_next, beyond, 0.0)
        lanes_done[pl.ds(at, chunk), :] = dot_split(x, here) + dot_split(beyond, after)

    for i in range(1024 // chunk):
        lane_part(0, i)

    to_col = lax.broadcasted_iota(I32, (128, 128), 0)
    from_col = lax.broadcasted_iota(I32, (128, 128), 1) & (COLS - 1)
    upper_half = to_col < COLS
    to_col = to_col & (COLS - 1)

    def column_field(mask):
        to_field, from_field = to_col & mask, from_col & mask
        bit = to_field & (-to_field)
        near = (from_field == to_field - bit) | (from_field == to_field + bit)
        near = jnp.where((to_field != 0) & near, -0.5, 0.0)
        return jnp.where(to_field == from_field, 1.0, near)

    same_a = jnp.where((to_col & mask_a) == (from_col & mask_a), 1.0, 0.0)
    columns_matrix = jnp.where(upper_half, column_field(mask_a), same_a) * column_field(mask_b)
    columns_matrix = columns_matrix.astype(BF16)

    def columns(rows):
        high = rows.astype(BF16)
        low = (rows - high.astype(F32)).astype(BF16)
        terms = jnp.concatenate([high, low], axis=0)
        done = jnp.dot(columns_matrix, terms, preferred_element_type=F32)
        lane_of_row = lax.broadcasted_iota(I32, (COLS, rows.shape[1]), 1) & 127
        return jnp.where(lane_of_row < limit_a, done[:COLS], done[COLS:])

    def edge_step(ref, moves):
        for i in range(8):
            ok = masks(i * 8 + sub)
            for slot, diff, write in moves:
                at = halo + slot * COLS + i * 8
                value = advance(
                    lambda k: pl.ds(at + k, 8), ref[at : at + 8, :],
                    ref[at + COLS : at + COLS + 8, :], ref[at - COLS : at - COLS + 8, :],
                    diff(i * 8), ok,
                )
                write(i * 8, value)

    def to_mid(slot, zero_at):
        def write(i, value):
            if zero_at is not None:
                value = jnp.where(d == zero_at, 0.0, value)
            mid[halo + slot * COLS + i : halo + slot * COLS + i + 8, :] = value

        return write

    def to_stepped(place):
        def write(i, value):
            stepped[EDGE + place * COLS + i : EDGE + place * COLS + i + 8, :] = value

        return write

    def lane_edge(place):
        at = EDGE + place * COLS
        x = stepped[at : at + 128, :]
        beyond = stepped[at + 1 : at + 129, :]
        column = lax.broadcasted_iota(I32, (128, 128), 0) & (COLS - 1)
        beyond = jnp.where((column & no_next) != no_next, beyond, 0.0)
        lanes_done[at : at + 128, :] = dot_split(x, here) + dot_split(beyond, after)

    coef0 = lambda i: packs[0, 128 + i : 136 + i, :]
    coef15 = lambda i: packs[1, 128 + i : 136 + i, :]

    @pl.when(d > 0)
    def _():
        upward().wait_recv()

    start[slot_rows(0, 2), :] = low_in[0:128]
    shift_lanes(start, halo + COLS)
    below = lambda i: low_in[128 + i : 136 + i, :]
    edge_step(start, ((1, below, to_mid(0, 0)), (2, coef0, to_mid(1, None))))
    shift_lanes(mid, halo + COLS)
    coef1 = lambda i: coef[1024 + i : 1032 + i, :]
    edge_step(mid, ((1, coef0, to_stepped(0)), (2, coef1, to_stepped(1))))
    lane_edge(0)

    def lead_copy(slot, target, sent):
        return pltpu.make_async_remote_copy(
            src_ref=lead, dst_ref=lead_in.at[slot], send_sem=lead_send.at[sent],
            recv_sem=lead_recv.at[slot], device_id=(g, target), device_id_type=MESH,
        )

    routes = [(0, d > 0, lax.rem(d + 7, 8)), (1, lax.rem(d, 2) == 0, lax.rem(d + 1, 8))]
    routes += [(1, d == 0, 2), (1, d == 0, 4), (1, d == 4, 6), (2, d == 4, 2)]
    lead[...] = columns(lanes_done[EDGE : EDGE + COLS, :])
    for sent, (slot, condition, target) in enumerate(routes):

        @pl.when(condition)
        def _():
            lead_copy(slot, target, sent).start()

    send_all(slots_out, slots_in, slot_sems, 1)

    @pl.when(d < 7)
    def _():
        down().wait_recv()

    start[slot_rows(6, 2), :] = high_in[0:128]
    shift_lanes(start, halo + 5 * COLS)
    above = lambda i: high_in[128 + i : 136 + i, :]
    edge_step(start, ((5, coef15, to_mid(6, None)), (6, above, to_mid(7, 7))))
    shift_lanes(mid, halo + 5 * COLS)
    coef14 = lambda i: coef[1088 + i : 1096 + i, :]
    edge_step(mid, ((5, coef14, to_stepped(2)), (6, coef15, to_stepped(3))))
    lane_edge(2)

    places = {0: 0, 1: 1, 14: 2, 15: 3}

    def lanes_of(node):
        if node in places:
            at = EDGE + places[node] * COLS
            return lanes_done[at : at + COLS, :]
        return lanes_done[node_rows(0, node), :]

    for node in range(0, 16, 2):
        pair = columns(jnp.concatenate([lanes_of(node), lanes_of(node + 1)], axis=1))
        rows_done[node * COLS : (node + 1) * COLS, :] = pair[:, :128]
        rows_done[(node + 1) * COLS : (node + 2) * COLS, :] = pair[:, 128:]

    for i in range(0, COLS, 8):
        nodes = [rows_done[n * COLS + i : n * COLS + i + 8, :] for n in range(16)]
        for n in range(16):
            value = nodes[n]
            bit = n & (-n)
            if n:
                near = nodes[n - bit]
                if n + bit < 16:
                    near = near + nodes[n + bit]
                value = value - 0.5 * near
            surplus[n * COLS + i : n * COLS + i + 8, :] = value

    zero_lead = jnp.zeros((64, 128), F32)

    @pl.when(d == 7)
    def _():
        lead_in[0] = zero_lead

    @pl.when(d == 0)
    def _():
        lead_in[1] = zero_lead

    @pl.when(d != 2)
    def _():
        lead_in[2] = zero_lead

    @pl.when(d < 7)
    def _():
        lead_copy(0, lax.rem(d + 7, 8), 0).wait_recv()

    @pl.when(d > 0)
    def _():
        lead_copy(1, lax.rem(d + 1, 8), 0).wait_recv()

    @pl.when(d == 2)
    def _():
        lead_copy(2, lax.rem(d + 1, 8), 0).wait_recv()

    following = 0.5 * lead_in[0]
    use_next = jnp.where(lax.rem(d, 2) == 1, 1.0, 0.0)
    around = 0.5 * (lead_in[1] + lead_in[2]) + use_next * following
    surplus[0:COLS] = surplus[0:COLS] - around
    for node in (8, 12, 14, 15):
        at = node * COLS
        surplus[at : at + COLS] = surplus[at : at + COLS] - following

    halves = ((out_a, in_a, ret_a, back_a), (out_b, in_b, ret_b, back_b))
    for half, (outgoing, arrived, _, _) in enumerate(halves):
        for o in range(128):
            of_rank = [surplus[tile(index_s[1 + r, o]), :] for r in range(2)]
            turned = pltpu.roll(of_rank[1], 4, 0)
            kept = (sub < 4) if half == 0 else (sub >= 4)
            outgoing[o * 8 : o * 8 + 8, :] = jnp.where(kept, of_rank[0], turned)
        send_all(outgoing, arrived, out_sems.at[half], 8)

    all_of(slots_out, slots_in, slot_sems, 1).wait_recv()
    ids_col = slots_in[:, 0, :]
    ids_row = ids_col.T
    equal = []
    for r in range(2):
        of_r = jnp.broadcast_to(ids_col[:, r : r + 1], (128, 128))
        parts = [
            jnp.where(of_r == jnp.broadcast_to(ids_row[s : s + 1, :], (128, 128)), 1.0, 0.0)
            for s in range(2)
        ]
        equal.append(jnp.concatenate(parts, axis=1))
    equal = jnp.concatenate(equal, axis=0).astype(BF16)

    for half, (outgoing, arrived, returned, back) in enumerate(halves):
        all_of(outgoing, arrived, out_sems.at[half], 8).wait_recv()
        for j in range(4):
            block = jnp.concatenate(
                [arrived[pl.ds((r ^ half) * 4 + j, 128, stride=8), :] for r in range(2)], axis=0
            )
            first = block.astype(BF16)
            second = (block - first.astype(F32)).astype(BF16)
            total = jnp.dot(equal, second, preferred_element_type=F32)
            total = total + jnp.dot(equal, first, preferred_element_type=F32)
            for r in range(2):
                returned[pl.ds((r ^ half) * 4 + j, 128, stride=8), :] = total[
                    r * 128 : (r + 1) * 128
                ]
        send_all(returned, back, back_sems.at[half], 8)

    for half, (_, _, returned, back) in enumerate(halves):
        all_of(returned, back, back_sems.at[half], 8).wait_recv()

        for block in range(128):
            at = (block // 64) * (8 * COLS) + (block % 8) * 64 + (block // 8) % 8 + half * 32
            out_ref[pl.ds(at, 4, stride=8), :] = back[pl.ds(index_s[3 * half, block], 4), :]

    @pl.when(d > 0)
    def _():
        down().wait_send()

    @pl.when(d < 7)
    def _():
        upward().wait_send()

    for sent, (slot, condition, target) in enumerate(routes):

        @pl.when(condition)
        def _():
            lead_copy(slot, target, sent).wait_send()

    all_of(slots_out, slots_in, slot_sems, 1).wait_send()
    for half, (outgoing, arrived, returned, back) in enumerate(halves):
        all_of(outgoing, arrived, out_sems.at[half], 8).wait_send()
        all_of(returned, back, back_sems.at[half], 8).wait_send()


def body(concentration, diffusion, velocity, levels, grid_signs, owner_list, slot_list):
    def in_hbm(array):
        return pltpu.with_memory_space_constraint(array, pltpu.HBM)

    def tiled(block):
        rows = block.reshape(2, 8, COLS, 128).transpose(0, 2, 1, 3).reshape(1024, 128)
        return in_hbm(rows)

    smem = pl.BlockSpec(memory_space=pltpu.SMEM)
    vmem = pl.BlockSpec(memory_space=pltpu.VMEM)
    anywhere = pl.BlockSpec(memory_space=pltpu.HBM)
    total_rows = (TILE_HALO + COLS + PAD) * 8
    rows = [total_rows, total_rows, 1152, 1296, 1296, 1032, 1032]
    combined = pl.pallas_call(
        combine_kernel,
        out_shape=jax.ShapeDtypeStruct((1032, 128), F32),
        in_specs=[smem, smem, smem, vmem, vmem, anywhere, anywhere],
        out_specs=vmem,
        scratch_shapes=[pltpu.VMEM((n, 128), F32) for n in rows]
        + [
            pltpu.VMEM((2, 192, 128), F32),
            pltpu.VMEM((192, 128), F32),
            pltpu.VMEM((192, 128), F32),
            pltpu.VMEM((64, 128), F32),
            pltpu.VMEM((3, 64, 128), F32),
        ]
        + [pltpu.VMEM((total_rows, 128), F32) for _ in range(5)]
        + [pltpu.VMEM((1032, 128), F32) for _ in range(8)]
        + [
            pltpu.VMEM((128, 1, 128), I32),
            pltpu.VMEM((128, 1, 128), I32),
            pltpu.VMEM((8, 128), I32),
            pltpu.SMEM((8, 128), I32),
            pltpu.SemaphoreType.DMA((3,)),
            pltpu.SemaphoreType.DMA((2,)),
            pltpu.SemaphoreType.DMA((2,)),
            pltpu.SemaphoreType.DMA((6,)),
            pltpu.SemaphoreType.DMA((3,)),
            pltpu.SemaphoreType.DMA((2,)),
            pltpu.SemaphoreType.DMA((2, 2)),
            pltpu.SemaphoreType.DMA((2, 2)),
        ],
        compiler_params=pltpu.CompilerParams(
            collective_id=0, has_side_effects=True, vmem_limit_bytes=24 << 20
        ),
        name="combine",
    )(
        in_hbm(levels), in_hbm(velocity), grid_signs, in_hbm(owner_list), in_hbm(slot_list),
        tiled(concentration), tiled(diffusion),
    )
    return combined[:1024].reshape(2, COLS, 8, 128).transpose(0, 2, 1, 3).reshape(1, 16, COLS * 128)


def solution(mesh):
    return jax.shard_map(
        body,
        mesh=mesh,
        in_specs=(
            P("grid", "dom", None),
            P("grid", "dom", None),
            P(),
            P("grid", None),
            P("grid"),
            P(("grid", "dom"), None),
            P(("grid", "dom"), None),
        ),
        out_specs=P("grid", "dom", None),
        check_vma=False,
    )
```

```python
import jax
import jax.numpy as jnp
from jax import lax
from jax.experimental import pallas as pl
from jax.experimental.pallas import tpu as pltpu
from jax.sharding import PartitionSpec as P

MESH = pl.DeviceIdType.MESH
F32 = jnp.float32
BF16 = jnp.bfloat16
I32 = jnp.int32

COLS = 64
PAD = 8
EDGE = 1032
TILE_HALO = PAD + 2 * COLS


def tile(at):
    return pl.ds(at * 8, 8)


def node_rows(base, node):
    return pl.ds(base + (node // 8) * COLS * 8 + node % 8, COLS, stride=8)


def dot_split(left, right):
    first = left.astype(BF16)
    second = (left - first.astype(F32)).astype(BF16)
    total = jnp.dot(second, right, preferred_element_type=F32)
    return total + jnp.dot(first, right, preferred_element_type=F32)


def lane_matrices(l1, l2, sign):
    source = lax.broadcasted_iota(I32, (128, 128), 0)
    target = lax.broadcasted_iota(I32, (128, 128), 1)
    both = l1 + l2
    low = [0, l1, both]
    top = [jnp.minimum(l1, 7), jnp.minimum(both, 7), 7]
    here = jnp.full((128, 128), sign, F32)
    after = jnp.full((128, 128), sign, F32)
    for field in range(3):
        width = jnp.maximum(top[field] - jnp.minimum(low[field], 7), 0)
        mask = jnp.left_shift(1, width) - 1
        shift = jnp.minimum(low[field], 7)
        fro = jnp.right_shift(source, shift) & mask
        to = jnp.right_shift(target, shift) & mask
        bit = to & (-to)
        same = jnp.where(fro == to, 1.0, 0.0)
        near = jnp.where((to != 0) & ((fro == to - bit) | (fro == to + bit)), -0.5, 0.0)
        plain = same + near
        wraps = (to != 0) & (to + bit == mask + 1) & (fro == 0)
        carry = jnp.where(wraps, -0.5, 0.0)
        here = here * plain
        if field == 0:
            after = after * plain
        elif field == 1:
            after = after * jnp.where(both > 6, jnp.where(width > 0, carry, 0.0), plain)
        else:
            after = after * jnp.where(both > 6, 1.0, carry)
    return here, after


def peer_offsets():
    offsets = [(k // 32, k // 8 % 4, k // 2 % 4, k % 2) for k in range(1, 128)]
    offsets.sort(key=lambda o: (o[0] * 37 + o[1] * 17 + o[2] * 29 + o[3] * 11) % 23)
    return sorted(offsets, key=lambda o: -sum(min(v, 4 - v) for v in o[:3]))


def unrolled(count, factor, step):
    def some(i, carry):
        for k in range(factor):
            step(i * factor + k)
        return carry

    lax.fori_loop(0, count // factor, some, 0)


def combine_kernel(
    lev_ref, vel_ref, sign_ref, own_ref, slot_ref, u_hbm, k_hbm, out_ref,
    start, mid, coef, stepped, lanes_done, rows_done, surplus, packs, low_in, high_in, lead, lead_in,
    sums, diffs, forth, back2, turned3,
    out_a, out_b, in_a, in_b, ret_a, ret_b, back_a, back_b, slots_out, slots_in, index_v, index_s,
    load_sem, send_sem, recv_sem, lead_send, lead_recv, slot_sems, out_sems, back_sems,
):
    g = lax.axis_index("grid")
    d = lax.axis_index("dom")
    me = g * 8 + d
    x_at, y_at = g // 4, g % 4
    z_at, core = d // 2, d % 2
    grids = [((x_at + i) % 4) * 4 + (y_at + j) % 4 for i in range(4) for j in range(4)]
    doms = [((z_at + i) % 4) * 2 + (core + j) % 2 for i in range(4) for j in range(2)]
    barrier = pltpu.get_barrier_semaphore()

    load_u = pltpu.make_async_copy(u_hbm, start.at[pl.ds(PAD * 8, 1024)], load_sem.at[0])
    load_k = pltpu.make_async_copy(k_hbm, coef.at[pl.ds(0, 1024)], load_sem.at[1])
    load_u.start()
    load_k.start()

    def peer(offset):
        return grids[offset[0] * 4 + offset[1]], doms[offset[2] * 2 + offset[3]]

    offsets = peer_offsets()
    for offset in offsets:
        pl.semaphore_signal(barrier, inc=1, device_id=peer(offset), device_id_type=MESH)

    owners = own_ref[...]
    own_row = jnp.broadcast_to(owners, (128, 128))
    own_col = own_row.T
    row = lax.broadcasted_iota(I32, (128, 128), 0)
    col = lax.broadcasted_iota(I32, (128, 128), 1)
    earlier = jnp.where((own_row == own_col) & (row < col), 1, 0)
    rank = jnp.sum(earlier, axis=0, keepdims=True)
    rank_row = jnp.broadcast_to(rank, (128, 128))
    rank_col = rank_row.T
    slot_row = jnp.broadcast_to(slot_ref[...], (128, 128))
    table = jnp.full((128, 128), -1, I32)
    index_v[...] = jnp.zeros((8, 128), I32)
    second_one = jnp.minimum(rank, 1)
    index_v[0:1] = 8 * owners + 4 * second_one
    index_v[3:4] = 8 * owners + 4 * (1 - second_one)
    for r in range(2):
        to_owner = (own_col == col) & (rank_col == r)
        index_v[1 + r : 2 + r] = jnp.sum(jnp.where(to_owner, row, 0), axis=0, keepdims=True)
        of_block = (own_row == row) & (rank_row == r)
        ids = jnp.sum(jnp.where(of_block, slot_row + 1, 0), axis=1, keepdims=True) - 1
        table = jnp.where(col == r, ids, table)
    slots_out[:, 0, :] = table
    fetch = pltpu.make_async_copy(index_v, index_s, load_sem.at[2])
    fetch.start()

    halo = TILE_HALO * 8

    def slot_rows(slot, count=1):
        return pl.ds(halo + slot * COLS, count * COLS)

    base = PAD * 8
    load_u.wait()
    load_k.wait()
    packs[0, 0:64] = start[node_rows(base, 0), :]
    packs[0, 64:128] = start[node_rows(base, 1), :]
    packs[0, 128:192] = coef[node_rows(0, 0), :]
    packs[1, 0:64] = start[node_rows(base, 14), :]
    packs[1, 64:128] = start[node_rows(base, 15), :]
    packs[1, 128:192] = coef[node_rows(0, 15), :]
    start[slot_rows(2, 2), :] = packs[0, 0:128]
    start[slot_rows(4, 2), :] = packs[1, 0:128]
    coef[1024:1088] = coef[node_rows(0, 1), :]
    coef[1088:1152] = coef[node_rows(0, 14), :]

    l1 = lev_ref[0, 0]
    l2 = lev_ref[0, 1]
    l3 = lev_ref[0, 2]
    both = l1 + l2
    lane = lax.broadcasted_iota(I32, (8, 128), 1)
    sub = lax.broadcasted_iota(I32, (8, 128), 0)
    span2 = jnp.left_shift(1, l1)
    span3 = jnp.minimum(jnp.left_shift(1, both), 128)
    skip3 = jnp.where(both == 8, 2, jnp.where(both == 9, 4, jnp.where(both == 10, 8, 1)))
    last1 = jnp.left_shift(1, l1) - 1
    last2 = jnp.left_shift(1, l2) - 1
    last3 = jnp.left_shift(1, l3) - 1
    drift1 = 0.1 * vel_ref[0]
    drift2 = 0.1 * vel_ref[1]
    drift3 = 0.1 * vel_ref[2]
    drift4 = 0.1 * vel_ref[3]
    stays2 = lane < 128 - span2
    comes2 = lane >= span2
    stays3 = lane < 128 - span3
    comes3 = lane >= span3

    source = lax.broadcasted_iota(I32, (128, 128), 0)
    target = lax.broadcasted_iota(I32, (128, 128), 1)
    at1 = target & last1
    from_up = jnp.where((source == target + 1) & (at1 != last1), 1.0, 0.0)
    from_down = jnp.where((source == target - 1) & (at1 != 0), 1.0, 0.0)
    turn2 = span2 & 127
    turn3 = span3 & 127
    forms = [
        from_up + from_down,
        from_up - from_down,
        jnp.where(source == ((target + turn2) & 127), 1.0, 0.0),
        jnp.where(source == ((target - turn2) & 127), 1.0, 0.0),
        jnp.where(source == ((target + turn3) & 127), 1.0, 0.0),
    ]
    forms = jnp.concatenate([jnp.concatenate([form, form], axis=0).astype(BF16) for form in forms], axis=1)
    shift_chunk = 128

    def shift_lanes(ref, at):
        x = ref[at : at + shift_chunk, :]
        high = x.astype(BF16)
        low = (x - high.astype(F32)).astype(BF16)
        shifted = jnp.dot(
            jnp.concatenate([high, low], axis=1), forms, preferred_element_type=F32
        )
        for form, scratch in enumerate((sums, diffs, forth, back2, turned3)):
            scratch[at : at + shift_chunk, :] = shifted[:, form * 128 : (form + 1) * 128]

    def masks(c):
        cell = c * 128 + lane
        i2 = jnp.right_shift(cell, l1) & last2
        i3 = jnp.right_shift(cell, both) & last3
        return (i2 != last2, i2 != 0, i3 != last3, i3 != 0)

    def advance(rows_at, x, ahead4, behind4, diff, ok):
        here = rows_at(0)
        p2 = jnp.where(stays2, forth[here, :], forth[rows_at(1), :])
        p2 = jnp.where(ok[0], p2, 0.0)
        m2 = jnp.where(comes2, back2[here, :], back2[rows_at(-1), :])
        m2 = jnp.where(ok[1], m2, 0.0)
        half = turned3[here, :]
        p3 = jnp.where(stays3, half, turned3[rows_at(skip3), :])
        p3 = jnp.where(ok[2], p3, 0.0)
        m3 = jnp.where(comes3, half, turned3[rows_at(-skip3), :])
        m3 = jnp.where(ok[3], m3, 0.0)
        second = (sums[here, :] + (p2 + m2)) + ((p3 + m3) + (ahead4 + behind4)) - 8.0 * x
        drift = (drift1 * diffs[here, :] + drift2 * (p2 - m2)) + (
            drift3 * (p3 - m3) + drift4 * (ahead4 - behind4)
        )
        return x + 0.1 * diff * second - drift

    def both_groups(ref, c, target, offset):
        ok = masks(c)
        x0 = ref[tile(PAD + c), :]
        x1 = ref[tile(PAD + COLS + c), :]
        value0 = advance(
            lambda k: tile(PAD + c + k), x0, pltpu.roll(jnp.where(sub == 0, x1, x0), 7, 0),
            pltpu.roll(x0, 1, 0), coef[tile(c), :], ok,
        )
        value1 = advance(
            lambda k: tile(PAD + COLS + c + k), x1, pltpu.roll(x1, 7, 0),
            pltpu.roll(jnp.where(sub == 7, x0, x1), 1, 0), coef[tile(COLS + c), :], ok,
        )
        target[tile(offset + c), :] = value0
        target[tile(offset + COLS + c), :] = value1

    for i in range(1024 // shift_chunk):
        shift_lanes(start, PAD * 8 + i * shift_chunk)
    unrolled(COLS, 2, lambda c: both_groups(start, c, mid, PAD))
    for i in range(1024 // shift_chunk):
        shift_lanes(mid, PAD * 8 + i * shift_chunk)
    pl.semaphore_wait(barrier, 127)

    def down():
        return pltpu.make_async_remote_copy(
            src_ref=packs.at[0], dst_ref=high_in, send_sem=send_sem.at[0], recv_sem=recv_sem.at[0],
            device_id=(g, lax.rem(d + 7, 8)), device_id_type=MESH,
        )

    def upward():
        return pltpu.make_async_remote_copy(
            src_ref=packs.at[1], dst_ref=low_in, send_sem=send_sem.at[1], recv_sem=recv_sem.at[1],
            device_id=(g, lax.rem(d + 1, 8)), device_id_type=MESH,
        )

    @pl.when(d > 0)
    def _():
        down().start()

    @pl.when(d < 7)
    def _():
        upward().start()

    def send_all(sources, targets, sems, size):
        for offset in offsets:
            pg, pd = peer(offset)
            pltpu.make_async_remote_copy(
                src_ref=sources.at[pl.ds((pg * 8 + pd) * size, size)],
                dst_ref=targets.at[pl.ds(me * size, size)],
                send_sem=sems.at[0], recv_sem=sems.at[1],
                device_id=(pg, pd), device_id_type=MESH,
            ).start()
        targets[pl.ds(me * size, size)] = sources[pl.ds(me * size, size)]

    def all_of(sources, targets, sems, size):
        return pltpu.make_async_remote_copy(
            src_ref=sources.at[pl.ds(0, 127 * size)], dst_ref=targets.at[pl.ds(0, 127 * size)],
            send_sem=sems.at[0], recv_sem=sems.at[1],
            device_id=(g, lax.rem(d + 1, 8)), device_id_type=MESH,
        )

    unrolled(COLS, 2, lambda c: both_groups(mid, c, stepped, 0))
    for slot, node in ((2, 1), (3, 2), (4, 13), (5, 14)):
        mid[slot_rows(slot), :] = mid[node_rows(base, node), :]
    fetch.wait()

    zero_rows = jnp.zeros((192, 128), F32)

    @pl.when(d == 0)
    def _():
        low_in[...] = zero_rows

    @pl.when(d == 7)
    def _():
        high_in[...] = zero_rows

    here, after = lane_matrices(l1, l2, sign_ref[0].astype(F32))
    here = here.astype(BF16)
    after = after.astype(BF16)

    straddles = jnp.where(both > 7, jnp.where(l1 < 7, 1, 0), jnp.where(both == 6, 1, 0))
    mask_a = jnp.where(both > 7, skip3 - 1, COLS - 1)
    no_next = jnp.where(straddles == 1, mask_a, 0)
    limit_a = jnp.where(both > 7, span2, span3)
    mask_b = jnp.where(both > 7, COLS - skip3, 0)
    inside = lane < limit_a
    chunk = 128

    def lane_part(base_row, i):
        at = base_row + i * chunk
        x = stepped[pl.ds(at, chunk), :]
        beyond = stepped[pl.ds(at + 8, chunk), :]
        column = jnp.right_shift(i * chunk + lax.broadcasted_iota(I32, (chunk, 128), 0), 3) & (COLS - 1)
        beyond = jnp.where((column & no_next) != no_next, beyond, 0.0)
        lanes_done[pl.ds(at, chunk), :] = dot_split(x, here) + dot_split(beyond, after)

    for i in range(1024 // chunk):
        lane_part(0, i)

    to_col = lax.broadcasted_iota(I32, (128, 128), 0)
    from_col = lax.broadcasted_iota(I32, (128, 128), 1) & (COLS - 1)
    upper_half = to_col < COLS
    to_col = to_col & (COLS - 1)

    def column_field(mask):
        to_field, from_field = to_col & mask, from_col & mask
        bit = to_field & (-to_field)
        near = (from_field == to_field - bit) | (from_field == to_field + bit)
        near = jnp.where((to_field != 0) & near, -0.5, 0.0)
        return jnp.where(to_field == from_field, 1.0, near)

    same_a = jnp.where((to_col & mask_a) == (from_col & mask_a), 1.0, 0.0)
    columns_matrix = jnp.where(upper_half, column_field(mask_a), same_a) * column_field(mask_b)
    columns_matrix = columns_matrix.astype(BF16)

    def columns(rows):
        high = rows.astype(BF16)
        low = (rows - high.astype(F32)).astype(BF16)
        terms = jnp.concatenate([high, low], axis=0)
        done = jnp.dot(columns_matrix, terms, preferred_element_type=F32)
        lane_of_row = lax.broadcasted_iota(I32, (COLS, rows.shape[1]), 1) & 127
        return jnp.where(lane_of_row < limit_a, done[:COLS], done[COLS:])

    def edge_step(ref, moves):
        for i in range(8):
            ok = masks(i * 8 + sub)
            for slot, diff, write in moves:
                at = halo + slot * COLS + i * 8
                value = advance(
                    lambda k: pl.ds(at + k, 8), ref[at : at + 8, :],
                    ref[at + COLS : at + COLS + 8, :], ref[at - COLS : at - COLS + 8, :],
                    diff(i * 8), ok,
                )
                write(i * 8, value)

    def to_mid(slot, zero_at):
        def write(i, value):
            if zero_at is not None:
                value = jnp.where(d == zero_at, 0.0, value)
            mid[halo + slot * COLS + i : halo + slot * COLS + i + 8, :] = value

        return write

    def to_stepped(place):
        def write(i, value):
            stepped[EDGE + place * COLS + i : EDGE + place * COLS + i + 8, :] = value

        return write

    def lane_edge(place):
        at = EDGE + place * COLS
        x = stepped[at : at + 128, :]
        beyond = stepped[at + 1 : at + 129, :]
        column = lax.broadcasted_iota(I32, (128, 128), 0) & (COLS - 1)
        beyond = jnp.where((column & no_next) != no_next, beyond, 0.0)
        lanes_done[at : at + 128, :] = dot_split(x, here) + dot_split(beyond, after)

    coef0 = lambda i: packs[0, 128 + i : 136 + i, :]
    coef15 = lambda i: packs[1, 128 + i : 136 + i, :]

    @pl.when(d > 0)
    def _():
        upward().wait_recv()

    start[slot_rows(0, 2), :] = low_in[0:128]
    shift_lanes(start, halo + COLS)
    below = lambda i: low_in[128 + i : 136 + i, :]
    edge_step(start, ((1, below, to_mid(0, 0)), (2, coef0, to_mid(1, None))))
    shift_lanes(mid, halo + COLS)
    coef1 = lambda i: coef[1024 + i : 1032 + i, :]
    edge_step(mid, ((1, coef0, to_stepped(0)), (2, coef1, to_stepped(1))))
    lane_edge(0)

    def lead_copy(slot, target, sent):
        return pltpu.make_async_remote_copy(
            src_ref=lead, dst_ref=lead_in.at[slot], send_sem=lead_send.at[sent],
            recv_sem=lead_recv.at[slot], device_id=(g, target), device_id_type=MESH,
        )

    routes = [(0, d > 0, lax.rem(d + 7, 8)), (1, lax.rem(d, 2) == 0, lax.rem(d + 1, 8))]
    routes += [(1, d == 0, 2), (1, d == 0, 4), (1, d == 4, 6), (2, d == 4, 2)]
    lead[...] = columns(lanes_done[EDGE : EDGE + COLS, :])
    for sent, (slot, condition, target) in enumerate(routes):

        @pl.when(condition)
        def _():
            lead_copy(slot, target, sent).start()

    send_all(slots_out, slots_in, slot_sems, 1)

    @pl.when(d < 7)
    def _():
        down().wait_recv()

    start[slot_rows(6, 2), :] = high_in[0:128]
    shift_lanes(start, halo + 5 * COLS)
    above = lambda i: high_in[128 + i : 136 + i, :]
    edge_step(start, ((5, coef15, to_mid(6, None)), (6, above, to_mid(7, 7))))
    shift_lanes(mid, halo + 5 * COLS)
    coef14 = lambda i: coef[1088 + i : 1096 + i, :]
    edge_step(mid, ((5, coef14, to_stepped(2)), (6, coef15, to_stepped(3))))
    lane_edge(2)

    places = {0: 0, 1: 1, 14: 2, 15: 3}

    def lanes_of(node):
        if node in places:
            at = EDGE + places[node] * COLS
            return lanes_done[at : at + COLS, :]
        return lanes_done[node_rows(0, node), :]

    for node in range(0, 16, 2):
        pair = columns(jnp.concatenate([lanes_of(node), lanes_of(node + 1)], axis=1))
        rows_done[node * COLS : (node + 1) * COLS, :] = pair[:, :128]
        rows_done[(node + 1) * COLS : (node + 2) * COLS, :] = pair[:, 128:]

    for i in range(0, COLS, 8):
        nodes = [rows_done[n * COLS + i : n * COLS + i + 8, :] for n in range(16)]
        for n in range(16):
            value = nodes[n]
            bit = n & (-n)
            if n:
                near = nodes[n - bit]
                if n + bit < 16:
                    near = near + nodes[n + bit]
                value = value - 0.5 * near
            surplus[n * COLS + i : n * COLS + i + 8, :] = value

    zero_lead = jnp.zeros((64, 128), F32)

    @pl.when(d == 7)
    def _():
        lead_in[0] = zero_lead

    @pl.when(d == 0)
    def _():
        lead_in[1] = zero_lead

    @pl.when(d != 2)
    def _():
        lead_in[2] = zero_lead

    @pl.when(d < 7)
    def _():
        lead_copy(0, lax.rem(d + 7, 8), 0).wait_recv()

    @pl.when(d > 0)
    def _():
        lead_copy(1, lax.rem(d + 1, 8), 0).wait_recv()

    @pl.when(d == 2)
    def _():
        lead_copy(2, lax.rem(d + 1, 8), 0).wait_recv()

    following = 0.5 * lead_in[0]
    use_next = jnp.where(lax.rem(d, 2) == 1, 1.0, 0.0)
    around = 0.5 * (lead_in[1] + lead_in[2]) + use_next * following
    surplus[0:COLS] = surplus[0:COLS] - around
    for node in (8, 12, 14, 15):
        at = node * COLS
        surplus[at : at + COLS] = surplus[at : at + COLS] - following

    halves = ((out_a, in_a, ret_a, back_a), (out_b, in_b, ret_b, back_b))
    for half, (outgoing, arrived, _, _) in enumerate(halves):
        for o in range(128):
            of_rank = [surplus[tile(index_s[1 + r, o]), :] for r in range(2)]
            turned = pltpu.roll(of_rank[1], 4, 0)
            kept = (sub < 4) if half == 0 else (sub >= 4)
            outgoing[o * 8 : o * 8 + 8, :] = jnp.where(kept, of_rank[0], turned)
        send_all(outgoing, arrived, out_sems.at[half], 8)

    all_of(slots_out, slots_in, slot_sems, 1).wait_recv()
    ids_col = slots_in[:, 0, :]
    ids_row = ids_col.T
    equal = []
    for r in range(2):
        of_r = jnp.broadcast_to(ids_col[:, r : r + 1], (128, 128))
        parts = [
            jnp.where(of_r == jnp.broadcast_to(ids_row[s : s + 1, :], (128, 128)), 1.0, 0.0)
            for s in range(2)
        ]
        equal.append(jnp.concatenate(parts, axis=1))
    equal = jnp.concatenate(equal, axis=0).astype(BF16)

    for half, (outgoing, arrived, returned, back) in enumerate(halves):
        all_of(outgoing, arrived, out_sems.at[half], 8).wait_recv()
        for j in range(4):
            block = jnp.concatenate(
                [arrived[pl.ds((r ^ half) * 4 + j, 128, stride=8), :] for r in range(2)], axis=0
            )
            first = block.astype(BF16)
            second = (block - first.astype(F32)).astype(BF16)
            total = jnp.dot(equal, second, preferred_element_type=F32)
            total = total + jnp.dot(equal, first, preferred_element_type=F32)
            for r in range(2):
                returned[pl.ds((r ^ half) * 4 + j, 128, stride=8), :] = total[
                    r * 128 : (r + 1) * 128
                ]
        send_all(returned, back, back_sems.at[half], 8)

    for half, (_, _, returned, back) in enumerate(halves):
        all_of(returned, back, back_sems.at[half], 8).wait_recv()

        for block in range(128):
            at = (block // 64) * (8 * COLS) + (block % 8) * 64 + (block // 8) % 8 + half * 32
            out_ref[pl.ds(at, 4, stride=8), :] = back[pl.ds(index_s[3 * half, block], 4), :]

    @pl.when(d > 0)
    def _():
        down().wait_send()

    @pl.when(d < 7)
    def _():
        upward().wait_send()

    for sent, (slot, condition, target) in enumerate(routes):

        @pl.when(condition)
        def _():
            lead_copy(slot, target, sent).wait_send()

    all_of(slots_out, slots_in, slot_sems, 1).wait_send()
    for half, (outgoing, arrived, returned, back) in enumerate(halves):
        all_of(outgoing, arrived, out_sems.at[half], 8).wait_send()
        all_of(returned, back, back_sems.at[half], 8).wait_send()


def body(concentration, diffusion, velocity, levels, grid_signs, owner_list, slot_list):
    def in_hbm(array):
        return pltpu.with_memory_space_constraint(array, pltpu.HBM)

    def tiled(block):
        rows = block.reshape(2, 8, COLS, 128).transpose(0, 2, 1, 3).reshape(1024, 128)
        return in_hbm(rows)

    smem = pl.BlockSpec(memory_space=pltpu.SMEM)
    vmem = pl.BlockSpec(memory_space=pltpu.VMEM)
    anywhere = pl.BlockSpec(memory_space=pltpu.HBM)
    total_rows = (TILE_HALO + COLS + PAD) * 8
    rows = [total_rows, total_rows, 1152, 1296, 1296, 1032, 1032]
    combined = pl.pallas_call(
        combine_kernel,
        out_shape=jax.ShapeDtypeStruct((1032, 128), F32),
        in_specs=[smem, smem, smem, vmem, vmem, anywhere, anywhere],
        out_specs=vmem,
        scratch_shapes=[pltpu.VMEM((n, 128), F32) for n in rows]
        + [
            pltpu.VMEM((2, 192, 128), F32),
            pltpu.VMEM((192, 128), F32),
            pltpu.VMEM((192, 128), F32),
            pltpu.VMEM((64, 128), F32),
            pltpu.VMEM((3, 64, 128), F32),
        ]
        + [pltpu.VMEM((total_rows, 128), F32) for _ in range(5)]
        + [pltpu.VMEM((1032, 128), F32) for _ in range(8)]
        + [
            pltpu.VMEM((128, 1, 128), I32),
            pltpu.VMEM((128, 1, 128), I32),
            pltpu.VMEM((8, 128), I32),
            pltpu.SMEM((8, 128), I32),
            pltpu.SemaphoreType.DMA((3,)),
            pltpu.SemaphoreType.DMA((2,)),
            pltpu.SemaphoreType.DMA((2,)),
            pltpu.SemaphoreType.DMA((6,)),
            pltpu.SemaphoreType.DMA((3,)),
            pltpu.SemaphoreType.DMA((2,)),
            pltpu.SemaphoreType.DMA((2, 2)),
            pltpu.SemaphoreType.DMA((2, 2)),
        ],
        compiler_params=pltpu.CompilerParams(
            collective_id=0, has_side_effects=True, vmem_limit_bytes=24 << 20
        ),
        name="combine",
    )(
        in_hbm(levels), in_hbm(velocity), grid_signs, in_hbm(owner_list), in_hbm(slot_list),
        tiled(concentration), tiled(diffusion),
    )
    return combined[:1024].reshape(2, COLS, 8, 128).transpose(0, 2, 1, 3).reshape(1, 16, COLS * 128)


def solution(mesh):
    return jax.shard_map(
        body,
        mesh=mesh,
        in_specs=(
            P("grid", "dom", None),
            P("grid", "dom", None),
            P(),
            P("grid", None),
            P("grid"),
            P(("grid", "dom"), None),
            P(("grid", "dom"), None),
        ),
        out_specs=P("grid", "dom", None),
        check_vma=False,
    )
```
